32 devices in a mesh: space: 8 (over z, y), view: 4 (over x, core).
Axes of the slice: x: 2, y: 2, z: 4, core: 2. Of those that a mesh axis runs over, the one named last changes fastest.
Arguments:
- params: float32 [59, 16384], P(None, 'space'), may hold values from -8 to 514, as said below
- visible: int32 [8, 128, 16], P('space'), may hold values from 0 to 2047, as said below
- blocks: int32 [8, 128], P('space'), may hold values from 0 to 63, as said below
- counts: int32 [8, 8], P('space'), may hold values from 1 to 16
- depth_rank: int32 [4, 8], P('view'), may hold values from 0 to 7, each once within a row
- camera: float32 [4, 3], P('view'), may hold values from -0.006 to 0.006
- background: float32 [4, 3], P('view'), may hold values from 0 to 1
- target: float32 [4, 3, 128, 512], P('view', None, 'space'), may hold values from 0 to 1
Outputs:
- grad_params: float32 [59, 16384], P(None, 'space')
- rendered: float32 [4, 3, 128, 512], P('view', None, 'space')
- loss: float32 [4], P('view')
The draws below stay inside these ranges and needn't reach their ends.
Inputs may be any that keep to these rules, and one draw needn't show every extreme that they name: `visible`: each row of a subspace's table lists 16 different splats of that subspace in increasing order; every splat of the subspace is listed exactly once. Slot j of a subspace goes to owner j // 16; the 16 slots that one subspace sends to one owner name different blocks. counts[s, o] live slots lead the 16 slots that subspace s sends to owner o. `params`: rows 6 to 9 of a column hold a quaternion whose first component lies in [1, 2].
All inputs are finite; a program needn't handle non-finite values.
Results may differ from the reference program's by a relative error of at most 0.0003.
Values sent between devices are 32-bit elements; how exact they have to be, the bound alone decides.
A program may use at most 64 MiB of HBM per device.

```python
import math
import jax
import jax.numpy as jnp
from jax import lax

K = 16
SEG_DEV = 128
ROWS_DEV = 16
IMG_W = 512
SUBS = 8
VIEWS = 4
CAP = 16
SPL = 2048
HEIGHT = 128
BLK_DEV = 64
N_VIEW = 4


def layout(key):
    base_key = jax.random.fold_in(key, 7)
    key_blocks, key_lists = jax.random.split(base_key)
    scores = jax.random.randint(key_blocks, (SUBS, SUBS, BLK_DEV), 0, 1 << 20) * BLK_DEV + jnp.arange(BLK_DEV)[None, None, :]
    chosen = jnp.argsort(scores, axis=-1)[:, :, :CAP].astype(jnp.int32).reshape(SUBS, SEG_DEV)
    rank_keys = jax.random.randint(key_lists, (SUBS, SPL), 0, 1 << 16) * SPL + jnp.arange(SPL)[None, :]
    listing = jnp.argsort(rank_keys, axis=-1).astype(jnp.int32)
    return (chosen, listing)


def draw_visible(key, part):
    chosen, listing = layout(key)
    return jnp.sort(listing.reshape(SUBS, SEG_DEV, K), axis=-1).astype(jnp.int32)


def draw_blocks(key, part):
    chosen, listing = layout(key)
    return chosen


def draw_params(key, part):
    chosen, listing = layout(key)
    home_slot = jnp.argsort(listing, axis=-1).astype(jnp.int32) // K
    home_owner = home_slot // CAP
    home_block = jnp.take_along_axis(chosen, home_slot, axis=1)
    corner_y = (home_owner * ROWS_DEV + home_block // (IMG_W // 16) * 8).astype(jnp.float32)
    corner_x = (home_block % (IMG_W // 16) * 16).astype(jnp.float32)
    subkeys = jax.random.split(jax.random.fold_in(key, 3), 8)
    grid_shape = (SUBS, SPL)
    pos_x = corner_x + jax.random.uniform(subkeys[0], grid_shape, jnp.float32, -2.0, 18.0)
    pos_y = corner_y + jax.random.uniform(subkeys[1], grid_shape, jnp.float32, -2.0, 10.0)
    depths = jax.random.uniform(subkeys[2], grid_shape, jnp.float32, -8.0, 8.0)
    log_scale = jax.random.uniform(subkeys[3], (3, SUBS, SPL), jnp.float32, 0.0, 1.8)
    quat_real = jax.random.uniform(subkeys[4], grid_shape, jnp.float32, 1.0, 2.0)
    quat_rest = jax.random.uniform(subkeys[5], (3, SUBS, SPL), jnp.float32, -1.0, 1.0)
    logits = jax.random.uniform(subkeys[6], grid_shape, jnp.float32, -2.0, 3.0)
    harmonic = jnp.clip(0.3 * jax.random.normal(subkeys[7], (48, SUBS, SPL), jnp.float32), -1.2, 1.2)
    stacked = jnp.concatenate([pos_x[None], pos_y[None], depths[None], log_scale, quat_real[None], quat_rest, logits[None], harmonic], axis=0)
    return stacked.reshape(59, SUBS * SPL).astype(jnp.float32)


def with_ends(values, own_key, least, top_value):
    dims = values.shape
    index_at = [jax.random.randint(jax.random.fold_in(own_key, axis), (), 0, dims[axis]) for axis in range(len(dims))]
    values = values.at[tuple(index_at)].set(least)
    longest = dims.index(max(dims))
    index_at[longest] = (index_at[longest] + 1) % dims[longest]
    return values.at[tuple(index_at)].set(top_value)


def level_of(stream_key, dims, cuts, low, largest):
    gain = 1.0
    for axis_at, parts in cuts:
        steps = jax.random.uniform(jax.random.fold_in(jax.random.fold_in(stream_key, 6), axis_at), (parts,), jnp.float32, low / len(cuts), largest / len(cuts))
        gain = gain * jnp.repeat(jnp.exp(steps), dims[axis_at] // parts).reshape((-1,) + (1,) * (len(dims) - 1 - axis_at))
    return gain


def setup_inputs(seed: int = 0) -> dict:
    key_list = jax.random.split(jax.random.key(seed), 9)
    return {
        "params": draw_params(jax.random.fold_in(key_list[8], 71), 0),
        "visible": draw_visible(jax.random.fold_in(key_list[8], 71), 0),
        "blocks": draw_blocks(jax.random.fold_in(key_list[8], 71), 0),
        "counts": with_ends(jax.random.randint(key_list[3], (SUBS, SUBS), 1, CAP + 1), jax.random.fold_in(key_list[3], 1), 1, CAP).astype(jnp.int32),
        "depth_rank": jax.vmap(lambda own: jax.random.permutation(own, SUBS))(jax.random.split(key_list[4], VIEWS)).reshape((VIEWS, SUBS)).astype(jnp.int32),
        "camera": jnp.clip(jax.random.uniform(key_list[5], (VIEWS, 3), jnp.float32, -0.006, 0.006) * level_of(key_list[5], (VIEWS, 3), ((0, 4),), -0.4, 0.0), -0.006, 0.006),
        "background": jnp.clip(1.0 * jax.random.uniform(key_list[6], (VIEWS, 3), jnp.float32) ** level_of(key_list[6], (VIEWS, 3), ((0, 4),), -0.2, 0.2), 0.0, 1.0),
        "target": jnp.clip(1.0 * jax.random.uniform(key_list[7], (VIEWS, 3, HEIGHT, IMG_W), jnp.float32) ** level_of(key_list[7], (VIEWS, 3, HEIGHT, IMG_W), ((0, 4), (2, 8)), -0.2, 0.2), 0.0, 1.0),
    }


HIGHEST = lax.Precision.HIGHEST
SH_ZERO = 0.28209479177387814
SH_ONE = 0.4886025119029199
SH_TWO = (1.0925484305920792, -1.0925484305920792, 0.31539156525252005, -1.0925484305920792, 0.5462742152960396)
SH_THREE = (-0.5900435899266435, 2.890611442640554, -0.4570457994644658, 0.3731763325901154, -0.4570457994644658, 1.445305721320277, -0.5900435899266435)
DILATION = 0.3
SMOOTHING = 0.0001
SSIM_FIRST = 0.0001
SSIM_SECOND = 0.0009

def camera_rotation(angles):
    cos_a, sin_a = (jnp.cos(angles[0]), jnp.sin(angles[0]))
    cos_b, sin_b = (jnp.cos(angles[1]), jnp.sin(angles[1]))
    cos_c, sin_c = (jnp.cos(angles[2]), jnp.sin(angles[2]))
    unity = jnp.ones_like(cos_a)
    nought = jnp.zeros_like(cos_a)
    turn_x = jnp.stack([jnp.stack([unity, nought, nought]), jnp.stack([nought, cos_a, -sin_a]), jnp.stack([nought, sin_a, cos_a])])
    turn_y = jnp.stack([jnp.stack([cos_b, nought, sin_b]), jnp.stack([nought, unity, nought]), jnp.stack([-sin_b, nought, cos_b])])
    turn_z = jnp.stack([jnp.stack([cos_c, -sin_c, nought]), jnp.stack([sin_c, cos_c, nought]), jnp.stack([nought, nought, unity])])
    return jnp.dot(jnp.dot(turn_z, turn_y, precision=HIGHEST), turn_x, precision=HIGHEST)

def harmonics(view_axis):
    axis_x, axis_y, axis_z = (view_axis[0], view_axis[1], view_axis[2])
    sq_x, sq_y, sq_z = (axis_x * axis_x, axis_y * axis_y, axis_z * axis_z)
    values = [SH_ZERO * jnp.ones_like(axis_x), -SH_ONE * axis_y, SH_ONE * axis_z, -SH_ONE * axis_x, SH_TWO[0] * axis_x * axis_y, SH_TWO[1] * axis_y * axis_z, SH_TWO[2] * (2.0 * sq_z - sq_x - sq_y), SH_TWO[3] * axis_x * axis_z, SH_TWO[4] * (sq_x - sq_y), SH_THREE[0] * axis_y * (3.0 * sq_x - sq_y), SH_THREE[1] * axis_x * axis_y * axis_z, SH_THREE[2] * axis_y * (4.0 * sq_z - sq_x - sq_y), SH_THREE[3] * axis_z * (2.0 * sq_z - 3.0 * sq_x - 3.0 * sq_y), SH_THREE[4] * axis_x * (4.0 * sq_z - sq_x - sq_y), SH_THREE[5] * axis_z * (sq_x - sq_y), SH_THREE[6] * axis_x * (sq_x - 3.0 * sq_y)]
    return jnp.stack(values)

def project(param_in, angles, centre_x, centre_y):
    turn = camera_rotation(angles)
    scales = jnp.exp(param_in[3:6])
    quaternion = param_in[6:10]
    quaternion = quaternion / jnp.sqrt(lax.optimization_barrier(jnp.sum(quaternion * quaternion, axis=0)))
    part_w, part_x, part_y, part_z = (quaternion[0], quaternion[1], quaternion[2], quaternion[3])
    spin = [[1.0 - 2.0 * (part_y * part_y + part_z * part_z), 2.0 * (part_x * part_y - part_w * part_z), 2.0 * (part_x * part_z + part_w * part_y)], [2.0 * (part_x * part_y + part_w * part_z), 1.0 - 2.0 * (part_x * part_x + part_z * part_z), 2.0 * (part_y * part_z - part_w * part_x)], [2.0 * (part_x * part_z - part_w * part_y), 2.0 * (part_y * part_z + part_w * part_x), 1.0 - 2.0 * (part_x * part_x + part_y * part_y)]]
    frame = [[(turn[row, 0] * spin[0][col] + turn[row, 1] * spin[1][col] + turn[row, 2] * spin[2][col]) * scales[col] for col in range(3)] for row in range(2)]
    cov_xx = frame[0][0] * frame[0][0] + frame[0][1] * frame[0][1] + frame[0][2] * frame[0][2] + DILATION
    cov_xy = frame[0][0] * frame[1][0] + frame[0][1] * frame[1][1] + frame[0][2] * frame[1][2]
    cov_yy = frame[1][0] * frame[1][0] + frame[1][1] * frame[1][1] + frame[1][2] * frame[1][2] + DILATION
    determinant = cov_xx * cov_yy - cov_xy * cov_xy
    shift_x = param_in[0] - centre_x
    shift_y = param_in[1] - centre_y
    mean_u = turn[0, 0] * shift_x + turn[0, 1] * shift_y + turn[0, 2] * param_in[2] + centre_x
    mean_w = turn[1, 0] * shift_x + turn[1, 1] * shift_y + turn[1, 2] * param_in[2] + centre_y
    opacity = jax.nn.sigmoid(param_in[10])
    basis = harmonics(turn[2])
    coeffs = param_in[11:59].reshape(16, 3, param_in.shape[1])
    colour = 0.5 + lax.optimization_barrier(jnp.sum(basis[:, None, None] * coeffs, axis=0))
    record = jnp.stack([mean_u, mean_w, cov_yy / determinant, -cov_xy / determinant, cov_xx / determinant, opacity])
    return jnp.concatenate([record, colour], axis=0)

def render(gathered, grid_x, grid_y):
    delta_x = grid_x[:, None, :] - gathered[0][:, :, None]
    delta_y = grid_y[:, None, :] - gathered[1][:, :, None]
    powers = 0.5 * (gathered[2][:, :, None] * delta_x * delta_x + 2.0 * gathered[3][:, :, None] * delta_x * delta_y + gathered[4][:, :, None] * delta_y * delta_y)
    alphas = gathered[5][:, :, None] * jnp.exp(-powers)
    kept_log = jnp.log1p(-alphas)
    before = jnp.cumsum(kept_log, axis=1) - kept_log
    weights = alphas * jnp.exp(before)
    colour = jnp.einsum('skp,csk->scp', weights, gathered[6:9], precision=HIGHEST)
    return jnp.concatenate([colour, lax.optimization_barrier(jnp.sum(kept_log, axis=1))[:, None, :]], axis=1)

def pixel_grid(owners, blocks_used, strip_rows, block_cols):
    inner = jnp.arange(128).astype(jnp.int32)
    corner_y = owners * strip_rows + blocks_used // block_cols * 8
    corner_x = blocks_used % block_cols * 16
    grid_y = (corner_y[:, None] + inner[None, :] // 16).astype(jnp.float32) + 0.5
    grid_x = (corner_x[:, None] + inner[None, :] % 16).astype(jnp.float32) + 0.5
    return (grid_x, grid_y)

def composite(pieces, target_ids, depth_ranks, backdrop, block_rows, block_cols):
    block_count = block_rows * block_cols
    onehot = (target_ids[:, :, None] == jnp.arange(block_count).astype(jnp.int32)[None, None, :]).astype(jnp.float32)
    dense = jnp.einsum('scb,scqp->bsqp', onehot, pieces, precision=HIGHEST)
    kept_log = dense[:, :, 3]
    nearer = (depth_ranks[None, :] < depth_ranks[:, None]).astype(jnp.float32)
    before = jnp.einsum('st,btp->bsp', nearer, kept_log, precision=HIGHEST)
    picture = jnp.einsum('bsp,bscp->bcp', jnp.exp(before), dense[:, :, 0:3], precision=HIGHEST)
    picture = picture + backdrop[None, :, None] * jnp.exp(lax.optimization_barrier(jnp.sum(kept_log, axis=1)))[:, None, :]
    picture = picture.reshape(block_rows, block_cols, 3, 8, 16).transpose(2, 0, 3, 1, 4)
    return picture.reshape(3, block_rows * 8, block_cols * 16)

def blur_taps():
    raw_taps = [math.exp(-(offset - 5) * (offset - 5) / 4.5) for offset in range(11)]
    total = sum(raw_taps)
    return [value / total for value in raw_taps]

def blur(values, count):
    taps = blur_taps()
    width_px = values.shape[2]
    padded = jnp.pad(values, ((0, 0), (0, 0), (5, 5)))
    across = taps[0] * padded[:, :, 0:width_px]
    for offset in range(1, 11):
        across = across + taps[offset] * padded[:, :, offset:offset + width_px]
    result = taps[0] * across[:, 0:count]
    for offset in range(1, 11):
        result = result + taps[offset] * across[:, offset:offset + count]
    return result

def pixel_terms(picture, goal, count):
    mean_a = blur(picture, count)
    mean_b = blur(goal, count)
    var_a = blur(picture * picture, count) - mean_a * mean_a
    var_b = blur(goal * goal, count) - mean_b * mean_b
    cov_ab = blur(picture * goal, count) - mean_a * mean_b
    ssim = (2.0 * mean_a * mean_b + SSIM_FIRST) * (2.0 * cov_ab + SSIM_SECOND) / ((mean_a * mean_a + mean_b * mean_b + SSIM_FIRST) * (var_a + var_b + SSIM_SECOND))
    differ = picture[:, 5:5 + count] - goal[:, 5:5 + count]
    return 0.8 * jnp.sqrt(differ * differ + SMOOTHING) + 0.2 * (1.0 - ssim)

def reference(params, visible, blocks, counts, depth_rank, camera, background, target):
    subs_count = visible.shape[0]
    slot_total = visible.shape[1]
    capacity = slot_total // subs_count
    height_px = ROWS_DEV * subs_count
    width_px = IMG_W
    block_rows = ROWS_DEV // 8
    block_cols = IMG_W // 16
    slot_owner = (jnp.arange(slot_total) // capacity).astype(jnp.int32)
    live = jnp.arange(capacity).astype(jnp.int32)[None, None, :] < counts[:, :, None]
    target_ids = jnp.where(live, blocks.reshape(subs_count, subs_count, capacity), -1).astype(jnp.int32)
    grad_total = jnp.zeros(params.shape, jnp.float32)
    pictures = []
    losses = []
    for view_index in range(N_VIEW):

        def view_sum(param_in):
            records = project(param_in, camera[view_index], 0.5 * width_px, 0.5 * height_px)

            def one_sender(sender):
                local = lax.dynamic_slice_in_dim(records, sender * SPL, SPL, 1)
                lists = lax.dynamic_index_in_dim(visible, sender, 0, keepdims=False)
                slot_blocks = lax.dynamic_index_in_dim(blocks, sender, 0, keepdims=False)
                grid_x, grid_y = pixel_grid(slot_owner, slot_blocks, ROWS_DEV, block_cols)
                return render(local[:, lists], grid_x, grid_y)
            segments = lax.map(jax.checkpoint(one_sender), jnp.arange(subs_count).astype(jnp.int32))
            segments = segments.reshape(subs_count, subs_count, capacity, 4, 128)

            def one_owner(owner):
                pieces = lax.dynamic_index_in_dim(segments, owner, 1, keepdims=False)
                owned_ids = lax.dynamic_index_in_dim(target_ids, owner, 1, keepdims=False)
                return composite(pieces, owned_ids, depth_rank[view_index], background[view_index], block_rows, block_cols)
            strips = lax.map(jax.checkpoint(one_owner), jnp.arange(subs_count).astype(jnp.int32))
            picture = strips.transpose(1, 0, 2, 3).reshape(3, height_px, width_px)
            padded = jnp.pad(picture, ((0, 0), (5, 5), (0, 0)))
            goal = jnp.pad(target[view_index], ((0, 0), (5, 5), (0, 0)))
            return (jnp.sum(pixel_terms(padded, goal, height_px)), picture)
        (view_total, picture), view_grad = jax.value_and_grad(view_sum, has_aux=True)(params)
        grad_total = grad_total + view_grad
        pictures.append(picture)
        losses.append(view_total / (3.0 * height_px * width_px))
    return (grad_total, jnp.stack(pictures), jnp.stack(losses))
```

```python
import functools
import math

import jax
import jax.numpy as jnp
from jax import lax
from jax.experimental import pallas as pl
from jax.experimental.pallas import tpu as pltpu
from jax.sharding import PartitionSpec as P

F32 = jnp.float32
BF16 = jnp.bfloat16
I32 = jnp.int32
LANES = 128
LOG2E = 1.4426950408889634
SH_ZERO = 0.28209479177387814
SH_ONE = 0.4886025119029199
SH_TWO = (
    1.0925484305920792,
    -1.0925484305920792,
    0.31539156525252005,
    -1.0925484305920792,
    0.5462742152960396,
)
SH_THREE = (
    -0.5900435899266435,
    2.890611442640554,
    -0.4570457994644658,
    0.3731763325901154,
    -0.4570457994644658,
    1.445305721320277,
    -0.5900435899266435,
)
DILATION = 0.3
SMOOTHING = 0.0001
SSIM_FIRST = 0.0001
SSIM_SECOND = 0.0009


def camera_rotation(angles):
    cos_a, sin_a = (jnp.cos(angles[0]), jnp.sin(angles[0]))
    cos_b, sin_b = (jnp.cos(angles[1]), jnp.sin(angles[1]))
    cos_c, sin_c = (jnp.cos(angles[2]), jnp.sin(angles[2]))
    return [
        [cos_c * cos_b, cos_c * sin_b * sin_a - sin_c * cos_a, cos_c * sin_b * cos_a + sin_c * sin_a],
        [sin_c * cos_b, sin_c * sin_b * sin_a + cos_c * cos_a, sin_c * sin_b * cos_a - cos_c * sin_a],
        [-sin_b, cos_b * sin_a, cos_b * cos_a],
    ]


def harmonics(view_axis):
    axis_x, axis_y, axis_z = (view_axis[0], view_axis[1], view_axis[2])
    sq_x, sq_y, sq_z = (axis_x * axis_x, axis_y * axis_y, axis_z * axis_z)
    return [
        SH_ZERO * jnp.ones_like(axis_x),
        -SH_ONE * axis_y,
        SH_ONE * axis_z,
        -SH_ONE * axis_x,
        SH_TWO[0] * axis_x * axis_y,
        SH_TWO[1] * axis_y * axis_z,
        SH_TWO[2] * (2.0 * sq_z - sq_x - sq_y),
        SH_TWO[3] * axis_x * axis_z,
        SH_TWO[4] * (sq_x - sq_y),
        SH_THREE[0] * axis_y * (3.0 * sq_x - sq_y),
        SH_THREE[1] * axis_x * axis_y * axis_z,
        SH_THREE[2] * axis_y * (4.0 * sq_z - sq_x - sq_y),
        SH_THREE[3] * axis_z * (2.0 * sq_z - 3.0 * sq_x - 3.0 * sq_y),
        SH_THREE[4] * axis_x * (4.0 * sq_z - sq_x - sq_y),
        SH_THREE[5] * axis_z * (sq_x - sq_y),
        SH_THREE[6] * axis_x * (sq_x - 3.0 * sq_y),
    ]


def geometry(rows, turns, centre_x, centre_y):
    scales = [jnp.exp(rows[i]) for i in range(3, 6)]
    quat = rows[6:10]
    length = jnp.sqrt(quat[0] * quat[0] + quat[1] * quat[1] + quat[2] * quat[2] + quat[3] * quat[3])
    part_w, part_x, part_y, part_z = [q / length for q in quat]
    spin = [
        [
            1.0 - 2.0 * (part_y * part_y + part_z * part_z),
            2.0 * (part_x * part_y - part_w * part_z),
            2.0 * (part_x * part_z + part_w * part_y),
        ],
        [
            2.0 * (part_x * part_y + part_w * part_z),
            1.0 - 2.0 * (part_x * part_x + part_z * part_z),
            2.0 * (part_y * part_z - part_w * part_x),
        ],
        [
            2.0 * (part_x * part_z - part_w * part_y),
            2.0 * (part_y * part_z + part_w * part_x),
            1.0 - 2.0 * (part_x * part_x + part_y * part_y),
        ],
    ]
    local = [[spin[r][c] * scales[c] for c in range(3)] for r in range(3)]
    opacity = 1.0 / (1.0 + jnp.exp(-rows[10]))
    shift_x = rows[0] - centre_x
    shift_y = rows[1] - centre_y
    records = []
    for turn in turns:
        frame = [
            [
                turn[r][0] * local[0][c] + turn[r][1] * local[1][c] + turn[r][2] * local[2][c]
                for c in range(3)
            ]
            for r in range(2)
        ]
        cov_xx = sum(frame[0][c] * frame[0][c] for c in range(3)) + DILATION
        cov_xy = sum(frame[0][c] * frame[1][c] for c in range(3))
        cov_yy = sum(frame[1][c] * frame[1][c] for c in range(3)) + DILATION
        inverse = 1.0 / (cov_xx * cov_yy - cov_xy * cov_xy)
        mean_u = turn[0][0] * shift_x + turn[0][1] * shift_y + turn[0][2] * rows[2] + centre_x
        mean_w = turn[1][0] * shift_x + turn[1][1] * shift_y + turn[1][2] * rows[2] + centre_y
        records.append(
            [mean_u, mean_w, cov_yy * inverse, -cov_xy * inverse, cov_xx * inverse, opacity]
        )
    return records


def blur_taps():
    raw_taps = [math.exp(-(offset - 5) * (offset - 5) / 4.5) for offset in range(11)]
    total = sum(raw_taps)
    return [value / total for value in raw_taps]


NT = (((1,), (1,)), ((), ()))
COLOURS = 3
HALO = 5
MARGIN = 2 * HALO
OUT_LANES = LANES - 2 * MARGIN


def three_parts(value):
    high = value.astype(BF16)
    rest = value - high.astype(F32)
    middle = rest.astype(BF16)
    low = (rest - middle.astype(F32)).astype(BF16)
    return [high, middle, low]


def iota(shape, axis):
    return lax.broadcasted_iota(I32, shape, axis)


def step_kernel(
    sizes,
    params_hbm, visible_hbm, blocks_hbm, counts_hbm, rank_hbm, camera_hbm, backdrop_hbm, target_hbm,
    grad_out, picture_out, loss_out,
    params_v, visible_v, blocks_v, counts_v, rank_v, camera_v, backdrop_v, target_v,
    flat, fields, lists, head, head_space, head_view, out_msg, in_msg, ret_out, ret_in,
    rec, spread, nearer, further, taps_w, inverse, alpha_s, trans_s, seg, spread_in, goal, image,
    rows_buf, goal_buf, cols_buf, adj, moments, view_grads,
    in_sem, head_send, head_recv, camv_send, camv_recv, msg_send, msg_recv, ret_send, ret_recv,
    goal_send, goal_recv, image_send, image_recv, view_send, view_recv,
):
    devices, views, depth, slots, capacity, strip_rows, width_px, splats = sizes
    me = lax.axis_index("space")
    my_view = lax.axis_index("view")
    param_rows = params_v.shape[0]
    tall = splats // LANES
    block_cols = width_px // 16
    block_rows = strip_rows // 8
    groups = -(-width_px // OUT_LANES)
    subs = -(-COLOURS * groups // 8) * 8
    rows_in = strip_rows + 4 * HALO
    rows_mid = strip_rows + 2 * HALO
    centre_x = 0.5 * width_px
    centre_y = 0.5 * strip_rows * devices
    shift = capacity.bit_length() - 1
    taps = blur_taps()
    peers = [lax.rem(me + d, devices) for d in range(1, devices)]
    partners = [lax.rem(my_view + d, views) for d in range(1, views)]

    barrier = pltpu.get_barrier_semaphore()
    goal[...] = jnp.zeros_like(goal)
    image[...] = jnp.zeros_like(image)
    for peer in peers:
        pl.semaphore_signal(barrier, inc=1, device_id={"space": peer}, device_id_type=pl.DeviceIdType.MESH)
    for peer in partners:
        pl.semaphore_signal(barrier, inc=1, device_id={"view": peer}, device_id_type=pl.DeviceIdType.MESH)
    pairs = [
        (blocks_hbm, blocks_v), (counts_hbm, counts_v), (camera_hbm, camera_v), (params_hbm, params_v),
        (visible_hbm.at[0], visible_v), (rank_hbm, rank_v), (backdrop_hbm, backdrop_v), (target_hbm.at[0], target_v),
    ]
    fetches = [pltpu.make_async_copy(a, b, in_sem.at[i]) for i, (a, b) in enumerate(pairs)]
    for fetch in fetches:
        fetch.start()

    lane = iota((1, LANES), 1)
    chunk = lax.shift_right_logical(lane, shift)
    for fetch in fetches[0:3]:
        fetch.wait()
    counted = jnp.zeros((1, LANES), I32)
    for o in range(devices):
        counted = jnp.where(chunk == o, counts_v[:, o : o + 1], counted)
    live = (lane & (capacity - 1)) < counted
    head[...] = jnp.zeros_like(head)
    head[0:1, :] = jnp.where(live, blocks_v[...], -1).astype(F32)
    head[1:2, 0:3] = camera_v[...]
    head_space[me] = head[...]
    head_view[my_view] = head[...]
    pl.semaphore_wait(barrier, devices - 1 + views - 1)
    sends = []

    def remote(src, dst, send, recv, target):
        return pltpu.make_async_remote_copy(
            src_ref=src, dst_ref=dst, send_sem=send, recv_sem=recv, device_id=target,
            device_id_type=pl.DeviceIdType.MESH,
        )

    heads = [remote(head, head_space.at[me], head_send.at[d], head_recv.at[d], {"space": peer}) for d, peer in enumerate(peers)]
    heads += [remote(head, head_view.at[my_view], camv_send.at[d], camv_recv.at[d], {"view": peer}) for d, peer in enumerate(partners)]
    for copy in heads:
        copy.start()

    fetches[3].wait()
    for tile in range(-(-param_rows // 8)):
        size = min(8, param_rows - 8 * tile)
        for i in range(tall):
            start = (tile * tall + i) * 8
            flat[start : start + size, :] = params_v[8 * tile : 8 * tile + size, i * LANES : (i + 1) * LANES]

    def param_row(row):
        return flat[pl.ds(row // 8 * tall * 8 + row % 8, tall, stride=8), :]

    def turn_of(angles):
        return camera_rotation([angles[:, i : i + 1] for i in range(3)])

    turn = turn_of(camera_v[...])
    record = geometry([param_row(i) for i in range(11)], [turn], centre_x, centre_y)[0]
    basis = harmonics(turn[2])
    for c in range(COLOURS):
        colour = 0.5 + basis[0] * param_row(11 + c)
        for i in range(1, 16):
            colour = colour + basis[i] * param_row(11 + 3 * i + c)
        record.append(colour)
    for f in range(9):
        fields[f] = record[f]
    fetches[4].wait()
    listed = jnp.transpose(visible_v[...])
    lists[0] = lax.shift_right_logical(listed, 7)
    lists[1] = listed & (LANES - 1)
    picked = [[] for _ in range(9)]
    for half in range(depth // 8):
        high = lists[0, half * 8 : half * 8 + 8, :]
        low = lists[1, half * 8 : half * 8 + 8, :]
        for f in range(9):
            value = jnp.zeros((8, LANES), F32)
            for h in range(tall):
                row = jnp.broadcast_to(fields[f, h : h + 1, :], (8, LANES))
                row = jnp.take_along_axis(row, low, axis=1, mode="promise_in_bounds")
                value = jnp.where(high == h, row, value)
            picked[f].append(value)
    picked = [jnp.concatenate(p, axis=0) for p in picked]

    per_tile = LANES // capacity

    def pack(values, dst):
        for o in range(devices):
            for t in range(-(-len(values) // per_tile)):
                block = None
                for j, value in enumerate(values[t * per_tile : (t + 1) * per_tile]):
                    moved = pltpu.roll(value, (j - o) * capacity % LANES, axis=1)
                    block = moved if block is None else jnp.where(chunk == j, moved, block)
                dst[o, t * depth : (t + 1) * depth, :] = block

    def unpack(src, f):
        t, j = divmod(f, per_tile)
        value = None
        for s in range(devices):
            moved = pltpu.roll(src[s, t * depth : (t + 1) * depth, :], (s - j) * capacity % LANES, axis=1)
            value = moved if value is None else jnp.where(chunk == s, moved, value)
        return value

    pack(picked, out_msg)
    records_out = [
        remote(out_msg.at[peer], in_msg.at[me], msg_send.at[d], msg_recv.at[d], {"space": peer})
        for d, peer in enumerate(peers)
    ]
    for copy in records_out:
        copy.start()
    in_msg[me] = out_msg[me]

    for copy in heads[0 : devices - 1]:
        copy.wait_recv()
    owned = jnp.zeros((1, LANES), F32)
    for s in range(devices):
        amount = lax.rem(s - me + devices, devices) * capacity
        owned = jnp.where(chunk == s, pltpu.roll(head_space[s], amount, axis=1)[0:1, :], owned)
    owned_i = owned.astype(I32)
    fetches[5].wait()
    ranks = jnp.zeros((1, LANES), I32)
    for s in range(devices):
        ranks = jnp.where(chunk == s, rank_v[:, s : s + 1], ranks)
    square = (LANES, LANES)
    diagonal = iota(square, 0) == iota(square, 1)
    ranks_f = ranks.astype(F32)
    owned_c = jnp.sum(jnp.where(diagonal, owned, 0.0), axis=1, keepdims=True)
    ranks_c = jnp.sum(jnp.where(diagonal, ranks_f, 0.0), axis=1, keepdims=True)
    same = owned_c == owned
    fwd_mask = jnp.where(same & (ranks_c < ranks_f), 1.0, 0.0).astype(BF16)
    bwd_mask = jnp.where(same & (ranks_c > ranks_f), 1.0, 0.0).astype(BF16)
    for part in range(3):
        nearer[part * LANES : (part + 1) * LANES, :] = fwd_mask
        further[part * LANES : (part + 1) * LANES, :] = bwd_mask

    def spread_rows(index, carry):
        band = index // 8
        b = band // groups
        g = band - b * groups
        column = iota((16, LANES), 0) + (OUT_LANES * g - MARGIN + (index - band * 8) * 16)
        place = jnp.where((column >= 0) & (column < width_px), column + b * width_px, -4096)
        for c in range(16):
            spread[pl.ds(pl.multiple_of(index * 16, 16), 16), c * LANES : (c + 1) * LANES] = jnp.where(
                place == owned_i * 16 + c, 1.0, 0.0
            ).astype(BF16)
        return carry

    lax.fori_loop(0, block_rows * groups * 8, spread_rows, 0)

    offset = iota(square, 1) - iota(square, 0)
    taps_high = jnp.zeros(square, F32)
    for i in range(11):
        taps_high = jnp.where(offset == i - HALO, taps[i], taps_high)
    taps_parts = three_parts(taps_high)
    for part in range(3):
        taps_w[part * LANES : (part + 1) * LANES, 0:LANES] = taps_parts[0]
        taps_w[part * LANES : (part + 1) * LANES, LANES : 2 * LANES] = taps_parts[1]

    slot_value = lane.astype(F32)

    def invert(k, total):
        high = lists[0, pl.ds(k, 1), :]
        low = lists[1, pl.ds(k, 1), :]
        hit = iota((tall, LANES), 0) == high
        left = jnp.concatenate(
            [jnp.where(hit, slot_value, 0.0), jnp.where(hit, k.astype(F32), 0.0)], axis=0
        ).astype(BF16)
        right = jnp.where(iota(square, 0) == low, 1.0, 0.0).astype(BF16)
        return total + lax.dot_general(left, right, NT, preferred_element_type=F32)

    inverse[...] = lax.fori_loop(0, depth, invert, jnp.zeros((2 * tall, LANES), F32)).astype(I32)

    def column_of(g):
        return lane + (OUT_LANES * g - MARGIN)

    def to_groups(natural, g):
        first = OUT_LANES * g - MARGIN
        left, by = divmod(first, LANES)
        value = jnp.zeros((8, LANES), F32)
        for piece in (left, left + 1):
            if 0 <= piece < width_px // LANES:
                moved = pltpu.roll(natural[:, piece * LANES : (piece + 1) * LANES], -by % LANES, axis=1)
                keep = (lane < LANES - by) if piece == left else (lane >= LANES - by)
                value = jnp.where(keep, moved, value)
        return value

    def own_rows(b, sub):
        return pl.ds((MARGIN + b * 8) * subs + sub, 8, stride=subs)

    fetches[7].wait()
    for ch in range(COLOURS):
        for b in range(block_rows):
            natural = target_v[ch, b * 8 : b * 8 + 8, :]
            for g in range(groups):
                goal[own_rows(b, ch * groups + g), :] = to_groups(natural, g)

    reach = MARGIN * subs
    top, bottom = MARGIN * subs, strip_rows * subs

    def exchange(ref, send, recv):
        upward = remote(
            ref.at[pl.ds(top, reach)], ref.at[pl.ds((MARGIN + strip_rows) * subs, reach)],
            send.at[0], recv.at[0], {"space": lax.rem(me + devices - 1, devices)},
        )
        downward = remote(
            ref.at[pl.ds(bottom, reach)], ref.at[pl.ds(0, reach)],
            send.at[1], recv.at[1], {"space": lax.rem(me + 1, devices)},
        )
        return upward, downward

    not_first, not_last = me > 0, me < devices - 1

    def begin(copies):
        pl.when(not_first)(copies[0].start)
        pl.when(not_last)(copies[1].start)

    def arrived(copies):
        pl.when(not_last)(copies[0].wait_recv)
        pl.when(not_first)(copies[1].wait_recv)

    def left(copies):
        pl.when(not_first)(copies[0].wait_send)
        pl.when(not_last)(copies[1].wait_send)

    goal_copies = exchange(goal, goal_send, goal_recv)
    begin(goal_copies)

    for copy in records_out:
        copy.wait_recv()
    own_ids = jnp.maximum(owned, 0.0)
    block_y = jnp.floor((own_ids + 0.5) * (1.0 / block_cols))
    block_x = own_ids - block_y * block_cols
    corner_x = block_x * 16.0 + 0.5
    corner_y = block_y * 8.0 + (me * strip_rows).astype(F32) + 0.5
    got = [unpack(in_msg, f) for f in range(9)]
    rec[0] = corner_x - got[0]
    rec[1] = corner_y - got[1]
    rec[2] = -0.5 * LOG2E * got[2]
    rec[3] = -LOG2E * got[3]
    rec[4] = -0.5 * LOG2E * got[4]
    rec[5] = jnp.log2(got[5])
    for f in range(6, 9):
        rec[f] = got[f]
    for f in range(2, 6):
        rec[7 + f] = got[f]
    vreg = (8, LANES)
    rows_f = iota(vreg, 0).astype(F32)

    def wide(f, k):
        return jnp.broadcast_to(rec[f, k : k + 1, :], vreg)

    width_c = 4

    def render_some(index, carry):
        trans = [jnp.ones(vreg, F32)] * width_c
        logs = [jnp.zeros(vreg, F32)] * width_c
        run = [None] * width_c
        sums = [[jnp.zeros(vreg, F32)] * width_c for _ in range(COLOURS)]
        base = (index * width_c).astype(F32)
        for k in range(depth):
            delta_y = wide(1, k) + rows_f
            cross = wide(3, k) * delta_y
            square_y = wide(4, k) * delta_y * delta_y + wide(5, k)
            first_x = wide(0, k) + base
            curve = wide(2, k)
            tint = [wide(6 + ch, k) for ch in range(COLOURS)]
            for j in range(width_c):
                delta_x = first_x + float(j)
                alpha = jnp.exp2((curve * delta_x + cross) * delta_x + square_y)
                place = pl.ds(pl.multiple_of((index * width_c + j) * 8, 8), 8)
                alpha_s[k, place, :] = alpha
                trans_s[k, place, :] = trans[j]
                weight = alpha * trans[j]
                for ch in range(COLOURS):
                    sums[ch][j] = sums[ch][j] + weight * tint[ch]
                kept = 1.0 - alpha
                trans[j] = trans[j] * kept
                run[j] = kept if k % 4 == 0 else run[j] * kept
                if k % 4 == 3 or k == depth - 1:
                    logs[j] = logs[j] + jnp.log(run[j])
        for j in range(width_c):
            place = pl.ds(pl.multiple_of((index * width_c + j) * 8, 8), 8)
            for ch in range(COLOURS):
                seg[ch, place, :] = sums[ch][j]
            seg[3, place, :] = trans[j]
            seg[4, place, :] = logs[j]
        return carry

    lax.fori_loop(0, 16 // width_c, render_some, 0)

    before = jnp.dot(
        jnp.concatenate(three_parts(seg[4]), axis=1), nearer[...], preferred_element_type=F32
    )
    seg[4] = jnp.exp(before)
    fetches[6].wait()
    backs = [backdrop_v[:, ch : ch + 1] for ch in range(COLOURS)]
    spread_in[COLOURS * 8 : COLOURS * 8 + 8, :] = jnp.zeros((8, 16 * LANES), F32)
    for c in range(16):
        part = slice(c * 8, c * 8 + 8)
        share = seg[4, part, :]
        taken = 1.0 - seg[3, part, :]
        for ch in range(COLOURS):
            tinted = seg[ch, part, :] - backs[ch] * taken
            seg[ch, part, :] = tinted
            spread_in[ch * 8 : ch * 8 + 8, c * LANES : (c + 1) * LANES] = share * tinted
    rows32 = COLOURS * 8 + 8
    spread_out = lax.dot_general(
        jnp.concatenate(three_parts(spread_in[...]), axis=0), spread[...], NT, preferred_element_type=F32
    )
    spread_out = spread_out[0:rows32] + spread_out[rows32 : 2 * rows32] + spread_out[2 * rows32 : 3 * rows32]
    for g in range(groups):
        on_image = (column_of(g) >= 0) & (column_of(g) < width_px)
        for ch in range(COLOURS):
            for b in range(block_rows):
                value = spread_out[ch * 8 : ch * 8 + 8, (b * groups + g) * LANES : (b * groups + g + 1) * LANES]
                image[own_rows(b, ch * groups + g), :] = value + jnp.where(on_image, backs[ch], 0.0)
    image_copies = exchange(image, image_send, image_recv)
    begin(image_copies)

    for ch in range(COLOURS):
        for b in range(block_rows):
            for j in range(width_px // LANES):
                natural = jnp.zeros(vreg, F32)
                for g in range(groups):
                    first = OUT_LANES * g
                    if first < (j + 1) * LANES and first + OUT_LANES > j * LANES:
                        moved = pltpu.roll(
                            image[own_rows(b, ch * groups + g), :], (first - MARGIN - j * LANES) % LANES, axis=1
                        )
                        here = lane + j * LANES
                        natural = jnp.where((here >= first) & (here < first + OUT_LANES), moved, natural)
                picture_out[0, ch, b * 8 : b * 8 + 8, j * LANES : (j + 1) * LANES] = natural

    def blur_rows(load, count, store):
        for half in range(subs // 8):
            lines = [load(y, half) for y in range(count + 10)]
            for y in range(count):
                total = taps[5] * lines[y + 5]
                for i in range(5):
                    total = total + taps[i] * (lines[y + i] + lines[y + 10 - i])
                store(y, half, total)

    def reader(ref):
        return lambda y, half: ref[y * subs + half * 8 : y * subs + half * 8 + 8, :]

    def writer(ref, base):
        def store(y, half, value):
            ref[base + y * subs + half * 8 : base + y * subs + half * 8 + 8, :] = value

        return store

    def blur_columns(value):
        both = jnp.dot(jnp.concatenate(three_parts(value), axis=1), taps_w[...], preferred_element_type=F32)
        return both[:, 0:LANES] + both[:, LANES : 2 * LANES]

    mid = rows_mid * subs
    from_goal, from_image = reader(goal), reader(image)
    arrived(goal_copies)
    blur_rows(from_goal, rows_mid, writer(rows_buf, 0))
    blur_rows(lambda y, h: from_goal(y, h) * from_goal(y, h), rows_mid, writer(rows_buf, mid))
    goal_buf[...] = blur_columns(rows_buf[0 : 2 * mid, :])

    arrived(image_copies)
    blur_rows(from_image, rows_mid, writer(rows_buf, 0))
    blur_rows(lambda y, h: from_image(y, h) * from_image(y, h), rows_mid, writer(rows_buf, mid))
    blur_rows(lambda y, h: from_image(y, h) * from_goal(y, h), rows_mid, writer(rows_buf, 2 * mid))
    cols_buf[...] = blur_columns(rows_buf[...])

    two = 2 * subs
    sub_row = iota((two, LANES), 0)
    upper = sub_row >= subs
    in_sub = jnp.where(upper, sub_row - subs, sub_row)
    for _ in range(COLOURS - 1):
        in_sub = jnp.where(in_sub >= groups, in_sub - groups, in_sub)
    own_column = iota((two, LANES), 1) + in_sub * OUT_LANES - MARGIN
    used = jnp.where(upper, sub_row - subs, sub_row) < COLOURS * groups
    on_columns = (own_column >= 0) & (own_column < width_px) & used
    inner = (iota((two, LANES), 1) >= MARGIN) & (iota((two, LANES), 1) < MARGIN + OUT_LANES)
    height_px = strip_rows * devices

    def similarity(index, total):
        at = pl.multiple_of(index * two, 8)
        mean_a = cols_buf[pl.ds(at, two), :]
        raw_aa = cols_buf[pl.ds(at + mid, two), :]
        raw_ab = cols_buf[pl.ds(at + 2 * mid, two), :]
        mean_b = goal_buf[pl.ds(at, two), :]
        raw_bb = goal_buf[pl.ds(at + mid, two), :]
        pixel_a = image[pl.ds(at + HALO * subs, two), :]
        pixel_b = goal[pl.ds(at + HALO * subs, two), :]
        line = index * 2 + jnp.where(upper, 1, 0)
        y = line + (me * strip_rows - HALO)
        counted_here = on_columns & (y >= 0) & (y < height_px)
        square_a, square_b, cross = mean_a * mean_a, mean_b * mean_b, mean_a * mean_b
        first_n = 2.0 * cross + SSIM_FIRST
        second_n = 2.0 * (raw_ab - cross) + SSIM_SECOND
        first_d = square_a + square_b + SSIM_FIRST
        second_d = (raw_aa - square_a) + (raw_bb - square_b) + SSIM_SECOND
        scale = 1.0 / (first_d * second_d)
        ssim = first_n * second_n * scale
        inv_first, inv_second = second_d * scale, first_d * scale
        seed = jnp.where(counted_here, -0.2, 0.0)
        by_aa = -ssim * inv_second
        by_ab = 2.0 * first_n * scale
        by_a = 2.0 * (mean_b * second_n * scale - mean_a * (ssim * inv_first + by_aa)) - mean_b * by_ab
        adj[pl.ds(at, two), :] = seed * by_a
        adj[pl.ds(at + mid, two), :] = seed * by_aa
        adj[pl.ds(at + 2 * mid, two), :] = seed * by_ab
        differ = pixel_a - pixel_b
        term = 0.8 * jnp.sqrt(differ * differ + SMOOTHING) + 0.2 * (1.0 - ssim)
        own = counted_here & inner & (line >= HALO) & (line < HALO + strip_rows)
        return total + jnp.where(own, term, 0.0)

    own_terms = lax.fori_loop(0, rows_mid // 2, similarity, jnp.zeros((two, LANES), F32))
    own_loss = jnp.sum(jnp.sum(own_terms, axis=1, keepdims=True), axis=0, keepdims=True)

    end = strip_rows * subs
    for q in range(3):
        blur_rows(lambda y, h: reader(adj)(y + q * rows_mid, h), strip_rows, writer(rows_buf, q * end))
    cols_buf[0 : 3 * end, :] = blur_columns(rows_buf[0 : 3 * end, :])

    def pixel_grad(index, carry):
        at = pl.multiple_of(index * two, 8)
        pixel_a = image[pl.ds(at + MARGIN * subs, two), :]
        pixel_b = goal[pl.ds(at + MARGIN * subs, two), :]
        differ = pixel_a - pixel_b
        value = (
            cols_buf[pl.ds(at, two), :]
            + 2.0 * pixel_a * cols_buf[pl.ds(at + end, two), :]
            + pixel_b * cols_buf[pl.ds(at + 2 * end, two), :]
            + 0.8 * differ / jnp.sqrt(differ * differ + SMOOTHING)
        )
        adj[pl.ds(at, two), :] = jnp.where(on_columns & inner, value, 0.0)
        return carry

    lax.fori_loop(0, strip_rows // 2, pixel_grad, 0)

    pulled = []
    for ch in range(COLOURS):
        pulled.append(
            jnp.concatenate(
                [
                    adj[pl.ds(b * 8 * subs + ch * groups + g, 8, stride=subs), :]
                    for b in range(block_rows)
                    for g in range(groups)
                ],
                axis=1,
            )
        )
    pulled.append(jnp.zeros_like(pulled[0]))
    pulled = jnp.dot(
        jnp.concatenate(three_parts(jnp.concatenate(pulled, axis=0)), axis=0),
        spread[...],
        preferred_element_type=F32,
    )
    spread_in[...] = pulled[0:rows32] + pulled[rows32 : 2 * rows32] + pulled[2 * rows32 : 3 * rows32]
    for c in range(16):
        part = slice(c * 8, c * 8 + 8)
        share = seg[4, part, :]
        by_share, by_trans = None, None
        for ch in range(COLOURS):
            grad = spread_in[ch * 8 : ch * 8 + 8, c * LANES : (c + 1) * LANES]
            piece = grad * seg[ch, part, :]
            by_share = piece if by_share is None else by_share + piece
            grad = grad * share
            seg[ch, part, :] = grad
            piece = grad * backs[ch]
            by_trans = piece if by_trans is None else by_trans + piece
        rows_buf[part, :] = by_share * share
        cols_buf[part, :] = by_trans
    by_log = jnp.dot(
        jnp.concatenate(three_parts(rows_buf[0:LANES, :]), axis=1), further[...], preferred_element_type=F32
    )
    trans = seg[3]
    visible_through = trans > 2e-38
    cols_buf[0:LANES, :] += jnp.where(visible_through, by_log / jnp.where(visible_through, trans, 1.0), 0.0)

    def unrender(step, carry):
        k = depth - 1 - step
        row = pl.ds(k, 1)

        def across(f):
            return jnp.broadcast_to(rec[f, row, :], vreg)

        delta_y = across(1) + rows_f
        first_x = across(0)
        tint = [across(6 + ch) for ch in range(COLOURS)]
        sums = [jnp.zeros(vreg, F32)] * 6
        for c in range(16):
            part = slice(c * 8, c * 8 + 8)
            alpha = alpha_s[k, part, :]
            weight = alpha * trans_s[k, part, :]
            behind = cols_buf[part, :]
            grads = [seg[ch, part, :] for ch in range(COLOURS)]
            gap = grads[0] * tint[0] + grads[1] * tint[1] + grads[2] * tint[2] - behind
            cols_buf[part, :] = behind + alpha * gap
            slope = weight * gap
            delta_x = first_x + float(c)
            slope_x = slope * delta_x
            terms = [slope, slope_x, slope_x * delta_x] + [weight * g for g in grads]
            sums = [a + b for a, b in zip(sums, terms)]
        rows = [
            sums[0], sums[1], sums[0] * delta_y, sums[2], sums[1] * delta_y, sums[0] * delta_y * delta_y,
            sums[3], sums[4], sums[5],
        ]
        for f, value in enumerate(rows):
            moments[f, row, :] = jnp.sum(value, axis=0, keepdims=True)
        return carry

    lax.fori_loop(0, depth, unrender, 0)
    conic_a, conic_b, conic_c, opaque = [rec[9 + i] for i in range(4)]
    grads_out = [
        conic_a * moments[1] + conic_b * moments[2],
        conic_b * moments[1] + conic_c * moments[2],
        -0.5 * moments[3],
        -moments[4],
        -0.5 * moments[5],
        moments[0] / opaque,
        moments[6],
        moments[7],
        moments[8],
        jnp.broadcast_to(own_loss, (depth, LANES)),
    ]
    pack(grads_out, ret_out)
    grads_back = [
        remote(ret_out.at[peer], ret_in.at[me], ret_send.at[d], ret_recv.at[d], {"space": peer})
        for d, peer in enumerate(peers)
    ]
    for copy in grads_back:
        copy.start()
    ret_in[me] = ret_out[me]
    for copy in grads_back:
        copy.wait_recv()

    for f in range(9):
        fields[f] = unpack(ret_in, f)
    tile, j = divmod(9, per_tile)
    total_loss = jnp.zeros((1, 1), F32)
    for s in range(devices):
        total_loss = total_loss + ret_in[s, tile * depth : tile * depth + 1, j * capacity : j * capacity + 1]
    loss_out[...] = total_loss / (3.0 * height_px * width_px)
    for half in range(tall // 8):
        slot_of = inverse[half * 8 : half * 8 + 8, :]
        entry_of = inverse[tall + half * 8 : tall + half * 8 + 8, :]
        for f in range(9):
            value = jnp.zeros(vreg, F32)
            for h in range(depth):
                row = jnp.broadcast_to(fields[f, h : h + 1, :], vreg)
                row = jnp.take_along_axis(row, slot_of, axis=1, mode="promise_in_bounds")
                value = jnp.where(entry_of == h, row, value)
            view_grads[my_view, f, half * 8 : half * 8 + 8, :] = value
    views_out = [
        remote(view_grads.at[my_view], view_grads.at[my_view], view_send.at[d], view_recv.at[d], {"view": peer})
        for d, peer in enumerate(partners)
    ]
    for copy in views_out:
        copy.start()
    for copy in heads[devices - 1 :]:
        copy.wait_recv()
    turns = [turn_of(head_view[v, 1:2, :]) for v in range(views)]
    bases = [harmonics(turn[2]) for turn in turns]
    for copy in views_out:
        copy.wait_recv()

    def put_row(row, value):
        flat[pl.ds(row // 8 * tall * 8 + row % 8, tall, stride=8), :] = value

    pull = jax.vjp(lambda r: geometry(r, turns, centre_x, centre_y), [param_row(i) for i in range(11)])[1]
    for i, value in enumerate(pull([[view_grads[v, f] for f in range(6)] for v in range(views)])[0]):
        put_row(i, value)
    for c in range(COLOURS):
        by_colour = [view_grads[v, 6 + c] for v in range(views)]
        for i in range(16):
            value = bases[0][i] * by_colour[0]
            for v in range(1, views):
                value = value + bases[v][i] * by_colour[v]
            put_row(11 + 3 * i + c, value)
    for tile in range(-(-param_rows // 8)):
        size = min(8, param_rows - 8 * tile)
        for i in range(tall):
            start = (tile * tall + i) * 8
            grad_out[8 * tile : 8 * tile + size, i * LANES : (i + 1) * LANES] = flat[start : start + size, :]
    for copy in heads + records_out + grads_back + views_out:
        copy.wait_send()
    left(goal_copies)
    left(image_copies)


def shards(params, visible, blocks, counts, depth_rank, camera, background, target):
    devices, views = lax.axis_size("space"), lax.axis_size("view")
    slots, depth = visible.shape[1:]
    capacity = slots // devices
    strip_rows, width_px = target.shape[2:]
    splats = params.shape[1]
    tall = splats // LANES
    groups = -(-width_px // OUT_LANES)
    subs = -(-COLOURS * groups // 8) * 8
    rows_in, rows_mid = strip_rows + 4 * HALO, strip_rows + 2 * HALO
    sizes = (devices, views, depth, slots, capacity, strip_rows, width_px, splats)
    per_tile = LANES // capacity
    tiles_out, tiles_back = -(-9 // per_tile), -(-10 // per_tile)
    vmem = lambda *shape: pltpu.VMEM(shape, F32)
    dma = lambda count: pltpu.SemaphoreType.DMA((count,))
    scratch = [
        vmem(*params.shape), pltpu.VMEM((slots, depth), I32), pltpu.VMEM(blocks.shape, I32),
        pltpu.VMEM(counts.shape, I32), pltpu.VMEM(depth_rank.shape, I32), vmem(*camera.shape),
        vmem(*background.shape), vmem(*target.shape[1:]),
        vmem(-(-params.shape[0] // 8) * tall * 8, LANES), vmem(9, tall, LANES), pltpu.VMEM((2, depth, LANES), I32),
        vmem(8, LANES), vmem(devices, 8, LANES), vmem(views, 8, LANES),
        vmem(devices, tiles_out * depth, LANES), vmem(devices, tiles_out * depth, LANES),
        vmem(devices, tiles_back * depth, LANES), vmem(devices, tiles_back * depth, LANES),
        vmem(13, depth, LANES), pltpu.VMEM((strip_rows // 8 * groups * LANES, 16 * LANES), BF16),
        pltpu.VMEM((3 * LANES, LANES), BF16), pltpu.VMEM((3 * LANES, LANES), BF16),
        pltpu.VMEM((3 * LANES, 2 * LANES), BF16), pltpu.VMEM((2 * tall, LANES), I32),
        vmem(depth, LANES, LANES), vmem(depth, LANES, LANES), vmem(5, LANES, LANES),
        vmem(COLOURS * 8 + 8, 16 * LANES), vmem(rows_in * subs, LANES), vmem(rows_in * subs, LANES),
        vmem(3 * rows_mid * subs, LANES), vmem(2 * rows_mid * subs, LANES), vmem(3 * rows_mid * subs, LANES),
        vmem(3 * rows_mid * subs, LANES), vmem(9, depth, LANES), vmem(views, 9, tall, LANES),
        dma(8), dma(devices), dma(devices), dma(views), dma(views), dma(devices), dma(devices), dma(devices),
        dma(devices), dma(2), dma(2), dma(2), dma(2), dma(views), dma(views),
    ]
    grad, picture, loss = pl.pallas_call(
        functools.partial(step_kernel, sizes),
        name="step",
        out_shape=(
            jax.ShapeDtypeStruct(params.shape, F32),
            jax.ShapeDtypeStruct(target.shape, F32),
            jax.ShapeDtypeStruct((1, 1), F32),
        ),
        in_specs=[pl.BlockSpec(memory_space=pl.ANY)] * 8,
        out_specs=tuple([pl.BlockSpec(memory_space=pltpu.VMEM)] * 3),
        scratch_shapes=scratch,
        compiler_params=pltpu.CompilerParams(collective_id=0, has_side_effects=True),
    )(params, visible, blocks, counts, depth_rank, camera, background, target)
    return (grad, picture, loss.reshape(1))


def solution(mesh):
    in_specs = (
        P(None, "space"),
        P("space", None, None),
        P("space", None),
        P("space", None),
        P("view", None),
        P("view", None),
        P("view", None),
        P("view", None, "space", None),
    )
    out_specs = (P(None, "space"), P("view", None, "space", None), P("view"))
    return jax.shard_map(shards, mesh=mesh, in_specs=in_specs, out_specs=out_specs, check_vma=False)
```

```python
import functools
import math

import jax
import jax.numpy as jnp
import numpy as np
from jax import lax
from jax.experimental import pallas as pl
from jax.experimental.pallas import tpu as pltpu
from jax.sharding import PartitionSpec as P

F32 = jnp.float32
BF16 = jnp.bfloat16
I32 = jnp.int32
LANES = 128
LOG2E = 1.4426950408889634
SH_ZERO = 0.28209479177387814
SH_ONE = 0.4886025119029199
SH_TWO = (
    1.0925484305920792,
    -1.0925484305920792,
    0.31539156525252005,
    -1.0925484305920792,
    0.5462742152960396,
)
SH_THREE = (
    -0.5900435899266435,
    2.890611442640554,
    -0.4570457994644658,
    0.3731763325901154,
    -0.4570457994644658,
    1.445305721320277,
    -0.5900435899266435,
)
DILATION = 0.3
SMOOTHING = 0.0001
SSIM_FIRST = 0.0001
SSIM_SECOND = 0.0009


def camera_rotation(angles):
    cos_a, sin_a = (jnp.cos(angles[0]), jnp.sin(angles[0]))
    cos_b, sin_b = (jnp.cos(angles[1]), jnp.sin(angles[1]))
    cos_c, sin_c = (jnp.cos(angles[2]), jnp.sin(angles[2]))
    return [
        [cos_c * cos_b, cos_c * sin_b * sin_a - sin_c * cos_a, cos_c * sin_b * cos_a + sin_c * sin_a],
        [sin_c * cos_b, sin_c * sin_b * sin_a + cos_c * cos_a, sin_c * sin_b * cos_a - cos_c * sin_a],
        [-sin_b, cos_b * sin_a, cos_b * cos_a],
    ]


def harmonics(view_axis):
    axis_x, axis_y, axis_z = (view_axis[0], view_axis[1], view_axis[2])
    sq_x, sq_y, sq_z = (axis_x * axis_x, axis_y * axis_y, axis_z * axis_z)
    return [
        SH_ZERO * jnp.ones_like(axis_x),
        -SH_ONE * axis_y,
        SH_ONE * axis_z,
        -SH_ONE * axis_x,
        SH_TWO[0] * axis_x * axis_y,
        SH_TWO[1] * axis_y * axis_z,
        SH_TWO[2] * (2.0 * sq_z - sq_x - sq_y),
        SH_TWO[3] * axis_x * axis_z,
        SH_TWO[4] * (sq_x - sq_y),
        SH_THREE[0] * axis_y * (3.0 * sq_x - sq_y),
        SH_THREE[1] * axis_x * axis_y * axis_z,
        SH_THREE[2] * axis_y * (4.0 * sq_z - sq_x - sq_y),
        SH_THREE[3] * axis_z * (2.0 * sq_z - 3.0 * sq_x - 3.0 * sq_y),
        SH_THREE[4] * axis_x * (4.0 * sq_z - sq_x - sq_y),
        SH_THREE[5] * axis_z * (sq_x - sq_y),
        SH_THREE[6] * axis_x * (sq_x - 3.0 * sq_y),
    ]


def geometry(rows, turns, centre_x, centre_y):
    scales = [jnp.exp(rows[i]) for i in range(3, 6)]
    quat = rows[6:10]
    length = jnp.sqrt(quat[0] * quat[0] + quat[1] * quat[1] + quat[2] * quat[2] + quat[3] * quat[3])
    part_w, part_x, part_y, part_z = [q / length for q in quat]
    spin = [
        [
            1.0 - 2.0 * (part_y * part_y + part_z * part_z),
            2.0 * (part_x * part_y - part_w * part_z),
            2.0 * (part_x * part_z + part_w * part_y),
        ],
        [
            2.0 * (part_x * part_y + part_w * part_z),
            1.0 - 2.0 * (part_x * part_x + part_z * part_z),
            2.0 * (part_y * part_z - part_w * part_x),
        ],
        [
            2.0 * (part_x * part_z - part_w * part_y),
            2.0 * (part_y * part_z + part_w * part_x),
            1.0 - 2.0 * (part_x * part_x + part_y * part_y),
        ],
    ]
    local = [[spin[r][c] * scales[c] for c in range(3)] for r in range(3)]
    opacity = 1.0 / (1.0 + jnp.exp(-rows[10]))
    shift_x = rows[0] - centre_x
    shift_y = rows[1] - centre_y
    records = []
    for turn in turns:
        frame = [
            [
                turn[r][0] * local[0][c] + turn[r][1] * local[1][c] + turn[r][2] * local[2][c]
                for c in range(3)
            ]
            for r in range(2)
        ]
        cov_xx = sum(frame[0][c] * frame[0][c] for c in range(3)) + DILATION
        cov_xy = sum(frame[0][c] * frame[1][c] for c in range(3))
        cov_yy = sum(frame[1][c] * frame[1][c] for c in range(3)) + DILATION
        inverse = 1.0 / (cov_xx * cov_yy - cov_xy * cov_xy)
        mean_u = turn[0][0] * shift_x + turn[0][1] * shift_y + turn[0][2] * rows[2] + centre_x
        mean_w = turn[1][0] * shift_x + turn[1][1] * shift_y + turn[1][2] * rows[2] + centre_y
        records.append(
            [mean_u, mean_w, cov_yy * inverse, -cov_xy * inverse, cov_xx * inverse, opacity]
        )
    return records


def blur_taps():
    raw_taps = [math.exp(-(offset - 5) * (offset - 5) / 4.5) for offset in range(11)]
    total = sum(raw_taps)
    return [value / total for value in raw_taps]


NT = (((1,), (1,)), ((), ()))
COLOURS = 3
HALO = 5
MARGIN = 2 * HALO
TABLE = 32


def three_parts(value):
    high = value.astype(BF16)
    rest = value - high.astype(F32)
    middle = rest.astype(BF16)
    low = (rest - middle.astype(F32)).astype(BF16)
    return [high, middle, low]


def iota(shape, axis):
    return lax.broadcasted_iota(I32, shape, axis)


def swap_chunks(values, width):
    lane = iota((1, LANES), 1)
    for bit in range(3):
        step = 1 << bit
        low = (lane & (width * step)) == 0
        moved = list(values)
        for a in range(8):
            if not a & step:
                first, second = values[a], values[a | step]
                moved[a] = jnp.where(low, first, pltpu.roll(second, width * step, axis=1))
                moved[a | step] = jnp.where(low, pltpu.roll(first, LANES - width * step, axis=1), second)
        values = moved
    return values


def swap_sublanes(value, width):
    lane, row = iota((8, LANES), 1), iota((8, LANES), 0)
    for bit in range(3):
        step = 1 << bit
        low_lane, low_row = (lane & (width * step)) == 0, (row & step) == 0
        up = pltpu.roll(pltpu.roll(value, 8 - step, axis=0), width * step, axis=1)
        down = pltpu.roll(pltpu.roll(value, step, axis=0), LANES - width * step, axis=1)
        value = jnp.where(low_lane == low_row, value, jnp.where(low_row, up, down))
    return value


def step_kernel(
    sizes,
    params_hbm, visible_hbm, blocks_hbm, counts_hbm, rank_hbm, camera_hbm, backdrop_hbm, target_hbm,
    view_grads, table_out, picture_out, loss_out,
    params_v, visible_v, blocks_v, counts_v, rank_v, camera_v, backdrop_v, target_v,
    flat, fields, lists, head, head_view, out_msg, in_msg, ret_out, ret_in,
    rec, place_f, place_b, nearer, further, taps_w, inverse, alpha_s, trans_s, seg, goal, image,
    rows_buf, goal_buf, cols_buf, adj, seed_s, own_s, moments,
    in_sem, camv_send, camv_recv, msg_send, msg_recv, ret_send, ret_recv,
    goal_send, goal_recv, image_send, image_recv, view_send, view_recv,
):
    devices, views, depth, slots, capacity, strip_rows, width_px, splats = sizes
    me = lax.axis_index("space")
    my_view = lax.axis_index("view")
    param_rows = params_v.shape[0]
    tall = splats // LANES
    block_cols = width_px // 16
    block_rows = strip_rows // 8
    groups = width_px // LANES
    subs = COLOURS * groups
    bands = block_rows * groups
    rows_in = strip_rows + 4 * HALO
    rows_mid = strip_rows + 2 * HALO
    centre_x = 0.5 * width_px
    centre_y = 0.5 * strip_rows * devices
    shift = capacity.bit_length() - 1
    taps = blur_taps()
    peers = [lax.rem(me + d, devices) for d in range(1, devices)]
    partners = [lax.rem(my_view + d, views) for d in range(1, views)]

    barrier = pltpu.get_barrier_semaphore()
    goal[...] = jnp.zeros_like(goal)
    image[...] = jnp.zeros_like(image)
    for peer in peers:
        pl.semaphore_signal(barrier, inc=1, device_id={"space": peer}, device_id_type=pl.DeviceIdType.MESH)
    for peer in partners:
        pl.semaphore_signal(barrier, inc=1, device_id={"view": peer}, device_id_type=pl.DeviceIdType.MESH)
    pairs = [
        (blocks_hbm, blocks_v), (counts_hbm, counts_v), (camera_hbm, camera_v), (params_hbm, params_v),
        (visible_hbm.at[0], visible_v), (rank_hbm, rank_v), (backdrop_hbm, backdrop_v), (target_hbm.at[0], target_v),
    ]
    fetches = [pltpu.make_async_copy(a, b, in_sem.at[i]) for i, (a, b) in enumerate(pairs)]
    for fetch in fetches:
        fetch.start()

    lane = iota((1, LANES), 1)
    chunk = lax.shift_right_logical(lane, shift)
    for fetch in fetches[0:3]:
        fetch.wait()
    counted = jnp.zeros((1, LANES), I32)
    for o in range(devices):
        counted = jnp.where(chunk == o, counts_v[:, o : o + 1], counted)
    live = (lane & (capacity - 1)) < counted
    ids_row = jnp.where(live, blocks_v[...], -1).astype(F32)
    head[...] = jnp.zeros_like(head)
    head[0:1, 0:3] = camera_v[...]
    head_view[my_view] = head[...]

    def remote(src, dst, send, recv, target):
        return pltpu.make_async_remote_copy(
            src_ref=src, dst_ref=dst, send_sem=send, recv_sem=recv, device_id=target,
            device_id_type=pl.DeviceIdType.MESH,
        )

    fetches[3].wait()
    for tile in range(-(-param_rows // 8)):
        size = min(8, param_rows - 8 * tile)
        for i in range(tall):
            start = (tile * tall + i) * 8
            flat[start : start + size, :] = params_v[8 * tile : 8 * tile + size, i * LANES : (i + 1) * LANES]

    def param_row(row):
        return flat[pl.ds(row // 8 * tall * 8 + row % 8, tall, stride=8), :]

    def turn_of(angles):
        return camera_rotation([angles[:, i : i + 1] for i in range(3)])

    turn = turn_of(camera_v[...])
    record = geometry([param_row(i) for i in range(11)], [turn], centre_x, centre_y)[0]
    basis = harmonics(turn[2])
    for c in range(COLOURS):
        colour = 0.5 + basis[0] * param_row(11 + c)
        for i in range(1, 16):
            colour = colour + basis[i] * param_row(11 + 3 * i + c)
        record.append(colour)
    for f in range(9):
        fields[f] = record[f]
    fetches[4].wait()
    listed = visible_v[...]
    lists[0] = lax.shift_right_logical(listed, 7)
    lists[1] = listed & (LANES - 1)
    picked = [[] for _ in range(9)]
    for half in range(depth // 8):
        high = lists[0, half * 8 : half * 8 + 8, :]
        low = lists[1, half * 8 : half * 8 + 8, :]
        for f in range(9):
            value = jnp.zeros((8, LANES), F32)
            for h in range(tall):
                row = jnp.broadcast_to(fields[f, h : h + 1, :], (8, LANES))
                row = jnp.take_along_axis(row, low, axis=1, mode="promise_in_bounds")
                value = jnp.where(high == h, row, value)
            picked[f].append(value)
    picked = [jnp.concatenate(p, axis=0) for p in picked]

    per_tile = LANES // capacity
    dense = devices == 8 and per_tile == 8 and depth == 16
    body = depth + 2 if dense else depth * -(-9 // per_tile)

    def pack(values, extra, dst):
        if dense:
            for o, block in enumerate(swap_chunks(values[0:8], capacity)):
                dst[o, 0:depth, :] = block
            for half in range(2):
                last = swap_sublanes(values[8][half * 8 : half * 8 + 8], capacity)
                for o in range(devices):
                    dst[o, depth + half : depth + half + 1, :] = last[o : o + 1]
        for o in range(devices):
            dst[o, body : body + 1, :] = extra
            for t in range(0 if dense else -(-len(values) // per_tile)):
                block = None
                for j, value in enumerate(values[t * per_tile : (t + 1) * per_tile]):
                    moved = pltpu.roll(value, (j - o) * capacity % LANES, axis=1)
                    block = moved if block is None else jnp.where(chunk == j, moved, block)
                dst[o, t * depth : (t + 1) * depth, :] = block

    def unpack(src):
        if dense:
            values = swap_chunks([src[o, 0:depth, :] for o in range(devices)], capacity)
            last = [
                jnp.concatenate([src[o, depth + half : depth + half + 1, :] for o in range(devices)], axis=0)
                for half in range(2)
            ]
            return values + [jnp.concatenate([swap_sublanes(v, capacity) for v in last], axis=0)]
        values = []
        for f in range(9):
            t, j = divmod(f, per_tile)
            value = None
            for s in range(devices):
                moved = pltpu.roll(src[s, t * depth : (t + 1) * depth, :], (s - j) * capacity % LANES, axis=1)
                value = moved if value is None else jnp.where(chunk == s, moved, value)
            values.append(value)
        return values

    pack(picked, ids_row, out_msg)
    pl.semaphore_wait(barrier, devices - 1 + views - 1)
    records_out = [
        remote(out_msg.at[peer], in_msg.at[me], msg_send.at[d], msg_recv.at[d], {"space": peer})
        for d, peer in enumerate(peers)
    ]
    for copy in records_out:
        copy.start()
    cameras = [
        remote(head, head_view.at[my_view], camv_send.at[d], camv_recv.at[d], {"view": peer})
        for d, peer in enumerate(partners)
    ]
    for copy in cameras:
        copy.start()
    in_msg[me] = out_msg[me]

    def own_rows(b, sub):
        return pl.ds((MARGIN + b * 8) * subs + sub, 8, stride=subs)

    fetches[7].wait()
    for ch in range(COLOURS):
        for b in range(block_rows):
            for g in range(groups):
                goal[own_rows(b, ch * groups + g), :] = target_v[ch, b * 8 : b * 8 + 8, g * LANES : (g + 1) * LANES]

    reach = MARGIN * subs
    top, bottom = MARGIN * subs, strip_rows * subs

    def exchange(ref, send, recv):
        upward = remote(
            ref.at[pl.ds(top, reach)], ref.at[pl.ds((MARGIN + strip_rows) * subs, reach)],
            send.at[0], recv.at[0], {"space": lax.rem(me + devices - 1, devices)},
        )
        downward = remote(
            ref.at[pl.ds(bottom, reach)], ref.at[pl.ds(0, reach)],
            send.at[1], recv.at[1], {"space": lax.rem(me + 1, devices)},
        )
        return upward, downward

    not_first, not_last = me > 0, me < devices - 1

    def begin(copies):
        pl.when(not_first)(copies[0].start)
        pl.when(not_last)(copies[1].start)

    def arrived(copies):
        pl.when(not_last)(copies[0].wait_recv)
        pl.when(not_first)(copies[1].wait_recv)

    def left(copies):
        pl.when(not_first)(copies[0].wait_send)
        pl.when(not_last)(copies[1].wait_send)

    goal_copies = exchange(goal, goal_send, goal_recv)
    begin(goal_copies)

    square = (LANES, LANES)
    fetches[5].wait()
    ranks = jnp.zeros((1, LANES), I32)
    for s in range(devices):
        ranks = jnp.where(chunk == s, rank_v[:, s : s + 1], ranks)
    offset = iota(square, 1) - iota(square, 0)
    near = iota(square, 0) < LANES // 2
    beside = jnp.where(near, offset - LANES, offset + LANES)
    exact = [np.float32(tap) for tap in taps]
    highs = [float(tap.astype(jnp.bfloat16)) for tap in exact]
    lows = [float((tap - np.float32(high)).astype(jnp.bfloat16)) for tap, high in zip(exact, highs)]
    blur_norm = float(1.0 / (sum(highs) + sum(lows)))
    for side, values in enumerate((highs, lows)):
        for part, distance in enumerate((offset, beside)):
            weights = jnp.zeros(square, F32)
            for i in range(11):
                weights = jnp.where(distance == i - HALO, values[i], weights)
            weights = weights.astype(BF16)
            for term in range(3):
                start = (term * 2 + part) * LANES
                taps_w[start : start + LANES, side * LANES : (side + 1) * LANES] = weights

    slot_value = lane.astype(F32)

    def invert(k, total):
        high = lists[0, pl.ds(k, 1), :]
        low = lists[1, pl.ds(k, 1), :]
        hit = iota((tall, LANES), 0) == high
        left = jnp.concatenate(
            [jnp.where(hit, slot_value, 0.0), jnp.where(hit, k.astype(F32), 0.0)], axis=0
        ).astype(BF16)
        right = jnp.where(iota(square, 0) == low, 1.0, 0.0).astype(BF16)
        return total + lax.dot_general(left, right, NT, preferred_element_type=F32)

    inverse[...] = lax.fori_loop(0, depth, invert, jnp.zeros((2 * tall, LANES), F32)).astype(I32)

    height_px = strip_rows * devices
    mid, end = rows_mid * subs, strip_rows * subs
    for at in range(0, mid, 8):
        line = iota((8, LANES), 0) + at
        row_y = (line.astype(F32) + 0.5) * (1.0 / subs)
        y = row_y + (me * strip_rows - HALO).astype(F32)
        counts_here = (y > 0.0) & (y < float(height_px))
        seed_s[at : at + 8, :] = jnp.where(counts_here, -0.2, 0.0)
        own_s[at : at + 8, :] = jnp.where((row_y > HALO) & (row_y < HALO + strip_rows), 1.0, 0.0)

    for copy in records_out:
        copy.wait_recv()
    owned = jnp.zeros((1, LANES), F32)
    for s in range(devices):
        amount = lax.rem(s - me + devices, devices) * capacity
        owned = jnp.where(chunk == s, pltpu.roll(in_msg[s, body : body + 1, :], amount, axis=1), owned)
    own_ids = jnp.maximum(owned, 0.0)
    block_y = jnp.floor((own_ids + 0.5) * (1.0 / block_cols))
    block_x = own_ids - block_y * block_cols
    corner_x = block_x * 16.0 + 0.5
    corner_y = block_y * 8.0 + (me * strip_rows).astype(F32) + 0.5
    got = unpack(in_msg)
    rec[0] = corner_x - got[0]
    rec[1] = corner_y - got[1]
    rec[2] = -0.5 * LOG2E * got[2]
    rec[3] = -LOG2E * got[3]
    rec[4] = -0.5 * LOG2E * got[4]
    rec[5] = jnp.log2(got[5])
    for f in range(6, 9):
        rec[f] = got[f]
    for f in range(2, 6):
        rec[7 + f] = got[f]
    vreg = (8, LANES)
    rows_f = iota(vreg, 0).astype(F32)

    def wide(f, k):
        return jnp.broadcast_to(rec[f, k : k + 1, :], vreg)

    width_c = 4

    def render_some(index, carry):
        trans = [jnp.ones(vreg, F32)] * width_c
        logs = [jnp.zeros(vreg, F32)] * width_c
        run = [None] * width_c
        sums = [[jnp.zeros(vreg, F32)] * width_c for _ in range(COLOURS)]
        base = (index * width_c).astype(F32)
        for k in range(depth):
            delta_y = wide(1, k) + rows_f
            cross = wide(3, k) * delta_y
            square_y = wide(4, k) * delta_y * delta_y + wide(5, k)
            first_x = wide(0, k) + base
            curve = wide(2, k)
            tint = [wide(6 + ch, k) for ch in range(COLOURS)]
            for j in range(width_c):
                delta_x = first_x + float(j)
                alpha = jnp.exp2((curve * delta_x + cross) * delta_x + square_y)
                place = pl.ds(pl.multiple_of((index * width_c + j) * 8, 8), 8)
                alpha_s[k, place, :] = alpha
                trans_s[k, place, :] = trans[j]
                weight = alpha * trans[j]
                for ch in range(COLOURS):
                    sums[ch][j] = sums[ch][j] + weight * tint[ch]
                kept = 1.0 - alpha
                trans[j] = trans[j] * kept
                run[j] = kept if k % 4 == 0 else run[j] * kept
                if k % 4 == 3 or k == depth - 1:
                    logs[j] = logs[j] + jnp.log(run[j])
        for j in range(width_c):
            place = pl.ds(pl.multiple_of((index * width_c + j) * 8, 8), 8)
            for ch in range(COLOURS):
                seg[ch, place, :] = sums[ch][j]
            seg[3, place, :] = trans[j]
            seg[4, place, :] = logs[j]
        return carry

    lax.fori_loop(0, 16 // width_c, render_some, 0)

    diagonal = iota(square, 0) == iota(square, 1)
    ranks_f = ranks.astype(F32)
    owned_c = jnp.sum(jnp.where(diagonal, owned, 0.0), axis=1, keepdims=True)
    ranks_c = jnp.sum(jnp.where(diagonal, ranks_f, 0.0), axis=1, keepdims=True)
    same = owned_c == owned
    fwd_mask = jnp.where(same & (ranks_c < ranks_f), 1.0, 0.0).astype(BF16)
    bwd_mask = jnp.where(same & (ranks_c > ranks_f), 1.0, 0.0).astype(BF16)
    blocks_here = LANES // 2
    lane_sq, sub_sq = iota(square, 1).astype(F32), iota(square, 0).astype(F32)
    for part in range(3):
        nearer[part * LANES : (part + 1) * LANES, :] = fwd_mask
        further[part * LANES : (part + 1) * LANES, :] = bwd_mask
    for d in range(2):
        alive = owned_c >= 0.0
        forth = jnp.where(alive & (lane_sq == owned_c + d * blocks_here), 1.0, 0.0).astype(BF16)
        back = jnp.where((owned >= 0.0) & (sub_sq == owned + d * blocks_here), 1.0, 0.0).astype(BF16)
        for part in range(3):
            place_f[(part * 2 + d) * LANES : (part * 2 + d + 1) * LANES, :] = forth
            place_b[part * LANES : (part + 1) * LANES, d * LANES : (d + 1) * LANES] = back

    before = jnp.dot(
        jnp.concatenate(three_parts(seg[4]), axis=1), nearer[...], preferred_element_type=F32
    )
    seg[4] = jnp.exp(before)
    fetches[6].wait()
    backs = [backdrop_v[:, ch : ch + 1] for ch in range(COLOURS)]
    shares = [[None] * 16 for _ in range(COLOURS)]
    for c in range(16):
        part = slice(c * 8, c * 8 + 8)
        share = seg[4, part, :]
        taken = 1.0 - seg[3, part, :]
        for ch in range(COLOURS):
            tinted = seg[ch, part, :] - backs[ch] * taken
            seg[ch, part, :] = tinted
            shares[ch][c] = share * tinted
    across_lanes = iota(vreg, 1)
    to_natural = (across_lanes & 15) * 8 + lax.shift_right_logical(across_lanes, 4)
    from_natural = (across_lanes & 7) * 16 + lax.shift_right_logical(across_lanes, 3)
    for ch in range(COLOURS):
        paired = jnp.concatenate(
            [jnp.concatenate([shares[ch][c], shares[ch][c + 8]], axis=1) for c in range(8)], axis=0
        )
        placed = jnp.dot(
            jnp.concatenate(three_parts(paired), axis=1), place_f[...], preferred_element_type=F32
        )
        for q, value in enumerate(swap_chunks([placed[c * 8 : c * 8 + 8] for c in range(8)], 8)):
            b, g = divmod(q, groups)
            value = jnp.take_along_axis(value, to_natural, axis=1, mode="promise_in_bounds") + backs[ch]
            image[own_rows(b, ch * groups + g), :] = value
            picture_out[0, ch, b * 8 : b * 8 + 8, g * LANES : (g + 1) * LANES] = value
    image_copies = exchange(image, image_send, image_recv)
    begin(image_copies)

    def blur_rows(load, count, store):
        seen = {}

        def line(at):
            if at not in seen:
                seen[at] = load(at)
            return seen[at]

        for at in range(0, count * subs, 8):
            total = taps[5] * line(at + 5 * subs)
            for i in range(5):
                total = total + taps[i] * (line(at + i * subs) + line(at + (10 - i) * subs))
            store(at, total)

    def reader(ref, base=0):
        return lambda at: ref[base + at : base + at + 8, :]

    def writer(base):
        def store(at, value):
            rows_buf[8 + base + at : 16 + base + at, :] = value

        return store

    sub_group = iota((1, 8, LANES), 1) & (groups - 1)
    low_lanes = iota((1, 8, LANES), 2) < LANES // 2
    from_right = low_lanes & (sub_group < groups - 1)
    from_left = jnp.logical_not(low_lanes) & (sub_group > 0)

    def blur_columns(first, size):
        def read(at):
            return rows_buf[at : at + size, :].reshape(size // 8, 8, LANES)

        rim = jnp.where(from_right, read(first + 9), jnp.where(from_left, read(first + 7), 0.0))
        own_parts = three_parts(rows_buf[first + 8 : first + 8 + size, :])
        rim_parts = three_parts(rim.reshape(size, LANES))
        both = jnp.dot(
            jnp.concatenate([v for pair in zip(own_parts, rim_parts) for v in pair], axis=1),
            taps_w[...],
            preferred_element_type=F32,
        )
        return (both[:, 0:LANES] + both[:, LANES : 2 * LANES]) * blur_norm

    def blur_all(total, dst):
        half = -(-total // 32) * 16
        dst[0:half, :] = blur_columns(0, half)
        dst[half:total, :] = blur_columns(half, total - half)

    arrived(goal_copies)
    from_goal, from_image = reader(goal), reader(image)
    rows_buf[0:8, :] = jnp.zeros_like(rows_buf[0:8, :])
    rows_buf[8 + 3 * mid : 16 + 3 * mid, :] = jnp.zeros_like(rows_buf[0:8, :])
    blur_rows(from_goal, rows_mid, writer(0))
    blur_rows(lambda at: from_goal(at) * from_goal(at), rows_mid, writer(mid))
    blur_all(2 * mid, goal_buf)

    arrived(image_copies)
    blur_rows(from_image, rows_mid, writer(0))
    blur_rows(lambda at: from_image(at) * from_image(at), rows_mid, writer(mid))
    blur_rows(lambda at: from_image(at) * from_goal(at), rows_mid, writer(2 * mid))
    blur_all(3 * mid, cols_buf)

    step_rows = mid // 3

    def similarity(index, total):
        at = pl.multiple_of(index * step_rows, 8)

        def take(ref, base):
            return ref[pl.ds(at + base, step_rows), :]

        mean_a, raw_aa, raw_ab = take(cols_buf, 0), take(cols_buf, mid), take(cols_buf, 2 * mid)
        mean_b, raw_bb = take(goal_buf, 0), take(goal_buf, mid)
        pixel_a, pixel_b = take(image, HALO * subs), take(goal, HALO * subs)
        seed = take(seed_s, 0)
        square_a, square_b, cross = mean_a * mean_a, mean_b * mean_b, mean_a * mean_b
        first_n = 2.0 * cross + SSIM_FIRST
        second_n = 2.0 * (raw_ab - cross) + SSIM_SECOND
        first_d = square_a + square_b + SSIM_FIRST
        second_d = (raw_aa - square_a) + (raw_bb - square_b) + SSIM_SECOND
        scale = 1.0 / (first_d * second_d)
        ssim = first_n * second_n * scale
        inv_first, inv_second = second_d * scale, first_d * scale
        by_aa = -ssim * inv_second
        by_ab = 2.0 * first_n * scale
        by_a = 2.0 * (mean_b * second_n * scale - mean_a * (ssim * inv_first + by_aa)) - mean_b * by_ab
        adj[pl.ds(at, step_rows), :] = seed * by_a
        adj[pl.ds(at + mid, step_rows), :] = seed * by_aa
        adj[pl.ds(at + 2 * mid, step_rows), :] = seed * by_ab
        differ = pixel_a - pixel_b
        term = 0.8 * jnp.sqrt(differ * differ + SMOOTHING) + 0.2 * (1.0 - ssim)
        return total + term * take(own_s, 0)

    own_terms = lax.fori_loop(0, 3, similarity, jnp.zeros((step_rows, LANES), F32))
    own_loss = jnp.sum(jnp.sum(own_terms, axis=1, keepdims=True), axis=0, keepdims=True)

    for q in range(3):
        blur_rows(reader(adj, q * mid), strip_rows, writer(q * end))
    blur_all(3 * end, cols_buf)
    pixel_a = image[MARGIN * subs : MARGIN * subs + end, :]
    pixel_b = goal[MARGIN * subs : MARGIN * subs + end, :]
    differ = pixel_a - pixel_b
    adj[0:end, :] = (
        cols_buf[0:end, :]
        + 2.0 * pixel_a * cols_buf[end : 2 * end, :]
        + pixel_b * cols_buf[2 * end : 3 * end, :]
        + 0.8 * differ * lax.rsqrt(differ * differ + SMOOTHING)
    )

    pulled = []
    for ch in range(COLOURS):
        bands_here = []
        for q in range(bands):
            b, g = divmod(q, groups)
            value = adj[pl.ds(b * 8 * subs + ch * groups + g, 8, stride=subs), :]
            bands_here.append(jnp.take_along_axis(value, from_natural, axis=1, mode="promise_in_bounds"))
        pulled.append(
            jnp.dot(
                jnp.concatenate(three_parts(jnp.concatenate(swap_chunks(bands_here, 8), axis=0)), axis=1),
                place_b[...],
                preferred_element_type=F32,
            )
        )
    for c in range(16):
        part = slice(c * 8, c * 8 + 8)
        share = seg[4, part, :]
        by_share, by_trans = None, None
        for ch in range(COLOURS):
            grad = pulled[ch][c % 8 * 8 : c % 8 * 8 + 8, c // 8 * LANES : (c // 8 + 1) * LANES]
            piece = grad * seg[ch, part, :]
            by_share = piece if by_share is None else by_share + piece
            grad = grad * share
            seg[ch, part, :] = grad
            piece = grad * backs[ch]
            by_trans = piece if by_trans is None else by_trans + piece
        rows_buf[part, :] = by_share * share
        cols_buf[part, :] = by_trans
    by_log = jnp.dot(
        jnp.concatenate(three_parts(rows_buf[0:LANES, :]), axis=1), further[...], preferred_element_type=F32
    )
    trans = seg[3]
    visible_through = trans > 2e-38
    cols_buf[0:LANES, :] += jnp.where(visible_through, by_log / jnp.where(visible_through, trans, 1.0), 0.0)

    def unrender(step, carry):
        k = depth - 1 - step
        row = pl.ds(k, 1)

        def across(f):
            return jnp.broadcast_to(rec[f, row, :], vreg)

        delta_y = across(1) + rows_f
        first_x = across(0)
        tint = [across(6 + ch) for ch in range(COLOURS)]
        sums = [jnp.zeros(vreg, F32)] * 6
        for c in range(16):
            part = slice(c * 8, c * 8 + 8)
            alpha = alpha_s[k, part, :]
            weight = alpha * trans_s[k, part, :]
            behind = cols_buf[part, :]
            grads = [seg[ch, part, :] for ch in range(COLOURS)]
            gap = grads[0] * tint[0] + grads[1] * tint[1] + grads[2] * tint[2] - behind
            cols_buf[part, :] = behind + alpha * gap
            slope = weight * gap
            delta_x = first_x + float(c)
            slope_x = slope * delta_x
            terms = [slope, slope_x, slope_x * delta_x] + [weight * g for g in grads]
            sums = [a + b for a, b in zip(sums, terms)]
        rows = [
            sums[0], sums[1], sums[0] * delta_y, sums[2], sums[1] * delta_y, sums[0] * delta_y * delta_y,
            sums[3], sums[4], sums[5],
        ]
        for f, value in enumerate(rows):
            moments[f, row, :] = jnp.sum(value, axis=0, keepdims=True)
        return carry

    lax.fori_loop(0, depth, unrender, 0)
    conic_a, conic_b, conic_c, opaque = [rec[9 + i] for i in range(4)]
    grads_out = [
        conic_a * moments[1] + conic_b * moments[2],
        conic_b * moments[1] + conic_c * moments[2],
        -0.5 * moments[3],
        -moments[4],
        -0.5 * moments[5],
        moments[0] / opaque,
        moments[6],
        moments[7],
        moments[8],
    ]
    pack(grads_out, jnp.broadcast_to(own_loss, (1, LANES)), ret_out)
    grads_back = [
        remote(ret_out.at[peer], ret_in.at[me], ret_send.at[d], ret_recv.at[d], {"space": peer})
        for d, peer in enumerate(peers)
    ]
    for copy in grads_back:
        copy.start()
    ret_in[me] = ret_out[me]

    for copy in cameras:
        copy.wait_recv()
    for v in range(views):
        turned = turn_of(head_view[v, 0:1, :])
        for i, value in enumerate([x for row in turned for x in row] + harmonics(turned[2])):
            table_out[v, i : i + 1, :] = jnp.broadcast_to(value, (1, LANES))
    for copy in grads_back:
        copy.wait_recv()

    for f, value in enumerate(unpack(ret_in)):
        fields[f] = value
    total_loss = jnp.zeros((1, 1), F32)
    for s in range(devices):
        total_loss = total_loss + ret_in[s, body : body + 1, 0:1]
    loss_out[...] = total_loss / (3.0 * height_px * width_px)
    pair, across_x = my_view ^ 1, my_view ^ 2

    def forward(block, chunk_at, kind, target):
        piece = view_grads.at[block, pl.ds(chunk_at * 3, 3)]
        return remote(piece, piece, view_send.at[kind * 3 + chunk_at], view_recv.at[kind * 3 + chunk_at], {"view": target})

    views_out = []
    for third in range(3):
        for half in range(tall // 8):
            slot_of = inverse[half * 8 : half * 8 + 8, :]
            entry_of = inverse[tall + half * 8 : tall + half * 8 + 8, :]
            for f in range(third * 3, third * 3 + 3):
                value = jnp.zeros(vreg, F32)
                for h in range(depth):
                    row = jnp.broadcast_to(fields[f, h : h + 1, :], vreg)
                    row = jnp.take_along_axis(row, slot_of, axis=1, mode="promise_in_bounds")
                    value = jnp.where(entry_of == h, row, value)
                view_grads[my_view, f, half * 8 : half * 8 + 8, :] = value
        for kind, target in ((1, across_x), (0, pair)):
            views_out.append(forward(my_view, third, kind, target))
            views_out[-1].start()
    for third in range(3):
        forward(across_x, third, 1, across_x).wait_recv()
        views_out.append(forward(across_x, third, 2, pair))
        views_out[-1].start()
    for third in range(3):
        forward(pair, third, 0, pair).wait_recv()
        forward(my_view ^ 3, third, 2, pair).wait_recv()
    for copy in cameras + records_out + grads_back + views_out:
        copy.wait_send()
    left(goal_copies)
    left(image_copies)


def finish_kernel(sizes, params_ref, grads_ref, table_ref, picture_ref, grad_out, picture_out, flat):
    views, splats, centre_x, centre_y = sizes
    param_rows = params_ref.shape[0]
    tall = splats // LANES
    for tile in range(-(-param_rows // 8)):
        size = min(8, param_rows - 8 * tile)
        for i in range(tall) if tile < 2 else ():
            start = (tile * tall + i) * 8
            flat[start : start + size, :] = params_ref[8 * tile : 8 * tile + size, i * LANES : (i + 1) * LANES]

    def place(row):
        return pl.ds(row // 8 * tall * 8 + row % 8, tall, stride=8)

    turns = [[[table_ref[v, r * 3 + c : r * 3 + c + 1, :] for c in range(3)] for r in range(3)] for v in range(views)]
    bases = [[table_ref[v, 9 + i : 10 + i, :] for i in range(16)] for v in range(views)]
    rows = [flat[place(i), :] for i in range(11)]
    pull = jax.vjp(lambda r: geometry(r, turns, centre_x, centre_y), rows)[1]
    for i, value in enumerate(pull([[grads_ref[v, f] for f in range(6)] for v in range(views)])[0]):
        flat[place(i), :] = value
    for c in range(COLOURS):
        by_colour = [grads_ref[v, 6 + c] for v in range(views)]
        for i in range(16):
            value = bases[0][i] * by_colour[0]
            for v in range(1, views):
                value = value + bases[v][i] * by_colour[v]
            flat[place(11 + 3 * i + c), :] = value
    for tile in range(-(-param_rows // 8)):
        size = min(8, param_rows - 8 * tile)
        for i in range(tall):
            start = (tile * tall + i) * 8
            grad_out[8 * tile : 8 * tile + size, i * LANES : (i + 1) * LANES] = flat[start : start + size, :]
    picture_out[...] = picture_ref[...]


def shards(params, visible, blocks, counts, depth_rank, camera, background, target):
    devices, views = lax.axis_size("space"), lax.axis_size("view")
    slots, depth = visible.shape[1:]
    capacity = slots // devices
    strip_rows, width_px = target.shape[2:]
    splats = params.shape[1]
    tall = splats // LANES
    subs = COLOURS * (width_px // LANES)
    rows_in, rows_mid = strip_rows + 4 * HALO, strip_rows + 2 * HALO
    sizes = (devices, views, depth, slots, capacity, strip_rows, width_px, splats)
    per_tile = LANES // capacity
    dense = devices == 8 and per_tile == 8 and depth == 16
    message = (depth + 2 if dense else depth * -(-9 // per_tile)) + 1
    vmem = lambda *shape: pltpu.VMEM(shape, F32)
    half = lambda *shape: pltpu.VMEM(shape, BF16)
    dma = lambda count: pltpu.SemaphoreType.DMA((count,))
    scratch = [
        vmem(*params.shape), pltpu.VMEM((depth, slots), I32), pltpu.VMEM(blocks.shape, I32),
        pltpu.VMEM(counts.shape, I32), pltpu.VMEM(depth_rank.shape, I32), vmem(*camera.shape),
        vmem(*background.shape), vmem(*target.shape[1:]),
        vmem(-(-params.shape[0] // 8) * tall * 8, LANES), vmem(9, tall, LANES), pltpu.VMEM((2, depth, LANES), I32),
        vmem(8, LANES), vmem(views, 8, LANES),
        vmem(devices, message, LANES), vmem(devices, message, LANES),
        vmem(devices, message, LANES), vmem(devices, message, LANES),
        vmem(13, depth, LANES), half(6 * LANES, LANES), half(3 * LANES, 2 * LANES),
        half(3 * LANES, LANES), half(3 * LANES, LANES),
        half(6 * LANES, 2 * LANES), pltpu.VMEM((2 * tall, LANES), I32),
        vmem(depth, LANES, LANES), vmem(depth, LANES, LANES), vmem(5, LANES, LANES),
        vmem(rows_in * subs, LANES), vmem(rows_in * subs, LANES),
        vmem(3 * rows_mid * subs + 16, LANES), vmem(2 * rows_mid * subs, LANES), vmem(3 * rows_mid * subs, LANES),
        vmem(3 * rows_mid * subs, LANES), vmem(rows_mid * subs, LANES), vmem(rows_mid * subs, LANES),
        vmem(9, depth, LANES),
        dma(8), dma(views), dma(views), dma(devices), dma(devices), dma(devices),
        dma(devices), dma(2), dma(2), dma(2), dma(2), dma(9), dma(9),
    ]
    whole = pl.BlockSpec(memory_space=pltpu.VMEM)
    grads, table, picture, loss = pl.pallas_call(
        functools.partial(step_kernel, sizes),
        name="step",
        out_shape=(
            jax.ShapeDtypeStruct((views, 9, tall, LANES), F32),
            jax.ShapeDtypeStruct((views, TABLE, LANES), F32),
            jax.ShapeDtypeStruct(target.shape, F32),
            jax.ShapeDtypeStruct((1, 1), F32),
        ),
        in_specs=[pl.BlockSpec(memory_space=pltpu.HBM)] * 8,
        out_specs=(whole,) * 4,
        scratch_shapes=scratch,
        compiler_params=pltpu.CompilerParams(
            collective_id=0, has_side_effects=True, vmem_limit_bytes=20 * 1024 * 1024
        ),
    )(*[pltpu.with_memory_space_constraint(x, pltpu.HBM) for x in (params, jnp.swapaxes(visible, 1, 2), blocks, counts, depth_rank, camera, background, target)])
    centre = (0.5 * width_px, 0.5 * strip_rows * devices)
    grad, picture = pl.pallas_call(
        functools.partial(finish_kernel, (views, splats, *centre)),
        name="finish",
        out_shape=(jax.ShapeDtypeStruct(params.shape, F32), jax.ShapeDtypeStruct(target.shape, F32)),
        in_specs=[whole] * 4,
        out_specs=(whole,) * 2,
        scratch_shapes=[vmem(-(-params.shape[0] // 8) * tall * 8, LANES)],
        compiler_params=pltpu.CompilerParams(vmem_limit_bytes=20 * 1024 * 1024),
    )(params, grads, table, picture)
    return (grad, picture, loss.reshape(1))


def solution(mesh):
    in_specs = (
        P(None, "space"),
        P("space", None, None),
        P("space", None),
        P("space", None),
        P("view", None),
        P("view", None),
        P("view", None),
        P("view", None, "space", None),
    )
    out_specs = (P(None, "space"), P("view", None, "space", None), P("view"))
    return jax.shard_map(shards, mesh=mesh, in_specs=in_specs, out_specs=out_specs, check_vma=False)
```

```python
import functools
import math

import jax
import jax.numpy as jnp
import numpy as np
from jax import lax
from jax.experimental import pallas as pl
from jax.experimental.pallas import tpu as pltpu
from jax.sharding import PartitionSpec as P

F32 = jnp.float32
BF16 = jnp.bfloat16
I32 = jnp.int32
LANES = 128
LOG2E = 1.4426950408889634
SH_ZERO = 0.28209479177387814
SH_ONE = 0.4886025119029199
SH_TWO = (
    1.0925484305920792,
    -1.0925484305920792,
    0.31539156525252005,
    -1.0925484305920792,
    0.5462742152960396,
)
SH_THREE = (
    -0.5900435899266435,
    2.890611442640554,
    -0.4570457994644658,
    0.3731763325901154,
    -0.4570457994644658,
    1.445305721320277,
    -0.5900435899266435,
)
DILATION = 0.3
SMOOTHING = 0.0001
SSIM_FIRST = 0.0001
SSIM_SECOND = 0.0009


def camera_rotation(angles):
    cos_a, sin_a = (jnp.cos(angles[0]), jnp.sin(angles[0]))
    cos_b, sin_b = (jnp.cos(angles[1]), jnp.sin(angles[1]))
    cos_c, sin_c = (jnp.cos(angles[2]), jnp.sin(angles[2]))
    return [
        [cos_c * cos_b, cos_c * sin_b * sin_a - sin_c * cos_a, cos_c * sin_b * cos_a + sin_c * sin_a],
        [sin_c * cos_b, sin_c * sin_b * sin_a + cos_c * cos_a, sin_c * sin_b * cos_a - cos_c * sin_a],
        [-sin_b, cos_b * sin_a, cos_b * cos_a],
    ]


def harmonics(view_axis):
    axis_x, axis_y, axis_z = (view_axis[0], view_axis[1], view_axis[2])
    sq_x, sq_y, sq_z = (axis_x * axis_x, axis_y * axis_y, axis_z * axis_z)
    return [
        SH_ZERO * jnp.ones_like(axis_x),
        -SH_ONE * axis_y,
        SH_ONE * axis_z,
        -SH_ONE * axis_x,
        SH_TWO[0] * axis_x * axis_y,
        SH_TWO[1] * axis_y * axis_z,
        SH_TWO[2] * (2.0 * sq_z - sq_x - sq_y),
        SH_TWO[3] * axis_x * axis_z,
        SH_TWO[4] * (sq_x - sq_y),
        SH_THREE[0] * axis_y * (3.0 * sq_x - sq_y),
        SH_THREE[1] * axis_x * axis_y * axis_z,
        SH_THREE[2] * axis_y * (4.0 * sq_z - sq_x - sq_y),
        SH_THREE[3] * axis_z * (2.0 * sq_z - 3.0 * sq_x - 3.0 * sq_y),
        SH_THREE[4] * axis_x * (4.0 * sq_z - sq_x - sq_y),
        SH_THREE[5] * axis_z * (sq_x - sq_y),
        SH_THREE[6] * axis_x * (sq_x - 3.0 * sq_y),
    ]


def geometry(rows, turns, centre_x, centre_y):
    scales = [jnp.exp(rows[i]) for i in range(3, 6)]
    quat = rows[6:10]
    length = jnp.sqrt(quat[0] * quat[0] + quat[1] * quat[1] + quat[2] * quat[2] + quat[3] * quat[3])
    part_w, part_x, part_y, part_z = [q / length for q in quat]
    spin = [
        [
            1.0 - 2.0 * (part_y * part_y + part_z * part_z),
            2.0 * (part_x * part_y - part_w * part_z),
            2.0 * (part_x * part_z + part_w * part_y),
        ],
        [
            2.0 * (part_x * part_y + part_w * part_z),
            1.0 - 2.0 * (part_x * part_x + part_z * part_z),
            2.0 * (part_y * part_z - part_w * part_x),
        ],
        [
            2.0 * (part_x * part_z - part_w * part_y),
            2.0 * (part_y * part_z + part_w * part_x),
            1.0 - 2.0 * (part_x * part_x + part_y * part_y),
        ],
    ]
    local = [[spin[r][c] * scales[c] for c in range(3)] for r in range(3)]
    opacity = 1.0 / (1.0 + jnp.exp(-rows[10]))
    shift_x = rows[0] - centre_x
    shift_y = rows[1] - centre_y
    records = []
    for turn in turns:
        frame = [
            [
                turn[r][0] * local[0][c] + turn[r][1] * local[1][c] + turn[r][2] * local[2][c]
                for c in range(3)
            ]
            for r in range(2)
        ]
        cov_xx = sum(frame[0][c] * frame[0][c] for c in range(3)) + DILATION
        cov_xy = sum(frame[0][c] * frame[1][c] for c in range(3))
        cov_yy = sum(frame[1][c] * frame[1][c] for c in range(3)) + DILATION
        inverse = 1.0 / (cov_xx * cov_yy - cov_xy * cov_xy)
        mean_u = turn[0][0] * shift_x + turn[0][1] * shift_y + turn[0][2] * rows[2] + centre_x
        mean_w = turn[1][0] * shift_x + turn[1][1] * shift_y + turn[1][2] * rows[2] + centre_y
        records.append(
            [mean_u, mean_w, cov_yy * inverse, -cov_xy * inverse, cov_xx * inverse, opacity]
        )
    return records


def blur_taps():
    raw_taps = [math.exp(-(offset - 5) * (offset - 5) / 4.5) for offset in range(11)]
    total = sum(raw_taps)
    return [value / total for value in raw_taps]


NT = (((1,), (1,)), ((), ()))
COLOURS = 3
HALO = 5
MARGIN = 2 * HALO
TABLE = 32


def three_parts(value):
    high = value.astype(BF16)
    rest = value - high.astype(F32)
    middle = rest.astype(BF16)
    low = (rest - middle.astype(F32)).astype(BF16)
    return [high, middle, low]


def iota(shape, axis):
    return lax.broadcasted_iota(I32, shape, axis)


def swap_chunks(values, width):
    lane = iota((1, LANES), 1)
    for bit in range(3):
        step = 1 << bit
        low = (lane & (width * step)) == 0
        moved = list(values)
        for a in range(8):
            if not a & step:
                first, second = values[a], values[a | step]
                moved[a] = jnp.where(low, first, pltpu.roll(second, width * step, axis=1))
                moved[a | step] = jnp.where(low, pltpu.roll(first, LANES - width * step, axis=1), second)
        values = moved
    return values


def swap_sublanes(value, width):
    lane, row = iota((8, LANES), 1), iota((8, LANES), 0)
    for bit in range(3):
        step = 1 << bit
        low_lane, low_row = (lane & (width * step)) == 0, (row & step) == 0
        up = pltpu.roll(pltpu.roll(value, 8 - step, axis=0), width * step, axis=1)
        down = pltpu.roll(pltpu.roll(value, step, axis=0), LANES - width * step, axis=1)
        value = jnp.where(low_lane == low_row, value, jnp.where(low_row, up, down))
    return value


def step_kernel(
    sizes,
    params_hbm, visible_hbm, blocks_hbm, counts_hbm, rank_hbm, camera_hbm, backdrop_hbm, target_hbm,
    view_grads, table_out, picture_out, loss_out,
    params_v, visible_v, blocks_v, counts_v, rank_v, camera_v, backdrop_v, target_v,
    flat, fields, lists, head, head_view, out_msg, in_msg, ret_out, ret_in,
    rec, place_f, place_b, nearer, further, taps_w, inverse, alpha_s, trans_s, seg, goal, image,
    rows_buf, goal_buf, cols_buf, adj, seed_s, own_s, moments,
    in_sem, camv_send, camv_recv, msg_send, msg_recv, ret_send, ret_recv,
    goal_send, goal_recv, image_send, image_recv, view_send, view_recv,
):
    devices, views, depth, slots, capacity, strip_rows, width_px, splats = sizes
    me = lax.axis_index("space")
    my_view = lax.axis_index("view")
    param_rows = params_v.shape[0]
    tall = splats // LANES
    block_cols = width_px // 16
    block_rows = strip_rows // 8
    groups = width_px // LANES
    bands = block_rows * groups
    rows_in = strip_rows + 4 * HALO
    rows_mid = strip_rows + 2 * HALO
    centre_x = 0.5 * width_px
    centre_y = 0.5 * strip_rows * devices
    shift = capacity.bit_length() - 1
    taps = blur_taps()
    peers = [me ^ d for d in range(devices - 1, 0, -1)]
    partners = [my_view ^ d for d in range(1, views)]
    pair, across_x = my_view ^ 1, my_view ^ 2

    barrier = pltpu.get_barrier_semaphore()
    greeted = [{"space": peer, "view": view} for peer in peers for view in (my_view, across_x)]
    greeted += [{"space": me, "view": view} for view in partners]
    for target in greeted:
        pl.semaphore_signal(barrier, inc=1, device_id=target, device_id_type=pl.DeviceIdType.MESH)
    pairs = [
        (blocks_hbm, blocks_v), (counts_hbm, counts_v), (camera_hbm, camera_v), (params_hbm, params_v),
        (visible_hbm.at[0], visible_v), (rank_hbm, rank_v), (backdrop_hbm, backdrop_v), (target_hbm.at[0], target_v),
    ]
    fetches = [pltpu.make_async_copy(a, b, in_sem.at[i]) for i, (a, b) in enumerate(pairs)]
    for fetch in fetches:
        fetch.start()

    rim = MARGIN * groups

    @pl.when(me == 0)
    def _():
        goal[:, 0:rim, :] = jnp.zeros((COLOURS, rim, LANES), F32)
        image[:, 0:rim, :] = jnp.zeros((COLOURS, rim, LANES), F32)

    @pl.when(me == devices - 1)
    def _():
        low = (MARGIN + strip_rows) * groups
        goal[:, low : low + rim, :] = jnp.zeros((COLOURS, rim, LANES), F32)
        image[:, low : low + rim, :] = jnp.zeros((COLOURS, rim, LANES), F32)

    lane = iota((1, LANES), 1)
    chunk = lax.shift_right_logical(lane, shift)
    for fetch in fetches[0:3]:
        fetch.wait()
    counted = jnp.zeros((1, LANES), I32)
    for o in range(devices):
        counted = jnp.where(chunk == o, counts_v[:, o : o + 1], counted)
    live = (lane & (capacity - 1)) < counted
    ids_row = jnp.where(live, blocks_v[...], -1).astype(F32)
    head[...] = jnp.zeros_like(head)
    head[0:1, 0:3] = camera_v[...]
    head_view[my_view] = head[...]

    def remote(src, dst, send, recv, target):
        return pltpu.make_async_remote_copy(
            src_ref=src, dst_ref=dst, send_sem=send, recv_sem=recv, device_id=target,
            device_id_type=pl.DeviceIdType.MESH,
        )

    fetches[3].wait()
    for tile in range(-(-param_rows // 8)):
        size = min(8, param_rows - 8 * tile)
        for i in range(tall):
            start = (tile * tall + i) * 8
            flat[start : start + size, :] = params_v[8 * tile : 8 * tile + size, i * LANES : (i + 1) * LANES]

    def param_row(row):
        return flat[pl.ds(row // 8 * tall * 8 + row % 8, tall, stride=8), :]

    def turn_of(angles):
        return camera_rotation([angles[:, i : i + 1] for i in range(3)])

    turn = turn_of(camera_v[...])
    record = geometry([param_row(i) for i in range(11)], [turn], centre_x, centre_y)[0]
    basis = harmonics(turn[2])
    for c in range(COLOURS):
        colour = 0.5 + basis[0] * param_row(11 + c)
        for i in range(1, 16):
            colour = colour + basis[i] * param_row(11 + 3 * i + c)
        record.append(colour)
    for f in range(9):
        fields[f] = record[f]
    fetches[4].wait()
    listed = visible_v[...]
    lists[0] = lax.shift_right_logical(listed, 7)
    lists[1] = listed & (LANES - 1)
    picked = [[] for _ in range(9)]
    for half in range(depth // 8):
        high = lists[0, half * 8 : half * 8 + 8, :]
        low = lists[1, half * 8 : half * 8 + 8, :]
        for f in range(9):
            value = jnp.zeros((8, LANES), F32)
            for h in range(tall):
                row = jnp.broadcast_to(fields[f, h : h + 1, :], (8, LANES))
                row = jnp.take_along_axis(row, low, axis=1, mode="promise_in_bounds")
                value = jnp.where(high == h, row, value)
            picked[f].append(value)
    picked = [jnp.concatenate(p, axis=0) for p in picked]

    per_tile = LANES // capacity
    dense = devices == 8 and per_tile == 8 and depth == 16
    body = depth + 2 if dense else depth * -(-9 // per_tile)

    def pack(values, extra, dst):
        if dense:
            for o, block in enumerate(swap_chunks(values[0:8], capacity)):
                dst[o, 0:depth, :] = block
            for half in range(2):
                last = swap_sublanes(values[8][half * 8 : half * 8 + 8], capacity)
                for o in range(devices):
                    dst[o, depth + half : depth + half + 1, :] = last[o : o + 1]
        for o in range(devices):
            dst[o, body : body + 1, :] = extra
            for t in range(0 if dense else -(-len(values) // per_tile)):
                block = None
                for j, value in enumerate(values[t * per_tile : (t + 1) * per_tile]):
                    moved = pltpu.roll(value, (j - o) * capacity % LANES, axis=1)
                    block = moved if block is None else jnp.where(chunk == j, moved, block)
                dst[o, t * depth : (t + 1) * depth, :] = block

    def unpack(src):
        if dense:
            values = swap_chunks([src[o, 0:depth, :] for o in range(devices)], capacity)
            last = [
                jnp.concatenate([src[o, depth + half : depth + half + 1, :] for o in range(devices)], axis=0)
                for half in range(2)
            ]
            return values + [jnp.concatenate([swap_sublanes(v, capacity) for v in last], axis=0)]
        values = []
        for f in range(9):
            t, j = divmod(f, per_tile)
            value = None
            for s in range(devices):
                moved = pltpu.roll(src[s, t * depth : (t + 1) * depth, :], (s - j) * capacity % LANES, axis=1)
                value = moved if value is None else jnp.where(chunk == s, moved, value)
            values.append(value)
        return values

    pack(picked, ids_row, out_msg)
    pl.semaphore_wait(barrier, len(greeted))
    records_out = [
        remote(out_msg.at[peer], in_msg.at[me], msg_send.at[d], msg_recv.at[d], {"space": peer})
        for d, peer in enumerate(peers)
    ]
    for copy in records_out:
        copy.start()
    cameras = [
        remote(head, head_view.at[my_view], camv_send.at[d], camv_recv.at[d], {"view": peer})
        for d, peer in enumerate(partners)
    ]
    for copy in cameras:
        copy.start()
    in_msg[me] = out_msg[me]

    def own_rows(b, g):
        return pl.ds((MARGIN + b * 8) * groups + g, 8, stride=groups)

    fetches[7].wait()
    for ch in range(COLOURS):
        for b in range(block_rows):
            for g in range(groups):
                goal[ch, own_rows(b, g), :] = target_v[ch, b * 8 : b * 8 + 8, g * LANES : (g + 1) * LANES]

    top, bottom, below = MARGIN * groups, strip_rows * groups, (MARGIN + strip_rows) * groups

    def exchange(ref, channels, send, recv, at):
        upward = remote(
            ref.at[channels, pl.ds(top, rim)], ref.at[channels, pl.ds(below, rim)],
            send.at[at], recv.at[at], {"space": lax.rem(me + devices - 1, devices)},
        )
        downward = remote(
            ref.at[channels, pl.ds(bottom, rim)], ref.at[channels, pl.ds(0, rim)],
            send.at[at + 1], recv.at[at + 1], {"space": lax.rem(me + 1, devices)},
        )
        return upward, downward

    not_first, not_last = me > 0, me < devices - 1

    def begin(copies):
        pl.when(not_first)(copies[0].start)
        pl.when(not_last)(copies[1].start)

    def arrived(copies):
        pl.when(not_last)(copies[0].wait_recv)
        pl.when(not_first)(copies[1].wait_recv)

    def left(copies):
        pl.when(not_first)(copies[0].wait_send)
        pl.when(not_last)(copies[1].wait_send)

    goal_copies = exchange(goal, slice(None), goal_send, goal_recv, 0)
    begin(goal_copies)

    square = (LANES, LANES)
    fetches[5].wait()
    ranks = jnp.zeros((1, LANES), I32)
    for s in range(devices):
        ranks = jnp.where(chunk == s, rank_v[:, s : s + 1], ranks)
    offset = iota(square, 1) - iota(square, 0)
    near = iota(square, 0) < LANES // 2
    beside = jnp.where(near, offset - LANES, offset + LANES)
    exact = [np.float32(tap) for tap in taps]
    highs = [float(tap.astype(jnp.bfloat16)) for tap in exact]
    lows = [float((tap - np.float32(high)).astype(jnp.bfloat16)) for tap, high in zip(exact, highs)]
    blur_norm = float(1.0 / (sum(highs) + sum(lows)))
    for side, values in enumerate((highs, lows)):
        for part, distance in enumerate((offset, beside)):
            weights = jnp.zeros(square, F32)
            for i in range(11):
                weights = jnp.where(distance == i - HALO, values[i], weights)
            weights = weights.astype(BF16)
            for term in range(3):
                start = (term * 2 + part) * LANES
                taps_w[start : start + LANES, side * LANES : (side + 1) * LANES] = weights

    slot_value = lane.astype(F32)

    def invert(k, total):
        high = lists[0, pl.ds(k, 1), :]
        low = lists[1, pl.ds(k, 1), :]
        hit = iota((tall, LANES), 0) == high
        left = jnp.concatenate(
            [jnp.where(hit, slot_value, 0.0), jnp.where(hit, k.astype(F32), 0.0)], axis=0
        ).astype(BF16)
        right = jnp.where(iota(square, 0) == low, 1.0, 0.0).astype(BF16)
        return total + lax.dot_general(left, right, NT, preferred_element_type=F32)

    inverse[...] = lax.fori_loop(0, depth, invert, jnp.zeros((2 * tall, LANES), F32)).astype(I32)

    height_px = strip_rows * devices
    mid, end = rows_mid * groups, strip_rows * groups
    for at in range(0, mid, 8):
        line = iota((8, LANES), 0) + at
        row_y = (line.astype(F32) + 0.5) * (1.0 / groups)
        y = row_y + (me * strip_rows - HALO).astype(F32)
        counts_here = (y > 0.0) & (y < float(height_px))
        seed_s[at : at + 8, :] = jnp.where(counts_here, -0.2, 0.0)
        own_s[at : at + 8, :] = jnp.where((row_y > HALO) & (row_y < HALO + strip_rows), 1.0, 0.0)

    for copy in records_out:
        copy.wait_recv()
    owned = jnp.zeros((1, LANES), F32)
    for s in range(devices):
        amount = lax.rem(s - me + devices, devices) * capacity
        owned = jnp.where(chunk == s, pltpu.roll(in_msg[s, body : body + 1, :], amount, axis=1), owned)
    own_ids = jnp.maximum(owned, 0.0)
    block_y = jnp.floor((own_ids + 0.5) * (1.0 / block_cols))
    block_x = own_ids - block_y * block_cols
    corner_x = block_x * 16.0 + 0.5
    corner_y = block_y * 8.0 + (me * strip_rows).astype(F32) + 0.5
    got = unpack(in_msg)
    rec[0] = corner_x - got[0]
    rec[1] = corner_y - got[1]
    rec[2] = -0.5 * LOG2E * got[2]
    rec[3] = -LOG2E * got[3]
    rec[4] = -0.5 * LOG2E * got[4]
    rec[5] = jnp.log2(got[5])
    for f in range(6, 9):
        rec[f] = got[f]
    for f in range(2, 6):
        rec[7 + f] = got[f]
    vreg = (8, LANES)
    rows_f = iota(vreg, 0).astype(F32)

    def wide(f, k):
        return jnp.broadcast_to(rec[f, k : k + 1, :], vreg)

    width_c = 4

    def render_some(index, carry):
        trans = [jnp.ones(vreg, F32)] * width_c
        logs = [jnp.zeros(vreg, F32)] * width_c
        run = [None] * width_c
        sums = [[jnp.zeros(vreg, F32)] * width_c for _ in range(COLOURS)]
        base = (index * width_c).astype(F32)
        for k in range(depth):
            delta_y = wide(1, k) + rows_f
            cross = wide(3, k) * delta_y
            square_y = wide(4, k) * delta_y * delta_y + wide(5, k)
            first_x = wide(0, k) + base
            curve = wide(2, k)
            tint = [wide(6 + ch, k) for ch in range(COLOURS)]
            for j in range(width_c):
                delta_x = first_x + float(j)
                alpha = jnp.exp2((curve * delta_x + cross) * delta_x + square_y)
                place = pl.ds(pl.multiple_of((index * width_c + j) * 8, 8), 8)
                alpha_s[k, place, :] = alpha
                trans_s[k, place, :] = trans[j]
                weight = alpha * trans[j]
                for ch in range(COLOURS):
                    sums[ch][j] = sums[ch][j] + weight * tint[ch]
                kept = 1.0 - alpha
                trans[j] = trans[j] * kept
                run[j] = kept if k % 4 == 0 else run[j] * kept
                if k % 4 == 3 or k == depth - 1:
                    logs[j] = logs[j] + jnp.log(run[j])
        for j in range(width_c):
            place = pl.ds(pl.multiple_of((index * width_c + j) * 8, 8), 8)
            for ch in range(COLOURS):
                seg[ch, place, :] = sums[ch][j]
            seg[3, place, :] = trans[j]
            seg[4, place, :] = logs[j]
        return carry

    lax.fori_loop(0, 16 // width_c, render_some, 0)

    diagonal = iota(square, 0) == iota(square, 1)
    ranks_f = ranks.astype(F32)
    owned_c = jnp.sum(jnp.where(diagonal, owned, 0.0), axis=1, keepdims=True)
    ranks_c = jnp.sum(jnp.where(diagonal, ranks_f, 0.0), axis=1, keepdims=True)
    same = owned_c == owned
    fwd_mask = jnp.where(same & (ranks_c < ranks_f), 1.0, 0.0).astype(BF16)
    bwd_mask = jnp.where(same & (ranks_c > ranks_f), 1.0, 0.0).astype(BF16)
    blocks_here = LANES // 2
    lane_sq, sub_sq = iota(square, 1).astype(F32), iota(square, 0).astype(F32)
    for part in range(3):
        nearer[part * LANES : (part + 1) * LANES, :] = fwd_mask
        further[part * LANES : (part + 1) * LANES, :] = bwd_mask
    for d in range(2):
        alive = owned_c >= 0.0
        forth = jnp.where(alive & (lane_sq == owned_c + d * blocks_here), 1.0, 0.0).astype(BF16)
        back = jnp.where((owned >= 0.0) & (sub_sq == owned + d * blocks_here), 1.0, 0.0).astype(BF16)
        for part in range(3):
            place_f[(part * 2 + d) * LANES : (part * 2 + d + 1) * LANES, :] = forth
            place_b[part * LANES : (part + 1) * LANES, d * LANES : (d + 1) * LANES] = back

    before = jnp.dot(
        jnp.concatenate(three_parts(seg[4]), axis=1), nearer[...], preferred_element_type=F32
    )
    seg[4] = jnp.exp(before)
    fetches[6].wait()
    backs = [backdrop_v[:, ch : ch + 1] for ch in range(COLOURS)]
    shares = [[None] * 16 for _ in range(COLOURS)]
    for c in range(16):
        part = slice(c * 8, c * 8 + 8)
        share = seg[4, part, :]
        taken = 1.0 - seg[3, part, :]
        for ch in range(COLOURS):
            tinted = seg[ch, part, :] - backs[ch] * taken
            seg[ch, part, :] = tinted
            shares[ch][c] = share * tinted
    across_lanes = iota(vreg, 1)
    to_natural = (across_lanes & 15) * 8 + lax.shift_right_logical(across_lanes, 4)
    from_natural = (across_lanes & 7) * 16 + lax.shift_right_logical(across_lanes, 3)
    image_copies = []
    for ch in range(COLOURS):
        paired = jnp.concatenate(
            [jnp.concatenate([shares[ch][c], shares[ch][c + 8]], axis=1) for c in range(8)], axis=0
        )
        placed = jnp.dot(
            jnp.concatenate(three_parts(paired), axis=1), place_f[...], preferred_element_type=F32
        )
        for q, value in enumerate(swap_chunks([placed[c * 8 : c * 8 + 8] for c in range(8)], 8)):
            b, g = divmod(q, groups)
            value = jnp.take_along_axis(value, to_natural, axis=1, mode="promise_in_bounds") + backs[ch]
            image[ch, own_rows(b, g), :] = value
            picture_out[0, ch, b * 8 : b * 8 + 8, g * LANES : (g + 1) * LANES] = value
        image_copies.append(exchange(image, ch, image_send, image_recv, 2 * ch))
        begin(image_copies[ch])

    def blur_rows(load, count, store):
        seen = {}

        def line(at):
            if at not in seen:
                seen[at] = load(at)
            return seen[at]

        for at in range(0, count * groups, 8):
            total = taps[5] * line(at + 5 * groups)
            for i in range(5):
                total = total + taps[i] * (line(at + i * groups) + line(at + (10 - i) * groups))
            store(at, total)

    def reader(ref, ch):
        return lambda at: ref[ch, at : at + 8, :]

    def writer(base):
        def store(at, value):
            rows_buf[8 + base + at : 16 + base + at, :] = value

        return store

    sub_group = iota((1, 8, LANES), 1) & (groups - 1)
    low_lanes = iota((1, 8, LANES), 2) < LANES // 2
    from_right = low_lanes & (sub_group < groups - 1)
    from_left = jnp.logical_not(low_lanes) & (sub_group > 0)

    def blur_columns(first, size, terms):
        def read(at):
            return rows_buf[at : at + size, :].reshape(size // 8, 8, LANES)

        sides = jnp.where(from_right, read(first + 9), jnp.where(from_left, read(first + 7), 0.0))
        own_parts = three_parts(rows_buf[first + 8 : first + 8 + size, :])[0:terms]
        rim_parts = three_parts(sides.reshape(size, LANES))[0:terms]
        both = jnp.dot(
            jnp.concatenate([v for pair in zip(own_parts, rim_parts) for v in pair], axis=1),
            taps_w[0 : terms * 2 * LANES, :],
            preferred_element_type=F32,
        )
        return (both[:, 0:LANES] + both[:, LANES : 2 * LANES]) * blur_norm

    def blur_all(total, dst, terms=3):
        half = -(-total // 32) * 16
        dst[0:half, :] = blur_columns(0, half, terms)
        dst[half:total, :] = blur_columns(half, total - half, terms)

    rows_buf[0:8, :] = jnp.zeros_like(rows_buf[0:8, :])
    rows_buf[8 + 6 * mid : 16 + 6 * mid, :] = jnp.zeros_like(rows_buf[0:8, :])
    arrived(goal_copies)
    for ch in range(COLOURS):
        from_goal = reader(goal, ch)
        blur_rows(from_goal, rows_mid, writer(2 * ch * mid))
        blur_rows(lambda at: from_goal(at) * from_goal(at), rows_mid, writer((2 * ch + 1) * mid))
    blur_all(6 * mid, goal_buf)

    own_terms, pulled = None, []
    for ch in range(COLOURS):
        arrived(image_copies[ch])
        from_goal, from_image = reader(goal, ch), reader(image, ch)
        blur_rows(from_image, rows_mid, writer(0))
        blur_rows(lambda at: from_image(at) * from_image(at), rows_mid, writer(mid))
        blur_rows(lambda at: from_image(at) * from_goal(at), rows_mid, writer(2 * mid))
        blur_all(3 * mid, cols_buf)
        mean_a, raw_aa, raw_ab = (cols_buf[q * mid : (q + 1) * mid, :] for q in range(3))
        mean_b, raw_bb = (goal_buf[(2 * ch + q) * mid : (2 * ch + q + 1) * mid, :] for q in range(2))
        centre_rows = slice(HALO * groups, HALO * groups + mid)
        pixel_a, pixel_b = image[ch, centre_rows, :], goal[ch, centre_rows, :]
        seed = seed_s[...]
        square_a, square_b, cross = mean_a * mean_a, mean_b * mean_b, mean_a * mean_b
        first_n = 2.0 * cross + SSIM_FIRST
        second_n = 2.0 * (raw_ab - cross) + SSIM_SECOND
        first_d = square_a + square_b + SSIM_FIRST
        second_d = (raw_aa - square_a) + (raw_bb - square_b) + SSIM_SECOND
        scale = 1.0 / (first_d * second_d)
        ssim = first_n * second_n * scale
        inv_first, inv_second = second_d * scale, first_d * scale
        by_aa = -ssim * inv_second
        by_ab = 2.0 * first_n * scale
        by_a = 2.0 * (mean_b * second_n * scale - mean_a * (ssim * inv_first + by_aa)) - mean_b * by_ab
        adj[0, 0:mid, :] = seed * by_a
        adj[1, 0:mid, :] = seed * by_aa
        adj[2, 0:mid, :] = seed * by_ab
        differ = pixel_a - pixel_b
        term = (0.8 * jnp.sqrt(differ * differ + SMOOTHING) + 0.2 * (1.0 - ssim)) * own_s[...]
        own_terms = term if own_terms is None else own_terms + term
        for q in range(3):
            blur_rows(reader(adj, q), strip_rows, writer(q * end))
        blur_all(3 * end, cols_buf, terms=2)
        own_pixels = slice(MARGIN * groups, MARGIN * groups + end)
        pixel_a, pixel_b = image[ch, own_pixels, :], goal[ch, own_pixels, :]
        differ = pixel_a - pixel_b
        adj[0, 0:end, :] = (
            cols_buf[0:end, :]
            + 2.0 * pixel_a * cols_buf[end : 2 * end, :]
            + pixel_b * cols_buf[2 * end : 3 * end, :]
            + 0.8 * differ * lax.rsqrt(differ * differ + SMOOTHING)
        )
        bands_here = []
        for q in range(bands):
            b, g = divmod(q, groups)
            value = adj[0, pl.ds(b * 8 * groups + g, 8, stride=groups), :]
            bands_here.append(jnp.take_along_axis(value, from_natural, axis=1, mode="promise_in_bounds"))
        pulled.append(
            jnp.dot(
                jnp.concatenate(three_parts(jnp.concatenate(swap_chunks(bands_here, 8), axis=0)), axis=1),
                place_b[...],
                preferred_element_type=F32,
            )
        )
    own_loss = jnp.sum(jnp.sum(own_terms, axis=1, keepdims=True), axis=0, keepdims=True)

    for c in range(16):
        part = slice(c * 8, c * 8 + 8)
        share = seg[4, part, :]
        by_share, by_trans = None, None
        for ch in range(COLOURS):
            grad = pulled[ch][c % 8 * 8 : c % 8 * 8 + 8, c // 8 * LANES : (c // 8 + 1) * LANES]
            piece = grad * seg[ch, part, :]
            by_share = piece if by_share is None else by_share + piece
            grad = grad * share
            seg[ch, part, :] = grad
            piece = grad * backs[ch]
            by_trans = piece if by_trans is None else by_trans + piece
        rows_buf[part, :] = by_share * share
        cols_buf[part, :] = by_trans
    by_log = jnp.dot(
        jnp.concatenate(three_parts(rows_buf[0:LANES, :]), axis=1), further[...], preferred_element_type=F32
    )
    trans = seg[3]
    visible_through = trans > 2e-38
    cols_buf[0:LANES, :] += jnp.where(visible_through, by_log / jnp.where(visible_through, trans, 1.0), 0.0)

    def unrender(step, carry):
        k = depth - 1 - step
        row = pl.ds(k, 1)

        def across(f):
            return jnp.broadcast_to(rec[f, row, :], vreg)

        delta_y = across(1) + rows_f
        first_x = across(0)
        tint = [across(6 + ch) for ch in range(COLOURS)]
        sums = [jnp.zeros(vreg, F32)] * 6
        for c in range(16):
            part = slice(c * 8, c * 8 + 8)
            alpha = alpha_s[k, part, :]
            weight = alpha * trans_s[k, part, :]
            behind = cols_buf[part, :]
            grads = [seg[ch, part, :] for ch in range(COLOURS)]
            gap = grads[0] * tint[0] + grads[1] * tint[1] + grads[2] * tint[2] - behind
            cols_buf[part, :] = behind + alpha * gap
            slope = weight * gap
            delta_x = first_x + float(c)
            slope_x = slope * delta_x
            terms = [slope, slope_x, slope_x * delta_x] + [weight * g for g in grads]
            sums = [a + b for a, b in zip(sums, terms)]
        rows = [
            sums[0], sums[1], sums[0] * delta_y, sums[2], sums[1] * delta_y, sums[0] * delta_y * delta_y,
            sums[3], sums[4], sums[5],
        ]
        for f, value in enumerate(rows):
            moments[f, row, :] = jnp.sum(value, axis=0, keepdims=True)
        return carry

    lax.fori_loop(0, depth, unrender, 0)
    conic_a, conic_b, conic_c, opaque = [rec[9 + i] for i in range(4)]
    grads_out = [
        conic_a * moments[1] + conic_b * moments[2],
        conic_b * moments[1] + conic_c * moments[2],
        -0.5 * moments[3],
        -moments[4],
        -0.5 * moments[5],
        moments[0] / opaque,
        moments[6],
        moments[7],
        moments[8],
    ]
    pack(grads_out, jnp.broadcast_to(own_loss, (1, LANES)), ret_out)
    grads_back = [
        remote(ret_out.at[peer], ret_in.at[0, me], ret_send.at[d], ret_recv.at[d], {"space": peer})
        for d, peer in enumerate(peers)
    ]
    grads_across = [
        remote(
            ret_out.at[peer], ret_in.at[1, me], ret_send.at[devices + d], ret_recv.at[devices + d],
            {"space": peer, "view": across_x},
        )
        for d, peer in enumerate(peers + [me])
    ]
    for copy in grads_across + grads_back:
        copy.start()
    ret_in[0, me] = ret_out[me]

    for copy in cameras:
        copy.wait_recv()
    for v in range(views):
        turned = turn_of(head_view[v, 0:1, :])
        for i, value in enumerate([x for row in turned for x in row] + harmonics(turned[2])):
            table_out[v, i : i + 1, :] = jnp.broadcast_to(value, (1, LANES))

    views_out = []
    for which, (view, waits) in enumerate(((across_x, grads_across), (my_view, grads_back))):
        for copy in waits:
            copy.wait_recv()
        for f, value in enumerate(unpack(ret_in.at[1 - which])):
            fields[f] = value
        for half in range(tall // 8):
            slot_of = inverse[half * 8 : half * 8 + 8, :]
            entry_of = inverse[tall + half * 8 : tall + half * 8 + 8, :]
            for f in range(9):
                value = jnp.zeros(vreg, F32)
                for h in range(depth):
                    row = jnp.broadcast_to(fields[f, h : h + 1, :], vreg)
                    row = jnp.take_along_axis(row, slot_of, axis=1, mode="promise_in_bounds")
                    value = jnp.where(entry_of == h, row, value)
                view_grads[view, f, half * 8 : half * 8 + 8, :] = value
        piece = view_grads.at[view]
        views_out.append(remote(piece, piece, view_send.at[which], view_recv.at[which], {"view": pair}))
        views_out[which].start()
    total_loss = jnp.zeros((1, 1), F32)
    for s in range(devices):
        total_loss = total_loss + ret_in[0, s, body : body + 1, 0:1]
    loss_out[...] = total_loss / (3.0 * height_px * width_px)
    for copy in views_out:
        copy.wait_recv()
    for copy in cameras + records_out + grads_back + grads_across + views_out:
        copy.wait_send()
    left(goal_copies)
    for copies in image_copies:
        left(copies)


def finish_kernel(sizes, params_ref, grads_ref, table_ref, picture_ref, grad_hbm, picture_hbm, flat, grad_v, sems):
    views, splats, centre_x, centre_y = sizes
    param_rows = params_ref.shape[0]
    tall = splats // LANES
    tiles = -(-param_rows // 8)
    writes = [pltpu.make_async_copy(picture_ref, picture_hbm, sems.at[tiles])]
    writes[0].start()

    def write_tile(tile):
        size = min(8, param_rows - 8 * tile)
        for i in range(tall):
            start = (tile * tall + i) * 8
            grad_v[8 * tile : 8 * tile + size, i * LANES : (i + 1) * LANES] = flat[start : start + size, :]
        rows = pl.ds(8 * tile, size)
        writes.append(pltpu.make_async_copy(grad_v.at[rows], grad_hbm.at[rows], sems.at[tile]))
        writes[-1].start()

    for tile in range(-(-param_rows // 8)):
        size = min(8, param_rows - 8 * tile)
        for i in range(tall) if tile < 2 else ():
            start = (tile * tall + i) * 8
            flat[start : start + size, :] = params_ref[8 * tile : 8 * tile + size, i * LANES : (i + 1) * LANES]

    def place(row):
        return pl.ds(row // 8 * tall * 8 + row % 8, tall, stride=8)

    turns = [[[table_ref[v, r * 3 + c : r * 3 + c + 1, :] for c in range(3)] for r in range(3)] for v in range(views)]
    bases = [[table_ref[v, 9 + i : 10 + i, :] for i in range(16)] for v in range(views)]
    rows = [flat[place(i), :] for i in range(11)]
    for c in range(COLOURS):
        by_colour = [grads_ref[v, 6 + c] for v in range(views)]
        for i in range(16):
            value = bases[0][i] * by_colour[0]
            for v in range(1, views):
                value = value + bases[v][i] * by_colour[v]
            flat[place(11 + 3 * i + c), :] = value
    for tile in range(2, tiles):
        write_tile(tile)
    pull = jax.vjp(lambda r: geometry(r, turns, centre_x, centre_y), rows)[1]
    for i, value in enumerate(pull([[grads_ref[v, f] for f in range(6)] for v in range(views)])[0]):
        flat[place(i), :] = value
    for tile in range(2):
        write_tile(tile)
    for copy in writes:
        copy.wait()


def shards(params, visible, blocks, counts, depth_rank, camera, background, target):
    devices, views = lax.axis_size("space"), lax.axis_size("view")
    slots, depth = visible.shape[1:]
    capacity = slots // devices
    strip_rows, width_px = target.shape[2:]
    splats = params.shape[1]
    tall = splats // LANES
    groups = width_px // LANES
    rows_in, rows_mid = strip_rows + 4 * HALO, strip_rows + 2 * HALO
    sizes = (devices, views, depth, slots, capacity, strip_rows, width_px, splats)
    per_tile = LANES // capacity
    dense = devices == 8 and per_tile == 8 and depth == 16
    message = (depth + 2 if dense else depth * -(-9 // per_tile)) + 1
    vmem = lambda *shape: pltpu.VMEM(shape, F32)
    half = lambda *shape: pltpu.VMEM(shape, BF16)
    dma = lambda count: pltpu.SemaphoreType.DMA((count,))
    scratch = [
        vmem(*params.shape), pltpu.VMEM((depth, slots), I32), pltpu.VMEM(blocks.shape, I32),
        pltpu.VMEM(counts.shape, I32), pltpu.VMEM(depth_rank.shape, I32), vmem(*camera.shape),
        vmem(*background.shape), vmem(*target.shape[1:]),
        vmem(-(-params.shape[0] // 8) * tall * 8, LANES), vmem(9, tall, LANES), pltpu.VMEM((2, depth, LANES), I32),
        vmem(8, LANES), vmem(views, 8, LANES),
        vmem(devices, message, LANES), vmem(devices, message, LANES),
        vmem(devices, message, LANES), vmem(2, devices, message, LANES),
        vmem(13, depth, LANES), half(6 * LANES, LANES), half(3 * LANES, 2 * LANES),
        half(3 * LANES, LANES), half(3 * LANES, LANES),
        half(6 * LANES, 2 * LANES), pltpu.VMEM((2 * tall, LANES), I32),
        vmem(depth, LANES, LANES), vmem(depth, LANES, LANES), vmem(5, LANES, LANES),
        vmem(COLOURS, rows_in * groups, LANES), vmem(COLOURS, rows_in * groups, LANES),
        vmem(6 * rows_mid * groups + 16, LANES), vmem(6 * rows_mid * groups, LANES), vmem(3 * rows_mid * groups, LANES),
        vmem(3, rows_mid * groups, LANES), vmem(rows_mid * groups, LANES), vmem(rows_mid * groups, LANES),
        vmem(9, depth, LANES),
        dma(8), dma(views), dma(views), dma(devices), dma(devices), dma(2 * devices),
        dma(2 * devices), dma(2), dma(2), dma(6), dma(6), dma(2), dma(2),
    ]
    whole = pl.BlockSpec(memory_space=pltpu.VMEM)
    grads, table, picture, loss = pl.pallas_call(
        functools.partial(step_kernel, sizes),
        name="step",
        out_shape=(
            jax.ShapeDtypeStruct((views, 9, tall, LANES), F32),
            jax.ShapeDtypeStruct((views, TABLE, LANES), F32),
            jax.ShapeDtypeStruct(target.shape, F32),
            jax.ShapeDtypeStruct((1, 1), F32),
        ),
        in_specs=[pl.BlockSpec(memory_space=pltpu.HBM)] * 8,
        out_specs=(whole,) * 4,
        scratch_shapes=scratch,
        compiler_params=pltpu.CompilerParams(
            collective_id=0, has_side_effects=True, vmem_limit_bytes=20 * 1024 * 1024
        ),
    )(*[pltpu.with_memory_space_constraint(x, pltpu.HBM) for x in (params, jnp.swapaxes(visible, 1, 2), blocks, counts, depth_rank, camera, background, target)])
    centre = (0.5 * width_px, 0.5 * strip_rows * devices)
    grad, picture = pl.pallas_call(
        functools.partial(finish_kernel, (views, splats, *centre)),
        name="finish",
        out_shape=(jax.ShapeDtypeStruct(params.shape, F32), jax.ShapeDtypeStruct(target.shape, F32)),
        in_specs=[whole] * 4,
        out_specs=(pl.BlockSpec(memory_space=pl.ANY),) * 2,
        scratch_shapes=[
            vmem(-(-params.shape[0] // 8) * tall * 8, LANES), vmem(*params.shape), dma(-(-params.shape[0] // 8) + 1)
        ],
        compiler_params=pltpu.CompilerParams(vmem_limit_bytes=20 * 1024 * 1024),
    )(params, grads, table, picture)
    return (grad, picture, loss.reshape(1))


def solution(mesh):
    in_specs = (
        P(None, "space"),
        P("space", None, None),
        P("space", None),
        P("space", None),
        P("view", None),
        P("view", None),
        P("view", None),
        P("view", None, "space", None),
    )
    out_specs = (P(None, "space"), P("view", None, "space", None), P("view"))
    return jax.shard_map(shards, mesh=mesh, in_specs=in_specs, out_specs=out_specs, check_vma=False)
```

```python
import functools
import math

import jax
import jax.numpy as jnp
import numpy as np
from jax import lax
from jax.experimental import pallas as pl
from jax.experimental.pallas import tpu as pltpu
from jax.sharding import PartitionSpec as P

F32 = jnp.float32
BF16 = jnp.bfloat16
I32 = jnp.int32
LANES = 128
LOG2E = 1.4426950408889634
SH_ZERO = 0.28209479177387814
SH_ONE = 0.4886025119029199
SH_TWO = (
    1.0925484305920792,
    -1.0925484305920792,
    0.31539156525252005,
    -1.0925484305920792,
    0.5462742152960396,
)
SH_THREE = (
    -0.5900435899266435,
    2.890611442640554,
    -0.4570457994644658,
    0.3731763325901154,
    -0.4570457994644658,
    1.445305721320277,
    -0.5900435899266435,
)
DILATION = 0.3
SMOOTHING = 0.0001
SSIM_FIRST = 0.0001
SSIM_SECOND = 0.0009


def camera_rotation(angles):
    cos_a, sin_a = (jnp.cos(angles[0]), jnp.sin(angles[0]))
    cos_b, sin_b = (jnp.cos(angles[1]), jnp.sin(angles[1]))
    cos_c, sin_c = (jnp.cos(angles[2]), jnp.sin(angles[2]))
    return [
        [cos_c * cos_b, cos_c * sin_b * sin_a - sin_c * cos_a, cos_c * sin_b * cos_a + sin_c * sin_a],
        [sin_c * cos_b, sin_c * sin_b * sin_a + cos_c * cos_a, sin_c * sin_b * cos_a - cos_c * sin_a],
        [-sin_b, cos_b * sin_a, cos_b * cos_a],
    ]


def harmonics(view_axis):
    axis_x, axis_y, axis_z = (view_axis[0], view_axis[1], view_axis[2])
    sq_x, sq_y, sq_z = (axis_x * axis_x, axis_y * axis_y, axis_z * axis_z)
    return [
        SH_ZERO * jnp.ones_like(axis_x),
        -SH_ONE * axis_y,
        SH_ONE * axis_z,
        -SH_ONE * axis_x,
        SH_TWO[0] * axis_x * axis_y,
        SH_TWO[1] * axis_y * axis_z,
        SH_TWO[2] * (2.0 * sq_z - sq_x - sq_y),
        SH_TWO[3] * axis_x * axis_z,
        SH_TWO[4] * (sq_x - sq_y),
        SH_THREE[0] * axis_y * (3.0 * sq_x - sq_y),
        SH_THREE[1] * axis_x * axis_y * axis_z,
        SH_THREE[2] * axis_y * (4.0 * sq_z - sq_x - sq_y),
        SH_THREE[3] * axis_z * (2.0 * sq_z - 3.0 * sq_x - 3.0 * sq_y),
        SH_THREE[4] * axis_x * (4.0 * sq_z - sq_x - sq_y),
        SH_THREE[5] * axis_z * (sq_x - sq_y),
        SH_THREE[6] * axis_x * (sq_x - 3.0 * sq_y),
    ]


def geometry(rows, turns, centre_x, centre_y):
    scales = [jnp.exp(rows[i]) for i in range(3, 6)]
    quat = rows[6:10]
    length = jnp.sqrt(quat[0] * quat[0] + quat[1] * quat[1] + quat[2] * quat[2] + quat[3] * quat[3])
    part_w, part_x, part_y, part_z = [q / length for q in quat]
    spin = [
        [
            1.0 - 2.0 * (part_y * part_y + part_z * part_z),
            2.0 * (part_x * part_y - part_w * part_z),
            2.0 * (part_x * part_z + part_w * part_y),
        ],
        [
            2.0 * (part_x * part_y + part_w * part_z),
            1.0 - 2.0 * (part_x * part_x + part_z * part_z),
            2.0 * (part_y * part_z - part_w * part_x),
        ],
        [
            2.0 * (part_x * part_z - part_w * part_y),
            2.0 * (part_y * part_z + part_w * part_x),
            1.0 - 2.0 * (part_x * part_x + part_y * part_y),
        ],
    ]
    local = [[spin[r][c] * scales[c] for c in range(3)] for r in range(3)]
    opacity = 1.0 / (1.0 + jnp.exp(-rows[10]))
    shift_x = rows[0] - centre_x
    shift_y = rows[1] - centre_y
    records = []
    for turn in turns:
        frame = [
            [
                turn[r][0] * local[0][c] + turn[r][1] * local[1][c] + turn[r][2] * local[2][c]
                for c in range(3)
            ]
            for r in range(2)
        ]
        cov_xx = sum(frame[0][c] * frame[0][c] for c in range(3)) + DILATION
        cov_xy = sum(frame[0][c] * frame[1][c] for c in range(3))
        cov_yy = sum(frame[1][c] * frame[1][c] for c in range(3)) + DILATION
        inverse = 1.0 / (cov_xx * cov_yy - cov_xy * cov_xy)
        mean_u = turn[0][0] * shift_x + turn[0][1] * shift_y + turn[0][2] * rows[2] + centre_x
        mean_w = turn[1][0] * shift_x + turn[1][1] * shift_y + turn[1][2] * rows[2] + centre_y
        records.append(
            [mean_u, mean_w, cov_yy * inverse, -cov_xy * inverse, cov_xx * inverse, opacity]
        )
    return records


def blur_taps():
    raw_taps = [math.exp(-(offset - 5) * (offset - 5) / 4.5) for offset in range(11)]
    total = sum(raw_taps)
    return [value / total for value in raw_taps]


NT = (((1,), (1,)), ((), ()))
COLOURS = 3
HALO = 5
MARGIN = 2 * HALO
TABLE = 32


def three_parts(value):
    high = value.astype(BF16)
    rest = value - high.astype(F32)
    middle = rest.astype(BF16)
    low = (rest - middle.astype(F32)).astype(BF16)
    return [high, middle, low]


def iota(shape, axis):
    return lax.broadcasted_iota(I32, shape, axis)


def swap_chunks(values, width):
    lane = iota((1, LANES), 1)
    for bit in range(3):
        step = 1 << bit
        low = (lane & (width * step)) == 0
        moved = list(values)
        for a in range(8):
            if not a & step:
                first, second = values[a], values[a | step]
                moved[a] = jnp.where(low, first, pltpu.roll(second, width * step, axis=1))
                moved[a | step] = jnp.where(low, pltpu.roll(first, LANES - width * step, axis=1), second)
        values = moved
    return values


def swap_sublanes(value, width):
    lane, row = iota((8, LANES), 1), iota((8, LANES), 0)
    for bit in range(3):
        step = 1 << bit
        low_lane, low_row = (lane & (width * step)) == 0, (row & step) == 0
        up = pltpu.roll(pltpu.roll(value, 8 - step, axis=0), width * step, axis=1)
        down = pltpu.roll(pltpu.roll(value, step, axis=0), LANES - width * step, axis=1)
        value = jnp.where(low_lane == low_row, value, jnp.where(low_row, up, down))
    return value


def step_kernel(
    sizes,
    params_hbm, visible_hbm, blocks_hbm, counts_hbm, rank_hbm, camera_hbm, backdrop_hbm, target_hbm,
    view_grads, table_out, picture_out, loss_out,
    params_v, visible_v, blocks_v, counts_v, rank_v, camera_v, backdrop_v, target_v,
    flat, fields, lists, head, head_view, out_msg, in_msg, ret_out, ret_in,
    rec, place_f, place_b, nearer, further, taps_w, inverse, alpha_s, trans_s, seg, goal, image,
    rows_buf, goal_buf, cols_buf, adj, seed_s, own_s, behind_s, spread,
    in_sem, camv_send, camv_recv, msg_send, msg_recv, ret_send, ret_recv,
    goal_send, goal_recv, image_send, image_recv, view_send, view_recv,
):
    devices, views, depth, slots, capacity, strip_rows, width_px, splats = sizes
    me = lax.axis_index("space")
    my_view = lax.axis_index("view")
    param_rows = params_v.shape[0]
    tall = splats // LANES
    block_cols = width_px // 16
    block_rows = strip_rows // 8
    groups = width_px // LANES
    bands = block_rows * groups
    rows_in = strip_rows + 4 * HALO
    rows_mid = strip_rows + 2 * HALO
    centre_x = 0.5 * width_px
    centre_y = 0.5 * strip_rows * devices
    shift = capacity.bit_length() - 1
    taps = blur_taps()
    peers = [me ^ d for d in range(devices - 1, 0, -1)]
    partners = [my_view ^ d for d in range(1, views)]
    pair, across_x = my_view ^ 1, my_view ^ 2

    barrier = pltpu.get_barrier_semaphore()
    greeted = [{"space": peer, "view": view} for peer in peers for view in (my_view, across_x)]
    greeted += [{"space": me, "view": view} for view in partners]
    for target in greeted:
        pl.semaphore_signal(barrier, inc=1, device_id=target, device_id_type=pl.DeviceIdType.MESH)
    pairs = [
        (blocks_hbm, blocks_v), (counts_hbm, counts_v), (camera_hbm, camera_v), (params_hbm, params_v),
        (visible_hbm.at[0], visible_v), (rank_hbm, rank_v), (backdrop_hbm, backdrop_v), (target_hbm.at[0], target_v),
    ]
    fetches = [pltpu.make_async_copy(a, b, in_sem.at[i]) for i, (a, b) in enumerate(pairs)]
    for fetch in fetches:
        fetch.start()

    rim = MARGIN * groups

    @pl.when(me == 0)
    def _():
        goal[:, 0:rim, :] = jnp.zeros((COLOURS, rim, LANES), F32)
        image[:, 0:rim, :] = jnp.zeros((COLOURS, rim, LANES), F32)

    @pl.when(me == devices - 1)
    def _():
        low = (MARGIN + strip_rows) * groups
        goal[:, low : low + rim, :] = jnp.zeros((COLOURS, rim, LANES), F32)
        image[:, low : low + rim, :] = jnp.zeros((COLOURS, rim, LANES), F32)

    lane = iota((1, LANES), 1)
    chunk = lax.shift_right_logical(lane, shift)
    for fetch in fetches[0:3]:
        fetch.wait()
    counted = jnp.zeros((1, LANES), I32)
    for o in range(devices):
        counted = jnp.where(chunk == o, counts_v[:, o : o + 1], counted)
    live = (lane & (capacity - 1)) < counted
    ids_row = jnp.where(live, blocks_v[...], -1).astype(F32)
    head[...] = jnp.zeros_like(head)
    head[0:1, 0:3] = camera_v[...]
    head_view[my_view] = head[...]

    def remote(src, dst, send, recv, target):
        return pltpu.make_async_remote_copy(
            src_ref=src, dst_ref=dst, send_sem=send, recv_sem=recv, device_id=target,
            device_id_type=pl.DeviceIdType.MESH,
        )

    fetches[3].wait()
    for tile in range(-(-param_rows // 8)):
        size = min(8, param_rows - 8 * tile)
        for i in range(tall):
            start = (tile * tall + i) * 8
            flat[start : start + size, :] = params_v[8 * tile : 8 * tile + size, i * LANES : (i + 1) * LANES]

    def param_row(row):
        return flat[pl.ds(row // 8 * tall * 8 + row % 8, tall, stride=8), :]

    def turn_of(angles):
        return camera_rotation([angles[:, i : i + 1] for i in range(3)])

    turn = turn_of(camera_v[...])
    record = geometry([param_row(i) for i in range(11)], [turn], centre_x, centre_y)[0]
    basis = harmonics(turn[2])
    for c in range(COLOURS):
        colour = 0.5 + basis[0] * param_row(11 + c)
        for i in range(1, 16):
            colour = colour + basis[i] * param_row(11 + 3 * i + c)
        record.append(colour)
    for f in range(9):
        fields[f] = record[f]
    fetches[4].wait()
    listed = visible_v[...]
    lists[0] = lax.shift_right_logical(listed, 7)
    lists[1] = listed & (LANES - 1)
    picked = [[] for _ in range(9)]
    for half in range(depth // 8):
        high = lists[0, half * 8 : half * 8 + 8, :]
        low = lists[1, half * 8 : half * 8 + 8, :]
        for f in range(9):
            value = jnp.zeros((8, LANES), F32)
            for h in range(tall):
                row = jnp.broadcast_to(fields[f, h : h + 1, :], (8, LANES))
                row = jnp.take_along_axis(row, low, axis=1, mode="promise_in_bounds")
                value = jnp.where(high == h, row, value)
            picked[f].append(value)
    picked = [jnp.concatenate(p, axis=0) for p in picked]

    per_tile = LANES // capacity
    dense = devices == 8 and per_tile == 8 and depth == 16
    body = depth + 2 if dense else depth * -(-9 // per_tile)

    def pack(values, extra, dst):
        if dense:
            for o, block in enumerate(swap_chunks(values[0:8], capacity)):
                dst[o, 0:depth, :] = block
            for half in range(2):
                last = swap_sublanes(values[8][half * 8 : half * 8 + 8], capacity)
                for o in range(devices):
                    dst[o, depth + half : depth + half + 1, :] = last[o : o + 1]
        for o in range(devices):
            dst[o, body : body + 1, :] = extra
            for t in range(0 if dense else -(-len(values) // per_tile)):
                block = None
                for j, value in enumerate(values[t * per_tile : (t + 1) * per_tile]):
                    moved = pltpu.roll(value, (j - o) * capacity % LANES, axis=1)
                    block = moved if block is None else jnp.where(chunk == j, moved, block)
                dst[o, t * depth : (t + 1) * depth, :] = block

    def unpack(src):
        if dense:
            values = swap_chunks([src[o, 0:depth, :] for o in range(devices)], capacity)
            last = [
                jnp.concatenate([src[o, depth + half : depth + half + 1, :] for o in range(devices)], axis=0)
                for half in range(2)
            ]
            return values + [jnp.concatenate([swap_sublanes(v, capacity) for v in last], axis=0)]
        values = []
        for f in range(9):
            t, j = divmod(f, per_tile)
            value = None
            for s in range(devices):
                moved = pltpu.roll(src[s, t * depth : (t + 1) * depth, :], (s - j) * capacity % LANES, axis=1)
                value = moved if value is None else jnp.where(chunk == s, moved, value)
            values.append(value)
        return values

    pack(picked, ids_row, out_msg)
    pl.semaphore_wait(barrier, len(greeted))
    records_out = [
        remote(out_msg.at[peer], in_msg.at[me], msg_send.at[d], msg_recv.at[d], {"space": peer})
        for d, peer in enumerate(peers)
    ]
    for copy in records_out:
        copy.start()
    cameras = [
        remote(head, head_view.at[my_view], camv_send.at[d], camv_recv.at[d], {"view": peer})
        for d, peer in enumerate(partners)
    ]
    for copy in cameras:
        copy.start()
    in_msg[me] = out_msg[me]

    def own_rows(b, g):
        return pl.ds((MARGIN + b * 8) * groups + g, 8, stride=groups)

    fetches[7].wait()
    for ch in range(COLOURS):
        for b in range(block_rows):
            for g in range(groups):
                goal[ch, own_rows(b, g), :] = target_v[ch, b * 8 : b * 8 + 8, g * LANES : (g + 1) * LANES]

    top, bottom, below = MARGIN * groups, strip_rows * groups, (MARGIN + strip_rows) * groups

    def exchange(ref, channels, send, recv, at):
        upward = remote(
            ref.at[channels, pl.ds(top, rim)], ref.at[channels, pl.ds(below, rim)],
            send.at[at], recv.at[at], {"space": lax.rem(me + devices - 1, devices)},
        )
        downward = remote(
            ref.at[channels, pl.ds(bottom, rim)], ref.at[channels, pl.ds(0, rim)],
            send.at[at + 1], recv.at[at + 1], {"space": lax.rem(me + 1, devices)},
        )
        return upward, downward

    not_first, not_last = me > 0, me < devices - 1

    def begin(copies):
        pl.when(not_first)(copies[0].start)
        pl.when(not_last)(copies[1].start)

    def arrived(copies):
        pl.when(not_last)(copies[0].wait_recv)
        pl.when(not_first)(copies[1].wait_recv)

    def left(copies):
        pl.when(not_first)(copies[0].wait_send)
        pl.when(not_last)(copies[1].wait_send)

    goal_copies = exchange(goal, slice(None), goal_send, goal_recv, 0)
    begin(goal_copies)

    square = (LANES, LANES)
    fetches[5].wait()
    ranks = jnp.zeros((1, LANES), I32)
    for s in range(devices):
        ranks = jnp.where(chunk == s, rank_v[:, s : s + 1], ranks)
    offset = iota(square, 1) - iota(square, 0)
    near = iota(square, 0) < LANES // 2
    beside = jnp.where(near, offset - LANES, offset + LANES)
    exact = [np.float32(tap) for tap in taps]
    highs = [float(tap.astype(jnp.bfloat16)) for tap in exact]
    lows = [float((tap - np.float32(high)).astype(jnp.bfloat16)) for tap, high in zip(exact, highs)]
    blur_norm = float(1.0 / (sum(highs) + sum(lows)))
    for side, values in enumerate((highs, lows)):
        for part, distance in enumerate((offset, beside)):
            weights = jnp.zeros(square, F32)
            for i in range(11):
                weights = jnp.where(distance == i - HALO, values[i], weights)
            weights = weights.astype(BF16)
            for term in range(3):
                start = (term * 2 + part) * LANES
                taps_w[start : start + LANES, side * LANES : (side + 1) * LANES] = weights

    slot_value = lane.astype(F32)

    def invert(k, total):
        high = lists[0, pl.ds(k, 1), :]
        low = lists[1, pl.ds(k, 1), :]
        hit = iota((tall, LANES), 0) == high
        left = jnp.concatenate(
            [jnp.where(hit, slot_value, 0.0), jnp.where(hit, k.astype(F32), 0.0)], axis=0
        ).astype(BF16)
        right = jnp.where(iota(square, 0) == low, 1.0, 0.0).astype(BF16)
        return total + lax.dot_general(left, right, NT, preferred_element_type=F32)

    inverse[...] = lax.fori_loop(0, depth, invert, jnp.zeros((2 * tall, LANES), F32)).astype(I32)

    height_px = strip_rows * devices
    mid, end = rows_mid * groups, strip_rows * groups
    for at in range(0, mid, 8):
        line = iota((8, LANES), 0) + at
        row_y = (line.astype(F32) + 0.5) * (1.0 / groups)
        y = row_y + (me * strip_rows - HALO).astype(F32)
        counts_here = (y > 0.0) & (y < float(height_px))
        seed_s[at : at + 8, :] = jnp.where(counts_here, -0.2, 0.0)
        own_s[at : at + 8, :] = jnp.where((row_y > HALO) & (row_y < HALO + strip_rows), 1.0, 0.0)

    for copy in records_out:
        copy.wait_recv()
    owned = jnp.zeros((1, LANES), F32)
    for s in range(devices):
        amount = lax.rem(s - me + devices, devices) * capacity
        owned = jnp.where(chunk == s, pltpu.roll(in_msg[s, body : body + 1, :], amount, axis=1), owned)
    own_ids = jnp.maximum(owned, 0.0)
    block_y = jnp.floor((own_ids + 0.5) * (1.0 / block_cols))
    block_x = own_ids - block_y * block_cols
    corner_x = block_x * 16.0 + 0.5
    corner_y = block_y * 8.0 + (me * strip_rows).astype(F32) + 0.5
    got = unpack(in_msg)
    rec[0] = corner_x - got[0]
    rec[1] = corner_y - got[1]
    rec[2] = -0.5 * LOG2E * got[2]
    rec[3] = -LOG2E * got[3]
    rec[4] = -0.5 * LOG2E * got[4]
    rec[5] = jnp.log2(got[5])
    for f in range(6, 9):
        rec[f] = got[f]
    for f in range(2, 6):
        rec[7 + f] = got[f]
    vreg = (8, LANES)
    rows_f = iota(vreg, 0).astype(F32)

    def wide(f, k):
        return jnp.broadcast_to(rec[f, k : k + 1, :], vreg)

    width_c = 4

    def render_some(index, carry):
        trans = [jnp.ones(vreg, F32)] * width_c
        logs = [jnp.zeros(vreg, F32)] * width_c
        run = [None] * width_c
        sums = [[jnp.zeros(vreg, F32)] * width_c for _ in range(COLOURS)]
        base = (index * width_c).astype(F32)
        for k in range(depth):
            delta_y = wide(1, k) + rows_f
            cross = wide(3, k) * delta_y
            square_y = wide(4, k) * delta_y * delta_y + wide(5, k)
            first_x = wide(0, k) + base
            curve = wide(2, k)
            tint = [wide(6 + ch, k) for ch in range(COLOURS)]
            for j in range(width_c):
                delta_x = first_x + float(j)
                alpha = jnp.exp2((curve * delta_x + cross) * delta_x + square_y)
                place = pl.ds(pl.multiple_of((index * width_c + j) * 8, 8), 8)
                alpha_s[k, place, :] = alpha
                trans_s[k, place, :] = trans[j]
                weight = alpha * trans[j]
                for ch in range(COLOURS):
                    sums[ch][j] = sums[ch][j] + weight * tint[ch]
                kept = 1.0 - alpha
                trans[j] = trans[j] * kept
                run[j] = kept if k % 4 == 0 else run[j] * kept
                if k % 4 == 3 or k == depth - 1:
                    logs[j] = logs[j] + jnp.log(run[j])
        for j in range(width_c):
            place = pl.ds(pl.multiple_of((index * width_c + j) * 8, 8), 8)
            for ch in range(COLOURS):
                seg[ch, place, :] = sums[ch][j]
            seg[3, place, :] = trans[j]
            seg[4, place, :] = logs[j]
        return carry

    lax.fori_loop(0, 16 // width_c, render_some, 0)

    diagonal = iota(square, 0) == iota(square, 1)
    ranks_f = ranks.astype(F32)
    owned_c = jnp.sum(jnp.where(diagonal, owned, 0.0), axis=1, keepdims=True)
    ranks_c = jnp.sum(jnp.where(diagonal, ranks_f, 0.0), axis=1, keepdims=True)
    same = owned_c == owned
    fwd_mask = jnp.where(same & (ranks_c < ranks_f), 1.0, 0.0).astype(BF16)
    bwd_mask = jnp.where(same & (ranks_c > ranks_f), 1.0, 0.0).astype(BF16)
    blocks_here = LANES // 2
    lane_sq, sub_sq = iota(square, 1).astype(F32), iota(square, 0).astype(F32)
    for part in range(3):
        nearer[part * LANES : (part + 1) * LANES, :] = fwd_mask
        further[part * LANES : (part + 1) * LANES, :] = bwd_mask
    for d in range(2):
        alive = owned_c >= 0.0
        forth = jnp.where(alive & (lane_sq == owned_c + d * blocks_here), 1.0, 0.0).astype(BF16)
        back = jnp.where((owned >= 0.0) & (sub_sq == owned + d * blocks_here), 1.0, 0.0).astype(BF16)
        for part in range(3):
            place_f[(part * 2 + d) * LANES : (part * 2 + d + 1) * LANES, :] = forth
            place_b[part * LANES : (part + 1) * LANES, d * LANES : (d + 1) * LANES] = back

    before = jnp.dot(
        jnp.concatenate(three_parts(seg[4]), axis=1), nearer[...], preferred_element_type=F32
    )
    seg[4] = jnp.exp(before)
    fetches[6].wait()
    backs = [backdrop_v[:, ch : ch + 1] for ch in range(COLOURS)]
    shares = [[None] * 16 for _ in range(COLOURS)]
    for c in range(16):
        part = slice(c * 8, c * 8 + 8)
        share = seg[4, part, :]
        taken = 1.0 - seg[3, part, :]
        for ch in range(COLOURS):
            tinted = seg[ch, part, :] - backs[ch] * taken
            seg[ch, part, :] = tinted
            shares[ch][c] = share * tinted
    across_lanes = iota(vreg, 1)
    to_natural = (across_lanes & 15) * 8 + lax.shift_right_logical(across_lanes, 4)
    from_natural = (across_lanes & 7) * 16 + lax.shift_right_logical(across_lanes, 3)
    image_copies, placed = [], []
    for ch in range(COLOURS):
        paired = jnp.concatenate(
            [jnp.concatenate([shares[ch][c], shares[ch][c + 8]], axis=1) for c in range(8)], axis=0
        )
        placed.append(
            jnp.dot(jnp.concatenate(three_parts(paired), axis=1), place_f[...], preferred_element_type=F32)
        )
    for ch in range(COLOURS):
        for q, value in enumerate(swap_chunks([placed[ch][c * 8 : c * 8 + 8] for c in range(8)], 8)):
            b, g = divmod(q, groups)
            value = jnp.take_along_axis(value, to_natural, axis=1, mode="promise_in_bounds") + backs[ch]
            image[ch, own_rows(b, g), :] = value
            picture_out[0, ch, b * 8 : b * 8 + 8, g * LANES : (g + 1) * LANES] = value
        image_copies.append(exchange(image, ch, image_send, image_recv, 2 * ch))
        begin(image_copies[ch])

    def blur_rows(load, count, store):
        seen = {}

        def line(at):
            if at not in seen:
                seen[at] = load(at)
            return seen[at]

        for at in range(0, count * groups, 8):
            total = taps[5] * line(at + 5 * groups)
            for i in range(5):
                total = total + taps[i] * (line(at + i * groups) + line(at + (10 - i) * groups))
            store(at, total)

    def reader(ref, ch):
        return lambda at: ref[ch, at : at + 8, :]

    def writer(ch, base):
        def store(at, value):
            rows_buf[ch, 8 + base + at : 16 + base + at, :] = value

        return store

    sub_group = iota((1, 8, LANES), 1) & (groups - 1)
    low_lanes = iota((1, 8, LANES), 2) < LANES // 2
    from_right = low_lanes & (sub_group < groups - 1)
    from_left = jnp.logical_not(low_lanes) & (sub_group > 0)

    def blur_columns(ch, first, size, terms):
        def read(at):
            return rows_buf[ch, at : at + size, :].reshape(size // 8, 8, LANES)

        sides = jnp.where(from_right, read(first + 9), jnp.where(from_left, read(first + 7), 0.0))
        own_parts = three_parts(rows_buf[ch, first + 8 : first + 8 + size, :])[0:terms]
        rim_parts = three_parts(sides.reshape(size, LANES))[0:terms]
        both = jnp.dot(
            jnp.concatenate([v for pair in zip(own_parts, rim_parts) for v in pair], axis=1),
            taps_w[0 : terms * 2 * LANES, :],
            preferred_element_type=F32,
        )
        return (both[:, 0:LANES] + both[:, LANES : 2 * LANES]) * blur_norm

    def blur_all(ch, total, dst, terms=3):
        half = -(-total // 32) * 16
        dst[ch, 0:half, :] = blur_columns(ch, 0, half, terms)
        dst[ch, half:total, :] = blur_columns(ch, half, total - half, terms)

    for ch in range(COLOURS):
        rows_buf[ch, 0:8, :] = jnp.zeros((8, LANES), F32)
        rows_buf[ch, 8 + 3 * mid : 16 + 3 * mid, :] = jnp.zeros((8, LANES), F32)
    arrived(goal_copies)
    for ch in range(COLOURS):
        from_goal = reader(goal, ch)
        blur_rows(from_goal, rows_mid, writer(ch, 0))
        blur_rows(lambda at: from_goal(at) * from_goal(at), rows_mid, writer(ch, mid))
        blur_all(ch, 2 * mid, goal_buf)

    def blur_picture(ch):
        from_goal, from_image = reader(goal, ch), reader(image, ch)
        blur_rows(from_image, rows_mid, writer(ch, 0))
        blur_rows(lambda at: from_image(at) * from_image(at), rows_mid, writer(ch, mid))
        blur_rows(lambda at: from_image(at) * from_goal(at), rows_mid, writer(ch, 2 * mid))
        blur_all(ch, 3 * mid, cols_buf)

    def terms_of(ch):
        mean_a, raw_aa, raw_ab = (cols_buf[ch, q * mid : (q + 1) * mid, :] for q in range(3))
        mean_b, raw_bb = (goal_buf[ch, q * mid : (q + 1) * mid, :] for q in range(2))
        centre_rows = slice(HALO * groups, HALO * groups + mid)
        pixel_a, pixel_b = image[ch, centre_rows, :], goal[ch, centre_rows, :]
        seed = seed_s[...]
        square_a, square_b, cross = mean_a * mean_a, mean_b * mean_b, mean_a * mean_b
        first_n = 2.0 * cross + SSIM_FIRST
        second_n = 2.0 * (raw_ab - cross) + SSIM_SECOND
        first_d = square_a + square_b + SSIM_FIRST
        second_d = (raw_aa - square_a) + (raw_bb - square_b) + SSIM_SECOND
        scale = 1.0 / (first_d * second_d)
        ssim = first_n * second_n * scale
        inv_first, inv_second = second_d * scale, first_d * scale
        by_aa = -ssim * inv_second
        by_ab = 2.0 * first_n * scale
        by_a = 2.0 * (mean_b * second_n * scale - mean_a * (ssim * inv_first + by_aa)) - mean_b * by_ab
        adj[3 * ch, 0:mid, :] = seed * by_a
        adj[3 * ch + 1, 0:mid, :] = seed * by_aa
        adj[3 * ch + 2, 0:mid, :] = seed * by_ab
        differ = pixel_a - pixel_b
        for q in range(3):
            blur_rows(reader(adj, 3 * ch + q), strip_rows, writer(ch, q * end))
        blur_all(ch, 3 * end, cols_buf, terms=2)
        return (0.8 * jnp.sqrt(differ * differ + SMOOTHING) + 0.2 * (1.0 - ssim)) * own_s[...]

    def to_slots(ch):
        own_pixels = slice(MARGIN * groups, MARGIN * groups + end)
        pixel_a, pixel_b = image[ch, own_pixels, :], goal[ch, own_pixels, :]
        differ = pixel_a - pixel_b
        adj[3 * ch, 0:end, :] = (
            cols_buf[ch, 0:end, :]
            + 2.0 * pixel_a * cols_buf[ch, end : 2 * end, :]
            + pixel_b * cols_buf[ch, 2 * end : 3 * end, :]
            + 0.8 * differ * lax.rsqrt(differ * differ + SMOOTHING)
        )
        bands_here = []
        for q in range(bands):
            b, g = divmod(q, groups)
            value = adj[3 * ch, pl.ds(b * 8 * groups + g, 8, stride=groups), :]
            bands_here.append(jnp.take_along_axis(value, from_natural, axis=1, mode="promise_in_bounds"))
        stacked = jnp.concatenate(swap_chunks(bands_here, 8), axis=0)
        return jnp.dot(
            jnp.concatenate(three_parts(stacked)[0:2], axis=1), place_b[0 : 2 * LANES, :], preferred_element_type=F32
        )

    arrived(image_copies[0])
    blur_picture(0)
    arrived(image_copies[1])
    blur_picture(1)
    own_terms = terms_of(0)
    arrived(image_copies[2])
    blur_picture(2)
    own_terms = own_terms + terms_of(1)
    pulled = [to_slots(0)]
    own_terms = own_terms + terms_of(2)
    pulled += [to_slots(1), to_slots(2)]
    own_loss = jnp.sum(jnp.sum(own_terms, axis=1, keepdims=True), axis=0, keepdims=True)

    for c in range(16):
        part = slice(c * 8, c * 8 + 8)
        share = seg[4, part, :]
        by_share, by_trans = None, None
        for ch in range(COLOURS):
            grad = pulled[ch][c % 8 * 8 : c % 8 * 8 + 8, c // 8 * LANES : (c // 8 + 1) * LANES]
            piece = grad * seg[ch, part, :]
            by_share = piece if by_share is None else by_share + piece
            grad = grad * share
            seg[ch, part, :] = grad
            piece = grad * backs[ch]
            by_trans = piece if by_trans is None else by_trans + piece
        rows_buf[0, part, :] = by_share * share
        behind_s[part, :] = by_trans
    by_log = jnp.dot(
        jnp.concatenate(three_parts(rows_buf[0, 0:LANES, :]), axis=1), further[...], preferred_element_type=F32
    )
    trans = seg[3]
    visible_through = trans > 2e-38
    behind_s[...] += jnp.where(visible_through, by_log / jnp.where(visible_through, trans, 1.0), 0.0)

    def unrender(step, carry):
        entries = [depth - 1 - 2 * step, depth - 2 - 2 * step]

        def across(f, k):
            return jnp.broadcast_to(rec[f, pl.ds(k, 1), :], vreg)

        first_x = [across(0, k) for k in entries]
        tint = [[across(6 + ch, k) for ch in range(COLOURS)] for k in entries]
        sums = [[jnp.zeros(vreg, F32)] * 6 for _ in entries]
        for c in range(16):
            part = slice(c * 8, c * 8 + 8)
            grads = [seg[ch, part, :] for ch in range(COLOURS)]
            behind = behind_s[part, :]
            for n, k in enumerate(entries):
                alpha = alpha_s[k, part, :]
                weight = alpha * trans_s[k, part, :]
                gap = grads[0] * tint[n][0] + grads[1] * tint[n][1] + grads[2] * tint[n][2] - behind
                behind = behind + alpha * gap
                slope = weight * gap
                delta_x = first_x[n] + float(c)
                slope_x = slope * delta_x
                terms = [slope, slope_x, slope_x * delta_x] + [weight * g for g in grads]
                sums[n] = [a + b for a, b in zip(sums[n], terms)]
            behind_s[part, :] = behind
        for n, k in enumerate(entries):
            delta_y = across(1, k) + rows_f
            by_y, total = sums[n][0] * delta_y, sums[n]
            rows = [total[0], total[1], by_y, total[2], total[1] * delta_y, by_y * delta_y, *total[3:6]]
            for f, value in enumerate(rows):
                spread[f, pl.ds(pl.multiple_of(k * 8, 8), 8), :] = value
        return carry

    lax.fori_loop(0, depth // 2, unrender, 0)
    moments = []
    for f in range(9):
        total = spread[f, pl.ds(0, depth, stride=8), :]
        for r in range(1, 8):
            total = total + spread[f, pl.ds(r, depth, stride=8), :]
        moments.append(total)
    conic_a, conic_b, conic_c, opaque = [rec[9 + i] for i in range(4)]
    grads_out = [
        conic_a * moments[1] + conic_b * moments[2],
        conic_b * moments[1] + conic_c * moments[2],
        -0.5 * moments[3],
        -moments[4],
        -0.5 * moments[5],
        moments[0] / opaque,
        moments[6],
        moments[7],
        moments[8],
    ]
    pack(grads_out, jnp.broadcast_to(own_loss, (1, LANES)), ret_out)
    grads_back = [
        remote(ret_out.at[peer], ret_in.at[0, me], ret_send.at[d], ret_recv.at[d], {"space": peer})
        for d, peer in enumerate(peers)
    ]
    grads_across = [
        remote(
            ret_out.at[peer], ret_in.at[1, me], ret_send.at[devices + d], ret_recv.at[devices + d],
            {"space": peer, "view": across_x},
        )
        for d, peer in enumerate(peers + [me])
    ]
    for copy in grads_across + grads_back:
        copy.start()
    ret_in[0, me] = ret_out[me]

    for copy in cameras:
        copy.wait_recv()
    for v in range(views):
        turned = turn_of(head_view[v, 0:1, :])
        for i, value in enumerate([x for row in turned for x in row] + harmonics(turned[2])):
            table_out[v, i : i + 1, :] = jnp.broadcast_to(value, (1, LANES))

    views_out = []
    for which, (view, waits) in enumerate(((across_x, grads_across), (my_view, grads_back))):
        for copy in waits:
            copy.wait_recv()
        for f, value in enumerate(unpack(ret_in.at[1 - which])):
            fields[f] = value
        for half in range(tall // 8):
            slot_of = inverse[half * 8 : half * 8 + 8, :]
            entry_of = inverse[tall + half * 8 : tall + half * 8 + 8, :]
            for f in range(9):
                value = jnp.zeros(vreg, F32)
                for h in range(depth):
                    row = jnp.broadcast_to(fields[f, h : h + 1, :], vreg)
                    row = jnp.take_along_axis(row, slot_of, axis=1, mode="promise_in_bounds")
                    value = jnp.where(entry_of == h, row, value)
                view_grads[view, f, half * 8 : half * 8 + 8, :] = value
        piece = view_grads.at[view]
        views_out.append(remote(piece, piece, view_send.at[which], view_recv.at[which], {"view": pair}))
        views_out[which].start()
    total_loss = jnp.zeros((1, 1), F32)
    for s in range(devices):
        total_loss = total_loss + ret_in[0, s, body : body + 1, 0:1]
    loss_out[...] = total_loss / (3.0 * height_px * width_px)
    for copy in views_out:
        copy.wait_recv()
    for copy in cameras + records_out + grads_back + grads_across + views_out:
        copy.wait_send()
    left(goal_copies)
    for copies in image_copies:
        left(copies)


def finish_kernel(sizes, params_ref, grads_ref, table_ref, picture_ref, grad_hbm, picture_hbm, flat, grad_v, sems):
    views, splats, centre_x, centre_y = sizes
    param_rows = params_ref.shape[0]
    tall = splats // LANES
    tiles = -(-param_rows // 8)
    writes = [pltpu.make_async_copy(picture_ref, picture_hbm, sems.at[tiles])]
    writes[0].start()

    def write_tile(tile):
        size = min(8, param_rows - 8 * tile)
        for i in range(tall):
            start = (tile * tall + i) * 8
            grad_v[8 * tile : 8 * tile + size, i * LANES : (i + 1) * LANES] = flat[start : start + size, :]
        rows = pl.ds(8 * tile, size)
        writes.append(pltpu.make_async_copy(grad_v.at[rows], grad_hbm.at[rows], sems.at[tile]))
        writes[-1].start()

    for tile in range(-(-param_rows // 8)):
        size = min(8, param_rows - 8 * tile)
        for i in range(tall) if tile < 2 else ():
            start = (tile * tall + i) * 8
            flat[start : start + size, :] = params_ref[8 * tile : 8 * tile + size, i * LANES : (i + 1) * LANES]

    def place(row):
        return pl.ds(row // 8 * tall * 8 + row % 8, tall, stride=8)

    turns = [[[table_ref[v, r * 3 + c : r * 3 + c + 1, :] for c in range(3)] for r in range(3)] for v in range(views)]
    bases = [[table_ref[v, 9 + i : 10 + i, :] for i in range(16)] for v in range(views)]
    rows = [flat[place(i), :] for i in range(11)]
    for c in range(COLOURS):
        by_colour = [grads_ref[v, 6 + c] for v in range(views)]
        for i in range(16):
            value = bases[0][i] * by_colour[0]
            for v in range(1, views):
                value = value + bases[v][i] * by_colour[v]
            flat[place(11 + 3 * i + c), :] = value
    for tile in range(2, tiles):
        write_tile(tile)
    pull = jax.vjp(lambda r: geometry(r, turns, centre_x, centre_y), rows)[1]
    for i, value in enumerate(pull([[grads_ref[v, f] for f in range(6)] for v in range(views)])[0]):
        flat[place(i), :] = value
    for tile in range(2):
        write_tile(tile)
    for copy in writes:
        copy.wait()


def shards(params, visible, blocks, counts, depth_rank, camera, background, target):
    devices, views = lax.axis_size("space"), lax.axis_size("view")
    slots, depth = visible.shape[1:]
    capacity = slots // devices
    strip_rows, width_px = target.shape[2:]
    splats = params.shape[1]
    tall = splats // LANES
    groups = width_px // LANES
    rows_in, rows_mid = strip_rows + 4 * HALO, strip_rows + 2 * HALO
    sizes = (devices, views, depth, slots, capacity, strip_rows, width_px, splats)
    per_tile = LANES // capacity
    dense = devices == 8 and per_tile == 8 and depth == 16
    message = (depth + 2 if dense else depth * -(-9 // per_tile)) + 1
    vmem = lambda *shape: pltpu.VMEM(shape, F32)
    half = lambda *shape: pltpu.VMEM(shape, BF16)
    dma = lambda count: pltpu.SemaphoreType.DMA((count,))
    scratch = [
        vmem(*params.shape), pltpu.VMEM((depth, slots), I32), pltpu.VMEM(blocks.shape, I32),
        pltpu.VMEM(counts.shape, I32), pltpu.VMEM(depth_rank.shape, I32), vmem(*camera.shape),
        vmem(*background.shape), vmem(*target.shape[1:]),
        vmem(-(-params.shape[0] // 8) * tall * 8, LANES), vmem(9, tall, LANES), pltpu.VMEM((2, depth, LANES), I32),
        vmem(8, LANES), vmem(views, 8, LANES),
        vmem(devices, message, LANES), vmem(devices, message, LANES),
        vmem(devices, message, LANES), vmem(2, devices, message, LANES),
        vmem(13, depth, LANES), half(6 * LANES, LANES), half(3 * LANES, 2 * LANES),
        half(3 * LANES, LANES), half(3 * LANES, LANES),
        half(6 * LANES, 2 * LANES), pltpu.VMEM((2 * tall, LANES), I32),
        vmem(depth, LANES, LANES), vmem(depth, LANES, LANES), vmem(5, LANES, LANES),
        vmem(COLOURS, rows_in * groups, LANES), vmem(COLOURS, rows_in * groups, LANES),
        vmem(COLOURS, 3 * rows_mid * groups + 16, LANES), vmem(COLOURS, 2 * rows_mid * groups, LANES),
        vmem(COLOURS, 3 * rows_mid * groups, LANES), vmem(3 * COLOURS, rows_mid * groups, LANES),
        vmem(rows_mid * groups, LANES), vmem(rows_mid * groups, LANES), vmem(LANES, LANES), vmem(9, 8 * depth, LANES),
        dma(8), dma(views), dma(views), dma(devices), dma(devices), dma(2 * devices),
        dma(2 * devices), dma(2), dma(2), dma(6), dma(6), dma(2), dma(2),
    ]
    whole = pl.BlockSpec(memory_space=pltpu.VMEM)
    grads, table, picture, loss = pl.pallas_call(
        functools.partial(step_kernel, sizes),
        name="step",
        out_shape=(
            jax.ShapeDtypeStruct((views, 9, tall, LANES), F32),
            jax.ShapeDtypeStruct((views, TABLE, LANES), F32),
            jax.ShapeDtypeStruct(target.shape, F32),
            jax.ShapeDtypeStruct((1, 1), F32),
        ),
        in_specs=[pl.BlockSpec(memory_space=pltpu.HBM)] * 8,
        out_specs=(whole,) * 4,
        scratch_shapes=scratch,
        compiler_params=pltpu.CompilerParams(
            collective_id=0, has_side_effects=True, vmem_limit_bytes=20 * 1024 * 1024
        ),
    )(*[pltpu.with_memory_space_constraint(x, pltpu.HBM) for x in (params, jnp.swapaxes(visible, 1, 2), blocks, counts, depth_rank, camera, background, target)])
    centre = (0.5 * width_px, 0.5 * strip_rows * devices)
    grad, picture = pl.pallas_call(
        functools.partial(finish_kernel, (views, splats, *centre)),
        name="finish",
        out_shape=(jax.ShapeDtypeStruct(params.shape, F32), jax.ShapeDtypeStruct(target.shape, F32)),
        in_specs=[whole] * 4,
        out_specs=(pl.BlockSpec(memory_space=pl.ANY),) * 2,
        scratch_shapes=[
            vmem(-(-params.shape[0] // 8) * tall * 8, LANES), vmem(*params.shape), dma(-(-params.shape[0] // 8) + 1)
        ],
        compiler_params=pltpu.CompilerParams(vmem_limit_bytes=20 * 1024 * 1024),
    )(params, grads, table, picture)
    return (grad, picture, loss.reshape(1))


def solution(mesh):
    in_specs = (
        P(None, "space"),
        P("space", None, None),
        P("space", None),
        P("space", None),
        P("view", None),
        P("view", None),
        P("view", None),
        P("view", None, "space", None),
    )
    out_specs = (P(None, "space"), P("view", None, "space", None), P("view"))
    return jax.shard_map(shards, mesh=mesh, in_specs=in_specs, out_specs=out_specs, check_vma=False)
```

```python
import functools
import math

import jax
import jax.numpy as jnp
import numpy as np
from jax import lax
from jax.experimental import pallas as pl
from jax.experimental.pallas import tpu as pltpu
from jax.sharding import PartitionSpec as P

F32 = jnp.float32
BF16 = jnp.bfloat16
I32 = jnp.int32
LANES = 128
LOG2E = 1.4426950408889634
SH_ZERO = 0.28209479177387814
SH_ONE = 0.4886025119029199
SH_TWO = (
    1.0925484305920792,
    -1.0925484305920792,
    0.31539156525252005,
    -1.0925484305920792,
    0.5462742152960396,
)
SH_THREE = (
    -0.5900435899266435,
    2.890611442640554,
    -0.4570457994644658,
    0.3731763325901154,
    -0.4570457994644658,
    1.445305721320277,
    -0.5900435899266435,
)
DILATION = 0.3
SMOOTHING = 0.0001
SSIM_FIRST = 0.0001
SSIM_SECOND = 0.0009


def camera_rotation(angles):
    cos_a, sin_a = (jnp.cos(angles[0]), jnp.sin(angles[0]))
    cos_b, sin_b = (jnp.cos(angles[1]), jnp.sin(angles[1]))
    cos_c, sin_c = (jnp.cos(angles[2]), jnp.sin(angles[2]))
    return [
        [cos_c * cos_b, cos_c * sin_b * sin_a - sin_c * cos_a, cos_c * sin_b * cos_a + sin_c * sin_a],
        [sin_c * cos_b, sin_c * sin_b * sin_a + cos_c * cos_a, sin_c * sin_b * cos_a - cos_c * sin_a],
        [-sin_b, cos_b * sin_a, cos_b * cos_a],
    ]


def harmonics(view_axis):
    axis_x, axis_y, axis_z = (view_axis[0], view_axis[1], view_axis[2])
    sq_x, sq_y, sq_z = (axis_x * axis_x, axis_y * axis_y, axis_z * axis_z)
    return [
        SH_ZERO * jnp.ones_like(axis_x),
        -SH_ONE * axis_y,
        SH_ONE * axis_z,
        -SH_ONE * axis_x,
        SH_TWO[0] * axis_x * axis_y,
        SH_TWO[1] * axis_y * axis_z,
        SH_TWO[2] * (2.0 * sq_z - sq_x - sq_y),
        SH_TWO[3] * axis_x * axis_z,
        SH_TWO[4] * (sq_x - sq_y),
        SH_THREE[0] * axis_y * (3.0 * sq_x - sq_y),
        SH_THREE[1] * axis_x * axis_y * axis_z,
        SH_THREE[2] * axis_y * (4.0 * sq_z - sq_x - sq_y),
        SH_THREE[3] * axis_z * (2.0 * sq_z - 3.0 * sq_x - 3.0 * sq_y),
        SH_THREE[4] * axis_x * (4.0 * sq_z - sq_x - sq_y),
        SH_THREE[5] * axis_z * (sq_x - sq_y),
        SH_THREE[6] * axis_x * (sq_x - 3.0 * sq_y),
    ]


def geometry(rows, turns, centre_x, centre_y):
    scales = [jnp.exp(rows[i]) for i in range(3, 6)]
    quat = rows[6:10]
    length = jnp.sqrt(quat[0] * quat[0] + quat[1] * quat[1] + quat[2] * quat[2] + quat[3] * quat[3])
    part_w, part_x, part_y, part_z = [q / length for q in quat]
    spin = [
        [
            1.0 - 2.0 * (part_y * part_y + part_z * part_z),
            2.0 * (part_x * part_y - part_w * part_z),
            2.0 * (part_x * part_z + part_w * part_y),
        ],
        [
            2.0 * (part_x * part_y + part_w * part_z),
            1.0 - 2.0 * (part_x * part_x + part_z * part_z),
            2.0 * (part_y * part_z - part_w * part_x),
        ],
        [
            2.0 * (part_x * part_z - part_w * part_y),
            2.0 * (part_y * part_z + part_w * part_x),
            1.0 - 2.0 * (part_x * part_x + part_y * part_y),
        ],
    ]
    local = [[spin[r][c] * scales[c] for c in range(3)] for r in range(3)]
    opacity = 1.0 / (1.0 + jnp.exp(-rows[10]))
    shift_x = rows[0] - centre_x
    shift_y = rows[1] - centre_y
    records = []
    for turn in turns:
        frame = [
            [
                turn[r][0] * local[0][c] + turn[r][1] * local[1][c] + turn[r][2] * local[2][c]
                for c in range(3)
            ]
            for r in range(2)
        ]
        cov_xx = sum(frame[0][c] * frame[0][c] for c in range(3)) + DILATION
        cov_xy = sum(frame[0][c] * frame[1][c] for c in range(3))
        cov_yy = sum(frame[1][c] * frame[1][c] for c in range(3)) + DILATION
        inverse = 1.0 / (cov_xx * cov_yy - cov_xy * cov_xy)
        mean_u = turn[0][0] * shift_x + turn[0][1] * shift_y + turn[0][2] * rows[2] + centre_x
        mean_w = turn[1][0] * shift_x + turn[1][1] * shift_y + turn[1][2] * rows[2] + centre_y
        records.append(
            [mean_u, mean_w, cov_yy * inverse, -cov_xy * inverse, cov_xx * inverse, opacity]
        )
    return records


def blur_taps():
    raw_taps = [math.exp(-(offset - 5) * (offset - 5) / 4.5) for offset in range(11)]
    total = sum(raw_taps)
    return [value / total for value in raw_taps]


NT = (((1,), (1,)), ((), ()))
COLOURS = 3
HALO = 5
MARGIN = 2 * HALO
TABLE = 32


def three_parts(value):
    high = value.astype(BF16)
    rest = value - high.astype(F32)
    middle = rest.astype(BF16)
    low = (rest - middle.astype(F32)).astype(BF16)
    return [high, middle, low]


def iota(shape, axis):
    return lax.broadcasted_iota(I32, shape, axis)


def swap_chunks(values, width):
    lane = iota((1, LANES), 1)
    for bit in range(3):
        step = 1 << bit
        low = (lane & (width * step)) == 0
        moved = list(values)
        for a in range(8):
            if not a & step:
                first, second = values[a], values[a | step]
                moved[a] = jnp.where(low, first, pltpu.roll(second, width * step, axis=1))
                moved[a | step] = jnp.where(low, pltpu.roll(first, LANES - width * step, axis=1), second)
        values = moved
    return values


def swap_sublanes(value, width):
    lane, row = iota((8, LANES), 1), iota((8, LANES), 0)
    for bit in range(3):
        step = 1 << bit
        low_lane, low_row = (lane & (width * step)) == 0, (row & step) == 0
        up = pltpu.roll(pltpu.roll(value, 8 - step, axis=0), width * step, axis=1)
        down = pltpu.roll(pltpu.roll(value, step, axis=0), LANES - width * step, axis=1)
        value = jnp.where(low_lane == low_row, value, jnp.where(low_row, up, down))
    return value


def step_kernel(
    sizes,
    params_hbm, visible_hbm, blocks_hbm, counts_hbm, rank_hbm, camera_hbm, backdrop_hbm, target_hbm,
    view_grads, table_out, picture_out, loss_out,
    params_v, visible_v, blocks_v, counts_v, rank_v, camera_v, backdrop_v, target_v,
    flat, fields, lists, head, head_view, out_msg, in_msg, ret_out, ret_in,
    rec, place_f, place_b, nearer, further, taps_w, inverse, alpha_s, weight_s, seg, goal, image,
    rows_buf, goal_buf, cols_buf, adj, seed_s, own_s, behind_s, spread, ahead_s,
    in_sem, camv_send, camv_recv, msg_send, msg_recv, ret_send, ret_recv,
    goal_send, goal_recv, image_send, image_recv, view_send, view_recv,
):
    devices, views, depth, slots, capacity, strip_rows, width_px, splats = sizes
    me = lax.axis_index("space")
    my_view = lax.axis_index("view")
    param_rows = params_v.shape[0]
    tall = splats // LANES
    block_cols = width_px // 16
    block_rows = strip_rows // 8
    groups = width_px // LANES
    bands = block_rows * groups
    rows_in = strip_rows + 4 * HALO
    rows_mid = strip_rows + 2 * HALO
    centre_x = 0.5 * width_px
    centre_y = 0.5 * strip_rows * devices
    shift = capacity.bit_length() - 1
    taps = blur_taps()
    peers = [me ^ d for d in range(devices - 1, 0, -1)]
    partners = [my_view ^ d for d in range(1, views)]
    pair, across_x = my_view ^ 1, my_view ^ 2

    barrier = pltpu.get_barrier_semaphore()
    greeted = [{"space": peer, "view": view} for peer in peers for view in (my_view, across_x)]
    greeted += [{"space": me, "view": view} for view in partners]
    for target in greeted:
        pl.semaphore_signal(barrier, inc=1, device_id=target, device_id_type=pl.DeviceIdType.MESH)
    pairs = [
        (blocks_hbm, blocks_v), (counts_hbm, counts_v), (camera_hbm, camera_v),
        (params_hbm.at[pl.ds(0, 16)], params_v.at[pl.ds(0, 16)]),
        (visible_hbm.at[0], visible_v), (rank_hbm, rank_v), (backdrop_hbm, backdrop_v), (target_hbm.at[0], target_v),
        (params_hbm.at[pl.ds(16, param_rows - 16)], params_v.at[pl.ds(16, param_rows - 16)]),
    ]
    fetches = [pltpu.make_async_copy(a, b, in_sem.at[i]) for i, (a, b) in enumerate(pairs)]
    for fetch in fetches[3:4] + fetches[8:9] + fetches[0:3] + fetches[4:8]:
        fetch.start()

    rim = MARGIN * groups

    @pl.when(me == 0)
    def _():
        goal[:, 0:rim, :] = jnp.zeros((COLOURS, rim, LANES), F32)
        image[:, 0:rim, :] = jnp.zeros((COLOURS, rim, LANES), F32)

    @pl.when(me == devices - 1)
    def _():
        low = (MARGIN + strip_rows) * groups
        goal[:, low : low + rim, :] = jnp.zeros((COLOURS, rim, LANES), F32)
        image[:, low : low + rim, :] = jnp.zeros((COLOURS, rim, LANES), F32)

    lane = iota((1, LANES), 1)
    chunk = lax.shift_right_logical(lane, shift)
    for fetch in fetches[0:3]:
        fetch.wait()
    counted = jnp.zeros((1, LANES), I32)
    for o in range(devices):
        counted = jnp.where(chunk == o, counts_v[:, o : o + 1], counted)
    live = (lane & (capacity - 1)) < counted
    ids_row = jnp.where(live, blocks_v[...], -1).astype(F32)
    head[...] = jnp.zeros_like(head)
    head[0:1, 0:3] = camera_v[...]
    head_view[my_view] = head[...]

    def remote(src, dst, send, recv, target):
        return pltpu.make_async_remote_copy(
            src_ref=src, dst_ref=dst, send_sem=send, recv_sem=recv, device_id=target,
            device_id_type=pl.DeviceIdType.MESH,
        )

    def flatten(tiles):
        for tile in tiles:
            size = min(8, param_rows - 8 * tile)
            for i in range(tall):
                start = (tile * tall + i) * 8
                flat[start : start + size, :] = params_v[8 * tile : 8 * tile + size, i * LANES : (i + 1) * LANES]

    fetches[3].wait()
    flatten(range(2))

    def param_row(row):
        return flat[pl.ds(row // 8 * tall * 8 + row % 8, tall, stride=8), :]

    def turn_of(angles):
        return camera_rotation([angles[:, i : i + 1] for i in range(3)])

    turn = turn_of(camera_v[...])
    record = geometry([param_row(i) for i in range(11)], [turn], centre_x, centre_y)[0]
    basis = harmonics(turn[2])
    fetches[8].wait()
    flatten(range(2, -(-param_rows // 8)))
    for c in range(COLOURS):
        colour = 0.5 + basis[0] * param_row(11 + c)
        for i in range(1, 16):
            colour = colour + basis[i] * param_row(11 + 3 * i + c)
        record.append(colour)
    for f in range(9):
        fields[f] = record[f]
    fetches[4].wait()
    listed = visible_v[...]
    lists[0] = lax.shift_right_logical(listed, 7)
    lists[1] = listed & (LANES - 1)
    picked = [[] for _ in range(9)]
    for half in range(depth // 8):
        high = lists[0, half * 8 : half * 8 + 8, :]
        low = lists[1, half * 8 : half * 8 + 8, :]
        for f in range(9):
            value = jnp.zeros((8, LANES), F32)
            for h in range(tall):
                row = jnp.broadcast_to(fields[f, h : h + 1, :], (8, LANES))
                row = jnp.take_along_axis(row, low, axis=1, mode="promise_in_bounds")
                value = jnp.where(high == h, row, value)
            picked[f].append(value)
    picked = [jnp.concatenate(p, axis=0) for p in picked]

    per_tile = LANES // capacity
    dense = devices == 8 and per_tile == 8 and depth == 16
    body = depth + 2 if dense else depth * -(-9 // per_tile)

    def pack(values, extra, dst):
        if dense:
            for o, block in enumerate(swap_chunks(values[0:8], capacity)):
                dst[o, 0:depth, :] = block
            for half in range(2):
                last = swap_sublanes(values[8][half * 8 : half * 8 + 8], capacity)
                for o in range(devices):
                    dst[o, depth + half : depth + half + 1, :] = last[o : o + 1]
        for o in range(devices):
            dst[o, body : body + 1, :] = extra
            for t in range(0 if dense else -(-len(values) // per_tile)):
                block = None
                for j, value in enumerate(values[t * per_tile : (t + 1) * per_tile]):
                    moved = pltpu.roll(value, (j - o) * capacity % LANES, axis=1)
                    block = moved if block is None else jnp.where(chunk == j, moved, block)
                dst[o, t * depth : (t + 1) * depth, :] = block

    def unpack(src):
        if dense:
            values = swap_chunks([src[o, 0:depth, :] for o in range(devices)], capacity)
            last = [
                jnp.concatenate([src[o, depth + half : depth + half + 1, :] for o in range(devices)], axis=0)
                for half in range(2)
            ]
            return values + [jnp.concatenate([swap_sublanes(v, capacity) for v in last], axis=0)]
        values = []
        for f in range(9):
            t, j = divmod(f, per_tile)
            value = None
            for s in range(devices):
                moved = pltpu.roll(src[s, t * depth : (t + 1) * depth, :], (s - j) * capacity % LANES, axis=1)
                value = moved if value is None else jnp.where(chunk == s, moved, value)
            values.append(value)
        return values

    pack(picked, ids_row, out_msg)
    pl.semaphore_wait(barrier, len(greeted))
    records_out = [
        remote(out_msg.at[peer], in_msg.at[me], msg_send.at[d], msg_recv.at[d], {"space": peer})
        for d, peer in enumerate(peers)
    ]
    for copy in records_out:
        copy.start()
    cameras = [
        remote(head, head_view.at[my_view], camv_send.at[d], camv_recv.at[d], {"view": peer})
        for d, peer in enumerate(partners)
    ]
    for copy in cameras:
        copy.start()
    in_msg[me] = out_msg[me]

    def own_rows(b, g):
        return pl.ds((MARGIN + b * 8) * groups + g, 8, stride=groups)

    fetches[7].wait()
    for ch in range(COLOURS):
        for b in range(block_rows):
            for g in range(groups):
                goal[ch, own_rows(b, g), :] = target_v[ch, b * 8 : b * 8 + 8, g * LANES : (g + 1) * LANES]

    top, bottom, below = MARGIN * groups, strip_rows * groups, (MARGIN + strip_rows) * groups

    def exchange(ref, channels, send, recv, at):
        upward = remote(
            ref.at[channels, pl.ds(top, rim)], ref.at[channels, pl.ds(below, rim)],
            send.at[at], recv.at[at], {"space": lax.rem(me + devices - 1, devices)},
        )
        downward = remote(
            ref.at[channels, pl.ds(bottom, rim)], ref.at[channels, pl.ds(0, rim)],
            send.at[at + 1], recv.at[at + 1], {"space": lax.rem(me + 1, devices)},
        )
        return upward, downward

    not_first, not_last = me > 0, me < devices - 1

    def begin(copies):
        pl.when(not_first)(copies[0].start)
        pl.when(not_last)(copies[1].start)

    def arrived(copies):
        pl.when(not_last)(copies[0].wait_recv)
        pl.when(not_first)(copies[1].wait_recv)

    def left(copies):
        pl.when(not_first)(copies[0].wait_send)
        pl.when(not_last)(copies[1].wait_send)

    goal_copies = exchange(goal, slice(None), goal_send, goal_recv, 0)
    begin(goal_copies)

    square = (LANES, LANES)
    fetches[5].wait()
    ranks = jnp.zeros((1, LANES), I32)
    for s in range(devices):
        ranks = jnp.where(chunk == s, rank_v[:, s : s + 1], ranks)
    offset = iota(square, 1) - iota(square, 0)
    near = iota(square, 0) < LANES // 2
    beside = jnp.where(near, offset - LANES, offset + LANES)
    exact = [np.float32(tap) for tap in taps]
    highs = [float(tap.astype(jnp.bfloat16)) for tap in exact]
    lows = [float((tap - np.float32(high)).astype(jnp.bfloat16)) for tap, high in zip(exact, highs)]
    blur_norm = float(1.0 / (sum(highs) + sum(lows)))
    for side, values in enumerate((highs, lows)):
        for part, distance in enumerate((offset, beside)):
            weights = jnp.zeros(square, F32)
            for i in range(11):
                weights = jnp.where(distance == i - HALO, values[i], weights)
            weights = weights.astype(BF16)
            for term in range(3):
                start = (term * 2 + part) * LANES
                taps_w[start : start + LANES, side * LANES : (side + 1) * LANES] = weights

    ranks_f = ranks.astype(F32)
    diagonal = iota(square, 0) == iota(square, 1)
    ranks_c = jnp.sum(jnp.where(diagonal, ranks_f, 0.0), axis=1, keepdims=True)
    ahead_s[0] = jnp.where(ranks_c < ranks_f, 1.0, 0.0)
    ahead_s[1] = jnp.where(ranks_c > ranks_f, 1.0, 0.0)
    slot_value = lane.astype(F32)

    def invert(k, total):
        high = lists[0, pl.ds(k, 1), :]
        low = lists[1, pl.ds(k, 1), :]
        hit = iota((tall, LANES), 0) == high
        left = jnp.concatenate(
            [jnp.where(hit, slot_value, 0.0), jnp.where(hit, k.astype(F32), 0.0)], axis=0
        ).astype(BF16)
        right = jnp.where(iota(square, 0) == low, 1.0, 0.0).astype(BF16)
        return total + lax.dot_general(left, right, NT, preferred_element_type=F32)

    inverse[...] = lax.fori_loop(0, depth, invert, jnp.zeros((2 * tall, LANES), F32)).astype(I32)

    height_px = strip_rows * devices
    mid, end = rows_mid * groups, strip_rows * groups
    for at in range(0, mid, 8):
        line = iota((8, LANES), 0) + at
        row_y = (line.astype(F32) + 0.5) * (1.0 / groups)
        y = row_y + (me * strip_rows - HALO).astype(F32)
        counts_here = (y > 0.0) & (y < float(height_px))
        seed_s[at : at + 8, :] = jnp.where(counts_here, -0.2, 0.0)
        own_s[at : at + 8, :] = jnp.where((row_y > HALO) & (row_y < HALO + strip_rows), 1.0, 0.0)

    for copy in records_out:
        copy.wait_recv()
    owned = jnp.zeros((1, LANES), F32)
    for s in range(devices):
        amount = lax.rem(s - me + devices, devices) * capacity
        owned = jnp.where(chunk == s, pltpu.roll(in_msg[s, body : body + 1, :], amount, axis=1), owned)
    own_ids = jnp.maximum(owned, 0.0)
    block_y = jnp.floor((own_ids + 0.5) * (1.0 / block_cols))
    block_x = own_ids - block_y * block_cols
    corner_x = block_x * 16.0 + 0.5
    corner_y = block_y * 8.0 + (me * strip_rows).astype(F32) + 0.5
    got = unpack(in_msg)
    rec[0] = corner_x - got[0]
    rec[1] = corner_y - got[1]
    rec[2] = -0.5 * LOG2E * got[2]
    rec[3] = -LOG2E * got[3]
    rec[4] = -0.5 * LOG2E * got[4]
    rec[5] = jnp.log2(got[5])
    for f in range(6, 9):
        rec[f] = got[f]
    for f in range(2, 6):
        rec[7 + f] = got[f]
    vreg = (8, LANES)
    rows_f = iota(vreg, 0).astype(F32)

    def wide(f, k):
        return jnp.broadcast_to(rec[f, k : k + 1, :], vreg)

    width_c = 4

    def render_some(index, carry):
        trans = [jnp.ones(vreg, F32)] * width_c
        logs = [jnp.zeros(vreg, F32)] * width_c
        run = [None] * width_c
        sums = [[jnp.zeros(vreg, F32)] * width_c for _ in range(COLOURS)]
        base = (index * width_c).astype(F32)
        for k in range(depth):
            delta_y = wide(1, k) + rows_f
            cross = wide(3, k) * delta_y
            square_y = wide(4, k) * delta_y * delta_y + wide(5, k)
            first_x = wide(0, k) + base
            curve = wide(2, k)
            tint = [wide(6 + ch, k) for ch in range(COLOURS)]
            for j in range(width_c):
                delta_x = first_x + float(j)
                alpha = jnp.exp2((curve * delta_x + cross) * delta_x + square_y)
                place = pl.ds(pl.multiple_of((index * width_c + j) * 8, 8), 8)
                alpha_s[k, place, :] = alpha
                weight = alpha * trans[j]
                weight_s[k, place, :] = weight
                for ch in range(COLOURS):
                    sums[ch][j] = sums[ch][j] + weight * tint[ch]
                kept = 1.0 - alpha
                trans[j] = trans[j] * kept
                run[j] = kept if k % 4 == 0 else run[j] * kept
                if k % 4 == 3 or k == depth - 1:
                    logs[j] = logs[j] + jnp.log(run[j])
        for j in range(width_c):
            place = pl.ds(pl.multiple_of((index * width_c + j) * 8, 8), 8)
            for ch in range(COLOURS):
                seg[ch, place, :] = sums[ch][j]
            seg[3, place, :] = trans[j]
            seg[4, place, :] = logs[j]
        return carry

    lax.fori_loop(0, 16 // width_c, render_some, 0)

    owned_c = jnp.transpose(jnp.broadcast_to(owned, (8, LANES)))[:, 0:1]
    same = owned_c == owned
    fwd_mask = jnp.where(same, ahead_s[0], 0.0).astype(BF16)
    bwd_mask = jnp.where(same, ahead_s[1], 0.0).astype(BF16)
    blocks_here = LANES // 2
    lane_sq, sub_sq = iota(square, 1).astype(F32), iota(square, 0).astype(F32)
    for part in range(3):
        nearer[part * LANES : (part + 1) * LANES, :] = fwd_mask
        further[part * LANES : (part + 1) * LANES, :] = bwd_mask
    for d in range(2):
        alive = owned_c >= 0.0
        forth = jnp.where(alive & (lane_sq == owned_c + d * blocks_here), 1.0, 0.0).astype(BF16)
        back = jnp.where((owned >= 0.0) & (sub_sq == owned + d * blocks_here), 1.0, 0.0).astype(BF16)
        for part in range(2):
            place_f[(part * 2 + d) * LANES : (part * 2 + d + 1) * LANES, :] = forth
            place_b[part * LANES : (part + 1) * LANES, d * LANES : (d + 1) * LANES] = back

    before = jnp.dot(
        jnp.concatenate(three_parts(seg[4]), axis=1), nearer[...], preferred_element_type=F32
    )
    seg[4] = jnp.exp(before)
    fetches[6].wait()
    backs = [backdrop_v[:, ch : ch + 1] for ch in range(COLOURS)]
    shares = [[None] * 16 for _ in range(COLOURS)]
    for c in range(16):
        part = slice(c * 8, c * 8 + 8)
        share = seg[4, part, :]
        taken = 1.0 - seg[3, part, :]
        for ch in range(COLOURS):
            tinted = seg[ch, part, :] - backs[ch] * taken
            seg[ch, part, :] = tinted
            shares[ch][c] = share * tinted
    across_lanes = iota(vreg, 1)
    to_natural = (across_lanes & 15) * 8 + lax.shift_right_logical(across_lanes, 4)
    from_natural = (across_lanes & 7) * 16 + lax.shift_right_logical(across_lanes, 3)
    image_copies, placed = [], []
    for ch in range(COLOURS):
        paired = jnp.concatenate(
            [jnp.concatenate([shares[ch][c], shares[ch][c + 8]], axis=1) for c in range(8)], axis=0
        )
        placed.append(
            jnp.dot(
                jnp.concatenate(three_parts(paired)[0:2], axis=1), place_f[0 : 4 * LANES, :], preferred_element_type=F32
            )
        )
    for ch in range(COLOURS):
        for q, value in enumerate(swap_chunks([placed[ch][c * 8 : c * 8 + 8] for c in range(8)], 8)):
            b, g = divmod(q, groups)
            value = jnp.take_along_axis(value, to_natural, axis=1, mode="promise_in_bounds") + backs[ch]
            image[ch, own_rows(b, g), :] = value
            picture_out[0, ch, b * 8 : b * 8 + 8, g * LANES : (g + 1) * LANES] = value
        image_copies.append(exchange(image, ch, image_send, image_recv, 2 * ch))
        begin(image_copies[ch])

    def blur_rows(load, count, store):
        seen = {}

        def line(at):
            if at not in seen:
                seen[at] = load(at)
            return seen[at]

        for at in range(0, count * groups, 8):
            total = taps[5] * line(at + 5 * groups)
            for i in range(5):
                total = total + taps[i] * (line(at + i * groups) + line(at + (10 - i) * groups))
            store(at, total)

    def reader(ref, ch):
        return lambda at: ref[ch, at : at + 8, :]

    def writer(ch, base):
        def store(at, value):
            rows_buf[ch, 8 + base + at : 16 + base + at, :] = value

        return store

    sub_group = iota((1, 8, LANES), 1) & (groups - 1)
    low_lanes = iota((1, 8, LANES), 2) < LANES // 2
    from_right = low_lanes & (sub_group < groups - 1)
    from_left = jnp.logical_not(low_lanes) & (sub_group > 0)

    def blur_columns(ch, first, size, terms):
        def read(at):
            return rows_buf[ch, at : at + size, :].reshape(size // 8, 8, LANES)

        sides = jnp.where(from_right, read(first + 9), jnp.where(from_left, read(first + 7), 0.0))
        own_parts = three_parts(rows_buf[ch, first + 8 : first + 8 + size, :])[0:terms]
        rim_parts = three_parts(sides.reshape(size, LANES))[0:terms]
        both = jnp.dot(
            jnp.concatenate([v for pair in zip(own_parts, rim_parts) for v in pair], axis=1),
            taps_w[0 : terms * 2 * LANES, :],
            preferred_element_type=F32,
        )
        return (both[:, 0:LANES] + both[:, LANES : 2 * LANES]) * blur_norm

    def blur_all(ch, total, dst, terms=3):
        half = -(-total // 32) * 16
        dst[ch, 0:half, :] = blur_columns(ch, 0, half, terms)
        dst[ch, half:total, :] = blur_columns(ch, half, total - half, terms)

    for ch in range(COLOURS):
        rows_buf[ch, 0:8, :] = jnp.zeros((8, LANES), F32)
        rows_buf[ch, 8 + 3 * mid : 16 + 3 * mid, :] = jnp.zeros((8, LANES), F32)
    arrived(goal_copies)
    for ch in range(COLOURS):
        from_goal = reader(goal, ch)
        blur_rows(from_goal, rows_mid, writer(ch, 0))
        blur_rows(lambda at: from_goal(at) * from_goal(at), rows_mid, writer(ch, mid))
        blur_all(ch, 2 * mid, goal_buf)

    def blur_picture(ch):
        from_goal, from_image = reader(goal, ch), reader(image, ch)
        blur_rows(from_image, rows_mid, writer(ch, 0))
        blur_rows(lambda at: from_image(at) * from_image(at), rows_mid, writer(ch, mid))
        blur_rows(lambda at: from_image(at) * from_goal(at), rows_mid, writer(ch, 2 * mid))
        blur_all(ch, 3 * mid, cols_buf)

    def terms_of(ch):
        mean_a, raw_aa, raw_ab = (cols_buf[ch, q * mid : (q + 1) * mid, :] for q in range(3))
        mean_b, raw_bb = (goal_buf[ch, q * mid : (q + 1) * mid, :] for q in range(2))
        centre_rows = slice(HALO * groups, HALO * groups + mid)
        pixel_a, pixel_b = image[ch, centre_rows, :], goal[ch, centre_rows, :]
        seed = seed_s[...]
        square_a, square_b, cross = mean_a * mean_a, mean_b * mean_b, mean_a * mean_b
        first_n = 2.0 * cross + SSIM_FIRST
        second_n = 2.0 * (raw_ab - cross) + SSIM_SECOND
        first_d = square_a + square_b + SSIM_FIRST
        second_d = (raw_aa - square_a) + (raw_bb - square_b) + SSIM_SECOND
        scale = 1.0 / (first_d * second_d)
        ssim = first_n * second_n * scale
        inv_first, inv_second = second_d * scale, first_d * scale
        by_aa = -ssim * inv_second
        by_ab = 2.0 * first_n * scale
        by_a = 2.0 * (mean_b * second_n * scale - mean_a * (ssim * inv_first + by_aa)) - mean_b * by_ab
        adj[3 * ch, 0:mid, :] = seed * by_a
        adj[3 * ch + 1, 0:mid, :] = seed * by_aa
        adj[3 * ch + 2, 0:mid, :] = seed * by_ab
        differ = pixel_a - pixel_b
        for q in range(3):
            blur_rows(reader(adj, 3 * ch + q), strip_rows, writer(ch, q * end))
        blur_all(ch, 3 * end, cols_buf, terms=2)
        return (0.8 * jnp.sqrt(differ * differ + SMOOTHING) + 0.2 * (1.0 - ssim)) * own_s[...]

    def to_slots(ch):
        own_pixels = slice(MARGIN * groups, MARGIN * groups + end)
        pixel_a, pixel_b = image[ch, own_pixels, :], goal[ch, own_pixels, :]
        differ = pixel_a - pixel_b
        adj[3 * ch, 0:end, :] = (
            cols_buf[ch, 0:end, :]
            + 2.0 * pixel_a * cols_buf[ch, end : 2 * end, :]
            + pixel_b * cols_buf[ch, 2 * end : 3 * end, :]
            + 0.8 * differ * lax.rsqrt(differ * differ + SMOOTHING)
        )
        bands_here = []
        for q in range(bands):
            b, g = divmod(q, groups)
            value = adj[3 * ch, pl.ds(b * 8 * groups + g, 8, stride=groups), :]
            bands_here.append(jnp.take_along_axis(value, from_natural, axis=1, mode="promise_in_bounds"))
        stacked = jnp.concatenate(swap_chunks(bands_here, 8), axis=0)
        return jnp.dot(
            jnp.concatenate(three_parts(stacked)[0:2], axis=1), place_b[0 : 2 * LANES, :], preferred_element_type=F32
        )

    arrived(image_copies[0])
    blur_picture(0)
    arrived(image_copies[1])
    blur_picture(1)
    own_terms = terms_of(0)
    arrived(image_copies[2])
    blur_picture(2)
    own_terms = own_terms + terms_of(1)
    pulled = [to_slots(0)]
    own_terms = own_terms + terms_of(2)
    pulled += [to_slots(1), to_slots(2)]
    own_loss = jnp.sum(jnp.sum(own_terms, axis=1, keepdims=True), axis=0, keepdims=True)

    for c in range(16):
        part = slice(c * 8, c * 8 + 8)
        share = seg[4, part, :]
        by_share, by_trans = None, None
        for ch in range(COLOURS):
            grad = pulled[ch][c % 8 * 8 : c % 8 * 8 + 8, c // 8 * LANES : (c // 8 + 1) * LANES]
            piece = grad * seg[ch, part, :]
            by_share = piece if by_share is None else by_share + piece
            grad = grad * share
            seg[ch, part, :] = grad
            piece = grad * backs[ch]
            by_trans = piece if by_trans is None else by_trans + piece
        rows_buf[0, part, :] = by_share * share
        behind_s[part, :] = by_trans
    by_log = jnp.dot(
        jnp.concatenate(three_parts(rows_buf[0, 0:LANES, :]), axis=1), further[...], preferred_element_type=F32
    )
    trans = seg[3]
    visible_through = trans > 2e-38
    behind_s[...] += jnp.where(visible_through, by_log / jnp.where(visible_through, trans, 1.0), 0.0)

    def unrender(step, carry):
        entries = [depth - 1 - 2 * step, depth - 2 - 2 * step]

        def across(f, k):
            return jnp.broadcast_to(rec[f, pl.ds(k, 1), :], vreg)

        first_x = [across(0, k) for k in entries]
        tint = [[across(6 + ch, k) for ch in range(COLOURS)] for k in entries]
        sums = [[jnp.zeros(vreg, F32)] * 6 for _ in entries]
        for c in range(16):
            part = slice(c * 8, c * 8 + 8)
            grads = [seg[ch, part, :] for ch in range(COLOURS)]
            behind = behind_s[part, :]
            for n, k in enumerate(entries):
                alpha = alpha_s[k, part, :]
                weight = weight_s[k, part, :]
                gap = grads[0] * tint[n][0] + grads[1] * tint[n][1] + grads[2] * tint[n][2] - behind
                behind = behind + alpha * gap
                slope = weight * gap
                delta_x = first_x[n] + float(c)
                slope_x = slope * delta_x
                terms = [slope, slope_x, slope_x * delta_x] + [weight * g for g in grads]
                sums[n] = [a + b for a, b in zip(sums[n], terms)]
            behind_s[part, :] = behind
        for n, k in enumerate(entries):
            delta_y = across(1, k) + rows_f
            by_y, total = sums[n][0] * delta_y, sums[n]
            rows = [total[0], total[1], by_y, total[2], total[1] * delta_y, by_y * delta_y, *total[3:6]]
            for f, value in enumerate(rows):
                spread[f, pl.ds(pl.multiple_of(k * 8, 8), 8), :] = value
        return carry

    lax.fori_loop(0, depth // 2, unrender, 0)
    moments = []
    for f in range(9):
        total = spread[f, pl.ds(0, depth, stride=8), :]
        for r in range(1, 8):
            total = total + spread[f, pl.ds(r, depth, stride=8), :]
        moments.append(total)
    conic_a, conic_b, conic_c, opaque = [rec[9 + i] for i in range(4)]
    grads_out = [
        conic_a * moments[1] + conic_b * moments[2],
        conic_b * moments[1] + conic_c * moments[2],
        -0.5 * moments[3],
        -moments[4],
        -0.5 * moments[5],
        moments[0] / opaque,
        moments[6],
        moments[7],
        moments[8],
    ]
    pack(grads_out, jnp.broadcast_to(own_loss, (1, LANES)), ret_out)
    grads_back = [
        remote(ret_out.at[peer], ret_in.at[0, me], ret_send.at[d], ret_recv.at[d], {"space": peer})
        for d, peer in enumerate(peers)
    ]
    grads_across = [
        remote(
            ret_out.at[peer], ret_in.at[1, me], ret_send.at[devices + d], ret_recv.at[devices + d],
            {"space": peer, "view": across_x},
        )
        for d, peer in enumerate(peers + [me])
    ]
    for copy in grads_back + grads_across:
        copy.start()
    ret_in[0, me] = ret_out[me]

    for copy in cameras:
        copy.wait_recv()
    for v in range(views):
        turned = turn_of(head_view[v, 0:1, :])
        for i, value in enumerate([x for row in turned for x in row] + harmonics(turned[2])):
            table_out[v, i : i + 1, :] = jnp.broadcast_to(value, (1, LANES))

    views_out = []
    for which, (view, waits) in enumerate(((my_view, grads_back), (across_x, grads_across))):
        for copy in waits:
            copy.wait_recv()
        for f, value in enumerate(unpack(ret_in.at[which])):
            fields[f] = value
        for half in range(tall // 8):
            slot_of = inverse[half * 8 : half * 8 + 8, :]
            entry_of = inverse[tall + half * 8 : tall + half * 8 + 8, :]
            for f in range(9):
                value = jnp.zeros(vreg, F32)
                for h in range(depth):
                    row = jnp.broadcast_to(fields[f, h : h + 1, :], vreg)
                    row = jnp.take_along_axis(row, slot_of, axis=1, mode="promise_in_bounds")
                    value = jnp.where(entry_of == h, row, value)
                view_grads[view, f, half * 8 : half * 8 + 8, :] = value
        piece = view_grads.at[view]
        views_out.append(remote(piece, piece, view_send.at[which], view_recv.at[which], {"view": pair}))
        views_out[which].start()
    total_loss = jnp.zeros((1, 1), F32)
    for s in range(devices):
        total_loss = total_loss + ret_in[0, s, body : body + 1, 0:1]
    loss_out[...] = total_loss / (3.0 * height_px * width_px)
    for copy in views_out:
        copy.wait_recv()
    for copy in cameras + records_out + grads_back + grads_across + views_out:
        copy.wait_send()
    left(goal_copies)
    for copies in image_copies:
        left(copies)


def finish_kernel(sizes, params_ref, grads_ref, table_ref, picture_ref, grad_hbm, picture_hbm, flat, grad_v, sems):
    views, splats, centre_x, centre_y = sizes
    param_rows = params_ref.shape[0]
    tall = splats // LANES
    tiles = -(-param_rows // 8)
    writes = [pltpu.make_async_copy(picture_ref, picture_hbm, sems.at[tiles])]
    writes[0].start()

    def write_tile(tile):
        size = min(8, param_rows - 8 * tile)
        for i in range(tall):
            start = (tile * tall + i) * 8
            grad_v[8 * tile : 8 * tile + size, i * LANES : (i + 1) * LANES] = flat[start : start + size, :]
        rows = pl.ds(8 * tile, size)
        writes.append(pltpu.make_async_copy(grad_v.at[rows], grad_hbm.at[rows], sems.at[tile]))
        writes[-1].start()

    for tile in range(-(-param_rows // 8)):
        size = min(8, param_rows - 8 * tile)
        for i in range(tall) if tile < 2 else ():
            start = (tile * tall + i) * 8
            flat[start : start + size, :] = params_ref[8 * tile : 8 * tile + size, i * LANES : (i + 1) * LANES]

    def place(row):
        return pl.ds(row // 8 * tall * 8 + row % 8, tall, stride=8)

    turns = [[[table_ref[v, r * 3 + c : r * 3 + c + 1, :] for c in range(3)] for r in range(3)] for v in range(views)]
    bases = [[table_ref[v, 9 + i : 10 + i, :] for i in range(16)] for v in range(views)]
    rows = [flat[place(i), :] for i in range(11)]
    for c in range(COLOURS):
        by_colour = [grads_ref[v, 6 + c] for v in range(views)]
        for i in range(16):
            value = bases[0][i] * by_colour[0]
            for v in range(1, views):
                value = value + bases[v][i] * by_colour[v]
            flat[place(11 + 3 * i + c), :] = value
    for tile in range(2, tiles):
        write_tile(tile)
    pull = jax.vjp(lambda r: geometry(r, turns, centre_x, centre_y), rows)[1]
    for i, value in enumerate(pull([[grads_ref[v, f] for f in range(6)] for v in range(views)])[0]):
        flat[place(i), :] = value
    for tile in range(2):
        write_tile(tile)
    for copy in writes:
        copy.wait()


def shards(params, visible, blocks, counts, depth_rank, camera, background, target):
    devices, views = lax.axis_size("space"), lax.axis_size("view")
    slots, depth = visible.shape[1:]
    capacity = slots // devices
    strip_rows, width_px = target.shape[2:]
    splats = params.shape[1]
    tall = splats // LANES
    groups = width_px // LANES
    rows_in, rows_mid = strip_rows + 4 * HALO, strip_rows + 2 * HALO
    sizes = (devices, views, depth, slots, capacity, strip_rows, width_px, splats)
    per_tile = LANES // capacity
    dense = devices == 8 and per_tile == 8 and depth == 16
    message = (depth + 2 if dense else depth * -(-9 // per_tile)) + 1
    vmem = lambda *shape: pltpu.VMEM(shape, F32)
    half = lambda *shape: pltpu.VMEM(shape, BF16)
    dma = lambda count: pltpu.SemaphoreType.DMA((count,))
    scratch = [
        vmem(*params.shape), pltpu.VMEM((depth, slots), I32), pltpu.VMEM(blocks.shape, I32),
        pltpu.VMEM(counts.shape, I32), pltpu.VMEM(depth_rank.shape, I32), vmem(*camera.shape),
        vmem(*background.shape), vmem(*target.shape[1:]),
        vmem(-(-params.shape[0] // 8) * tall * 8, LANES), vmem(9, tall, LANES), pltpu.VMEM((2, depth, LANES), I32),
        vmem(8, LANES), vmem(views, 8, LANES),
        vmem(devices, message, LANES), vmem(devices, message, LANES),
        vmem(devices, message, LANES), vmem(2, devices, message, LANES),
        vmem(13, depth, LANES), half(6 * LANES, LANES), half(3 * LANES, 2 * LANES),
        half(3 * LANES, LANES), half(3 * LANES, LANES),
        half(6 * LANES, 2 * LANES), pltpu.VMEM((2 * tall, LANES), I32),
        vmem(depth, LANES, LANES), vmem(depth, LANES, LANES), vmem(5, LANES, LANES),
        vmem(COLOURS, rows_in * groups, LANES), vmem(COLOURS, rows_in * groups, LANES),
        vmem(COLOURS, 3 * rows_mid * groups + 16, LANES), vmem(COLOURS, 2 * rows_mid * groups, LANES),
        vmem(COLOURS, 3 * rows_mid * groups, LANES), vmem(3 * COLOURS, rows_mid * groups, LANES),
        vmem(rows_mid * groups, LANES), vmem(rows_mid * groups, LANES), vmem(LANES, LANES), vmem(9, 8 * depth, LANES),
        vmem(2, LANES, LANES),
        dma(9), dma(views), dma(views), dma(devices), dma(devices), dma(2 * devices),
        dma(2 * devices), dma(2), dma(2), dma(6), dma(6), dma(2), dma(2),
    ]
    whole = pl.BlockSpec(memory_space=pltpu.VMEM)
    grads, table, picture, loss = pl.pallas_call(
        functools.partial(step_kernel, sizes),
        name="step",
        out_shape=(
            jax.ShapeDtypeStruct((views, 9, tall, LANES), F32),
            jax.ShapeDtypeStruct((views, TABLE, LANES), F32),
            jax.ShapeDtypeStruct(target.shape, F32),
            jax.ShapeDtypeStruct((1, 1), F32),
        ),
        in_specs=[pl.BlockSpec(memory_space=pltpu.HBM)] * 8,
        out_specs=(whole,) * 4,
        scratch_shapes=scratch,
        compiler_params=pltpu.CompilerParams(
            collective_id=0, has_side_effects=True, vmem_limit_bytes=20 * 1024 * 1024
        ),
    )(*[pltpu.with_memory_space_constraint(x, pltpu.HBM) for x in (params, jnp.swapaxes(visible, 1, 2), blocks, counts, depth_rank, camera, background, target)])
    centre = (0.5 * width_px, 0.5 * strip_rows * devices)
    grad, picture = pl.pallas_call(
        functools.partial(finish_kernel, (views, splats, *centre)),
        name="finish",
        out_shape=(jax.ShapeDtypeStruct(params.shape, F32), jax.ShapeDtypeStruct(target.shape, F32)),
        in_specs=[whole] * 4,
        out_specs=(pl.BlockSpec(memory_space=pl.ANY),) * 2,
        scratch_shapes=[
            vmem(-(-params.shape[0] // 8) * tall * 8, LANES), vmem(*params.shape), dma(-(-params.shape[0] // 8) + 1)
        ],
        compiler_params=pltpu.CompilerParams(vmem_limit_bytes=20 * 1024 * 1024),
    )(params, grads, table, picture)
    return (grad, picture, loss.reshape(1))


def solution(mesh):
    in_specs = (
        P(None, "space"),
        P("space", None, None),
        P("space", None),
        P("space", None),
        P("view", None),
        P("view", None),
        P("view", None),
        P("view", None, "space", None),
    )
    out_specs = (P(None, "space"), P("view", None, "space", None), P("view"))
    return jax.shard_map(shards, mesh=mesh, in_specs=in_specs, out_specs=out_specs, check_vma=False)
```
